32 devices in a mesh: grp: 4 (over z), row: 2 (over x), col: 4 (over y, core).
Axes of the slice: x: 2, y: 2, z: 4, core: 2. Of those that a mesh axis runs over, the one named last changes fastest.
Arguments:
- dec_input: bfloat16 [3, 4, 16, 64, 128], P(None, None, 'row', 'col'), may hold values from -6 to 6
- target: bfloat16 [3, 3, 4, 16, 64], P(None, None, 'col', 'row'), may hold values from -5 to 5
- conv_first: bfloat16 [3456, 128], replicated, may hold values from -0.109375 to 0.109375
- conv_second: bfloat16 [3456, 128], replicated, may hold values from -0.109375 to 0.109375
- rgb_weight: bfloat16 [3, 128], replicated, may hold values from -0.5 to 0.5
- vgg_first: bfloat16 [27, 64], replicated, may hold values from -1.25 to 1.25
- vgg_second: bfloat16 [576, 64], replicated, may hold values from -0.25 to 0.25
- vgg_third: bfloat16 [576, 128], replicated, may hold values from -0.25 to 0.25
Outputs:
- grad_first: float32 [442368], P(('grp', 'row', 'col'))
- grad_second: float32 [442368], P(('grp', 'row', 'col'))
The draws below stay inside these ranges and needn't reach their ends.
All inputs are finite; a program needn't handle non-finite values.
Results may differ from the reference program's by a relative error of at most 0.015.
Values may be sent and summed in bfloat16 or wider, within the bound.
No kernel may reach another device: no remote copies, remote signals or barrier semaphores. Data moves between devices by JAX's collectives and lax.ppermute only.
A program may use at most 128 MiB of HBM per device.

```python
import jax
import jax.numpy as jnp
from jax import lax

C = 128
V1 = 64
V2 = 128
FD = 4
H = 16
W = 64


def block_levels(rng, dims, shards, least, top_value):
    def one(axis_at, parts):
        heights = jax.random.uniform(jax.random.fold_in(jax.random.fold_in(rng, 6), axis_at), (parts,), jnp.float32, least / len(shards), top_value / len(shards))
        return jnp.repeat(jnp.exp(heights), dims[axis_at] // parts).reshape((-1,) + (1,) * (len(dims) - axis_at - 1))

    loudness = one(*shards[0])
    for cut in shards[1:]:
        loudness = loudness * one(*cut)
    return loudness


def normal_values(key, dims, width, limit, cuts=(), dtype=jnp.bfloat16):
    loudness = block_levels(key, dims, cuts, -0.22, 0.18) if cuts else 1.0
    entries = jax.random.normal(key, dims, jnp.float32) * width * loudness
    return jnp.minimum(jnp.maximum(entries, -limit), limit).astype(dtype)


def setup_inputs(seed: int = 0) -> dict:
    key_of = jax.random.split(jax.random.key(seed), 9)
    return {
        "dec_input": normal_values(key_of[0], (3, FD, H, W, C), 1.0, 6.0, ((2, 2), (3, 4))),
        "target": normal_values(key_of[1], (3, 3, FD, H, W), 1.0, 5.0, ((2, 4), (3, 2))),
        "conv_first": normal_values(key_of[2], (27 * C, C), (27 * C) ** -0.5, 0.109375),
        "conv_second": normal_values(key_of[3], (27 * C, C), (27 * C) ** -0.5, 0.109375),
        "rgb_weight": normal_values(key_of[4], (3, C), C ** -0.5, 0.5),
        "vgg_first": normal_values(key_of[5], (27, V1), 27 ** -0.5, 1.25),
        "vgg_second": normal_values(key_of[6], (9 * V1, V1), (9 * V1) ** -0.5, 0.25),
        "vgg_third": normal_values(key_of[7], (9 * V1, V2), (9 * V1) ** -0.5, 0.25),
    }


gelu_scale = 0.7978845608028654
gelu_cubic = 0.044715


def silu_slope(preact):
    sigmoid_value = jax.nn.sigmoid(preact)
    return sigmoid_value * (1.0 + preact * (1.0 - sigmoid_value))


def gelu_value(preact):
    return 0.5 * preact * (1.0 + jnp.tanh(gelu_scale * (preact + gelu_cubic * preact * preact * preact)))


def gelu_slope(preact):
    inner_tanh = jnp.tanh(gelu_scale * (preact + gelu_cubic * preact * preact * preact))
    return 0.5 * (1.0 + inner_tanh) + 0.5 * preact * (1.0 - inner_tanh * inner_tanh) * gelu_scale * (1.0 + 3.0 * gelu_cubic * preact * preact)


def conv_plane(images, weight):
    source_width = weight.shape[0] // 9
    kernel = weight.reshape(3, 3, source_width, weight.shape[1]).astype(jnp.float32)
    return lax.conv_general_dilated(images.astype(jnp.float32), kernel, (1, 1), "SAME", dimension_numbers=("NHWC", "HWIO", "NHWC"), precision=lax.Precision.HIGHEST, preferred_element_type=jnp.float32)


def flipped_plane(weight):
    source_width = weight.shape[0] // 9
    target_width = weight.shape[1]
    kernel = weight.reshape(3, 3, source_width, target_width)[::-1, ::-1]
    return jnp.transpose(kernel, (0, 1, 3, 2)).reshape(9 * target_width, source_width)


def conv_volume(volume, weight):
    source_width = weight.shape[0] // 27
    kernel = weight.reshape(3, 3, 3, source_width, weight.shape[1]).astype(jnp.float32)
    return lax.conv_general_dilated(volume[None].astype(jnp.float32), kernel, (1, 1, 1), "SAME", dimension_numbers=("NDHWC", "DHWIO", "NDHWC"), precision=lax.Precision.HIGHEST, preferred_element_type=jnp.float32)[0]


def flipped_volume(weight):
    source_width = weight.shape[0] // 27
    target_width = weight.shape[1]
    kernel = weight.reshape(3, 3, 3, source_width, target_width)[::-1, ::-1, ::-1]
    return jnp.transpose(kernel, (0, 1, 2, 4, 3)).reshape(27 * target_width, source_width)


def weight_gradient(source_cells, output_delta):
    frame_count, row_count, col_count, source_width = source_cells.shape
    padded = jnp.pad(source_cells, ((1, 1), (1, 1), (1, 1), (0, 0)))
    flat_delta = output_delta.reshape(-1, output_delta.shape[-1]).astype(jnp.float32)
    partial_terms = []
    for frame_step in range(3):
        for row_step in range(3):
            for col_step in range(3):
                shifted = padded[frame_step:frame_step + frame_count, row_step:row_step + row_count, col_step:col_step + col_count]
                shifted = shifted.reshape(-1, source_width).astype(jnp.float32)
                partial_terms.append(jnp.dot(shifted.T, flat_delta, precision=lax.Precision.HIGHEST, preferred_element_type=jnp.float32))
    return jnp.concatenate(partial_terms, axis=0).reshape(-1)


def pixel_gradient(images, guides, row_keep, vgg_first, vgg_second, vgg_third):
    cell_keep = row_keep[None, :, None, None]
    pool_keep = row_keep[::2][None, :, None, None]

    def features(source):
        first_plane = conv_plane(source, vgg_first)
        first_act = (gelu_value(first_plane) * cell_keep).astype(jnp.bfloat16)
        second_plane = conv_plane(first_act, vgg_second)
        second_feat = gelu_value(second_plane) * cell_keep
        image_count, row_count, col_count, channel_count = second_feat.shape
        pooled = second_feat.reshape(image_count, row_count // 2, 2, col_count // 2, 2, channel_count)
        pooled = (jnp.sum(pooled, axis=(2, 4)) * 0.25).astype(jnp.bfloat16)
        third_plane = conv_plane(pooled, vgg_third)
        third_feat = gelu_value(third_plane) * pool_keep
        return first_plane, second_plane, second_feat, third_plane, third_feat

    first_plane, second_plane, second_feat, third_plane, third_feat = features(images)
    guide_parts = features(guides)
    guide_second = guide_parts[2]
    guide_third = guide_parts[4]
    third_delta = ((64.0 / third_feat.shape[-1]) * (third_feat - guide_third) * gelu_slope(third_plane)).astype(jnp.bfloat16)
    pooled_grad = conv_plane(third_delta, flipped_plane(vgg_third))
    image_count, half_rows, half_cols, channel_count = pooled_grad.shape
    spread = jnp.broadcast_to(pooled_grad[:, :, None, :, None, :], (image_count, half_rows, 2, half_cols, 2, channel_count))
    spread = spread.reshape(image_count, 2 * half_rows, 2 * half_cols, channel_count)
    second_delta = ((0.25 * spread + (16.0 / channel_count) * (second_feat - guide_second)) * gelu_slope(second_plane) * cell_keep).astype(jnp.bfloat16)
    first_grad = conv_plane(second_delta, flipped_plane(vgg_second))
    first_delta = (first_grad * gelu_slope(first_plane) * cell_keep).astype(jnp.bfloat16)
    direct_term = (1.0 / 6.0) * (images.astype(jnp.float32) - guides.astype(jnp.float32))
    return conv_plane(first_delta, flipped_plane(vgg_first)) + direct_term


def reference(dec_input, target, conv_first, conv_second, rgb_weight, vgg_first, vgg_second, vgg_third):
    video_cells = dec_input.reshape(3 * FD, H, W, C)
    first_pre = conv_volume(video_cells, conv_first)
    first_out = jax.nn.silu(first_pre).astype(jnp.bfloat16)
    second_pre = conv_volume(first_out, conv_second)
    second_out = jax.nn.silu(second_pre).astype(jnp.bfloat16)
    colour = jnp.einsum("fhwc,kc->kfhw", second_out.astype(jnp.float32), rgb_weight.astype(jnp.float32), precision=lax.Precision.HIGHEST).astype(jnp.bfloat16)
    images = jnp.transpose(colour, (1, 2, 3, 0))
    guides = jnp.transpose(target.reshape(3, 3 * FD, H, W), (1, 2, 3, 0))
    row_keep = jnp.ones((H,), jnp.float32)
    pixel_grad = pixel_gradient(images, guides, row_keep, vgg_first, vgg_second, vgg_third)
    pixel_grad = jnp.transpose(pixel_grad, (3, 0, 1, 2))
    hidden_grad = jnp.einsum("kfhw,kc->fhwc", pixel_grad, rgb_weight.astype(jnp.float32), precision=lax.Precision.HIGHEST)
    decoder_second = (hidden_grad * silu_slope(second_pre)).astype(jnp.bfloat16)
    grad_second = weight_gradient(first_out, decoder_second)
    hidden_back = conv_volume(decoder_second, flipped_volume(conv_second))
    decoder_hidden = (hidden_back * silu_slope(first_pre)).astype(jnp.bfloat16)
    grad_first = weight_gradient(video_cells, decoder_hidden)
    return grad_first, grad_second
```

```python
import jax
import jax.numpy as jnp
from jax import lax
from jax.sharding import PartitionSpec as P

gelu_scale = 0.7978845608028654
gelu_cubic = 0.044715


def window_start(axis, tile, reach, total):
    size = min(total, tile + 2 * reach)
    return jnp.clip(lax.axis_index(axis) * tile - reach, 0, total - size), size


def exchange(shard, axis, dim, width):
    count, length = lax.axis_size(axis), shard.shape[dim]
    last = lax.slice_in_dim(shard, length - width, length, axis=dim)
    first = lax.slice_in_dim(shard, 0, width, axis=dim)
    before = lax.ppermute(last, axis, [(i, i + 1) for i in range(count - 1)])
    after = lax.ppermute(first, axis, [(i + 1, i) for i in range(count - 1)])
    return jnp.concatenate([before, shard, after], axis=dim)


def gather_plane(shard):
    count = lax.axis_size("row") * lax.axis_size("col")
    return lax.all_to_all(
        jnp.broadcast_to(shard[None], (count,) + shard.shape),
        ("row", "col"),
        split_axis=0,
        concat_axis=0,
        tiled=True,
    )


def reduce_plane(terms):
    count = lax.axis_size("row") * lax.axis_size("col")
    pieces = lax.all_to_all(
        terms.astype(jnp.bfloat16).reshape(count, -1),
        ("row", "col"),
        split_axis=0,
        concat_axis=0,
        tiled=True,
    )
    return jnp.sum(pieces.astype(jnp.float32), axis=0)


def inside(axis, tile, reach):
    total = tile * lax.axis_size(axis)
    at = lax.axis_index(axis) * tile - reach + jnp.arange(tile + 2 * reach)
    return (at >= 0) & (at < total)


def keep_inside(field, tile_rows, tile_cols, reach):
    rows = inside("row", tile_rows, reach)[None, :, None, None]
    cols = inside("col", tile_cols, reach)[None, None, :, None]
    return jnp.where(rows & cols, field, jnp.zeros_like(field))


def silu_slope(preact):
    sigmoid_value = jax.nn.sigmoid(preact)
    return sigmoid_value * (1.0 + preact * (1.0 - sigmoid_value))


def gelu_value(preact):
    return (
        0.5
        * preact
        * (1.0 + jnp.tanh(gelu_scale * (preact + gelu_cubic * preact * preact * preact)))
    )


def gelu_slope(preact):
    inner_tanh = jnp.tanh(gelu_scale * (preact + gelu_cubic * preact * preact * preact))
    return 0.5 * (1.0 + inner_tanh) + 0.5 * preact * (
        1.0 - inner_tanh * inner_tanh
    ) * gelu_scale * (1.0 + 3.0 * gelu_cubic * preact * preact)


def conv_plane(images, weight):
    source_width = weight.shape[0] // 9
    kernel = weight.reshape(3, 3, source_width, weight.shape[1])
    return lax.conv_general_dilated(
        images,
        kernel,
        (1, 1),
        "SAME",
        dimension_numbers=("NHWC", "HWIO", "NHWC"),
        preferred_element_type=jnp.float32,
    )


def flipped_plane(weight):
    source_width = weight.shape[0] // 9
    target_width = weight.shape[1]
    kernel = weight.reshape(3, 3, source_width, target_width)[::-1, ::-1]
    return jnp.transpose(kernel, (0, 1, 3, 2)).reshape(9 * target_width, source_width)


def conv_volume(field, weight):
    source_width = weight.shape[0] // 27
    kernel = weight.reshape(3, 3, 3, source_width, weight.shape[1])
    return lax.conv_general_dilated(
        field[None],
        kernel,
        (1, 1, 1),
        ((1, 1), (0, 0), (0, 0)),
        dimension_numbers=("NDHWC", "DHWIO", "NDHWC"),
        preferred_element_type=jnp.float32,
    )[0]


def flipped_volume(weight):
    source_width = weight.shape[0] // 27
    target_width = weight.shape[1]
    kernel = weight.reshape(3, 3, 3, source_width, target_width)[::-1, ::-1, ::-1]
    return jnp.transpose(kernel, (0, 1, 2, 4, 3)).reshape(27 * target_width, source_width)


def pixel_gradient(images, guides, vgg_first, vgg_second, vgg_third):
    def features(source):
        first_plane = conv_plane(source, vgg_first)
        first_act = gelu_value(first_plane).astype(jnp.bfloat16)
        second_plane = conv_plane(first_act, vgg_second)
        second_feat = gelu_value(second_plane)
        image_count, row_count, col_count, channel_count = second_feat.shape
        pooled = second_feat.reshape(
            image_count, row_count // 2, 2, col_count // 2, 2, channel_count
        )
        pooled = (jnp.sum(pooled, axis=(2, 4)) * 0.25).astype(jnp.bfloat16)
        third_plane = conv_plane(pooled, vgg_third)
        third_feat = gelu_value(third_plane)
        return (first_plane, second_plane, second_feat, third_plane, third_feat)

    first_plane, second_plane, second_feat, third_plane, third_feat = features(images)
    guide_parts = features(guides)
    guide_second = guide_parts[2]
    guide_third = guide_parts[4]
    third_delta = (
        64.0 / third_feat.shape[-1] * (third_feat - guide_third) * gelu_slope(third_plane)
    ).astype(jnp.bfloat16)
    pooled_grad = conv_plane(third_delta, flipped_plane(vgg_third))
    image_count, half_rows, half_cols, channel_count = pooled_grad.shape
    spread = jnp.broadcast_to(
        pooled_grad[:, :, None, :, None, :],
        (image_count, half_rows, 2, half_cols, 2, channel_count),
    )
    spread = spread.reshape(image_count, 2 * half_rows, 2 * half_cols, channel_count)
    second_delta = (
        (0.25 * spread + 16.0 / channel_count * (second_feat - guide_second))
        * gelu_slope(second_plane)
    ).astype(jnp.bfloat16)
    first_grad = conv_plane(second_delta, flipped_plane(vgg_second))
    first_delta = (first_grad * gelu_slope(first_plane)).astype(jnp.bfloat16)
    direct_term = 1.0 / 6.0 * (images.astype(jnp.float32) - guides.astype(jnp.float32))
    return conv_plane(first_delta, flipped_plane(vgg_first)) + direct_term


def tap_gradient(field, delta, out_rows):
    frames, rows, cols, channels = delta.shape
    groups = lax.axis_size("grp")
    group = lax.axis_index("grp")
    first_row = group * out_rows
    taps = max(
        -(-(g + 1) * out_rows // channels) - g * out_rows // channels for g in range(groups)
    )
    first_tap = first_row // channels
    padded = jnp.pad(field, ((1, 1), (0, 0), (0, 0), (0, 0)))
    flat_delta = delta.reshape(-1, channels)
    pieces = []
    for step in range(taps):
        tap = jnp.minimum(first_tap + step, 26)
        shifted = lax.dynamic_slice(
            padded,
            (tap // 9, tap // 3 % 3, tap % 3, 0),
            (frames, rows, cols, padded.shape[-1]),
        )
        pieces.append(shifted.reshape(frames * rows * cols, -1))
    patches = jnp.concatenate(pieces, axis=-1)
    terms = jnp.dot(patches.T, flat_delta, preferred_element_type=jnp.float32)
    return lax.dynamic_slice_in_dim(terms, first_row - first_tap * channels, out_rows, axis=0)


def local(dec_input, target, conv_first, conv_second, rgb_weight, vgg_first, vgg_second, vgg_third):
    groups = lax.axis_size("grp")
    row_count, col_count = lax.axis_size("row"), lax.axis_size("col")
    blocks, block_frames, tile_rows, tile_cols, channels = dec_input.shape
    frames = blocks * block_frames
    height, width = tile_rows * row_count, tile_cols * col_count
    cells = dec_input.reshape(frames, tile_rows, tile_cols, channels)

    guides = gather_plane(target)
    per_column = target.shape[2]
    guides = guides.reshape(row_count, col_count, 3, blocks, per_column, tile_rows, width)
    guides = jnp.transpose(guides, (3, 1, 4, 0, 5, 6, 2)).reshape(frames, height, width, 3)

    wide = exchange(exchange(cells, "row", 1, 3), "col", 2, 3)
    first_pre = conv_volume(wide, conv_first)
    first_out = keep_inside(
        jax.nn.silu(first_pre).astype(jnp.bfloat16), tile_rows, tile_cols, 2
    )
    second_pre = conv_volume(first_out, conv_second)
    second_out = jax.nn.silu(second_pre[:, 1:-1, 1:-1]).astype(jnp.bfloat16)
    colour = jnp.einsum(
        "fhwc,kc->kfhw", second_out, rgb_weight, preferred_element_type=jnp.float32
    ).astype(jnp.bfloat16)
    images = gather_plane(colour)
    images = images.reshape(row_count, col_count, 3, frames, tile_rows, tile_cols)
    images = jnp.transpose(images, (3, 0, 4, 1, 5, 2)).reshape(frames, height, width, 3)

    row_start, row_size = window_start("row", tile_rows, 10, height)
    col_start, col_size = window_start("col", tile_cols, 10, width)
    corner = (0, row_start, col_start, 0)
    view = (frames, row_size, col_size, 3)
    gradient = pixel_gradient(
        lax.dynamic_slice(images, corner, view),
        lax.dynamic_slice(guides, corner, view),
        vgg_first,
        vgg_second,
        vgg_third,
    )
    gradient = jnp.pad(gradient, ((0, 0), (1, 1), (1, 1), (0, 0)))
    pixel_tile = lax.dynamic_slice(
        gradient,
        (
            0,
            lax.axis_index("row") * tile_rows - row_start,
            lax.axis_index("col") * tile_cols - col_start,
            0,
        ),
        (frames, tile_rows + 2, tile_cols + 2, 3),
    )
    hidden_grad = jnp.einsum(
        "fhwk,kc->fhwc",
        pixel_tile,
        rgb_weight.astype(jnp.float32),
        precision=lax.Precision.HIGHEST,
    )
    decoder_second = keep_inside(
        (hidden_grad * silu_slope(second_pre)).astype(jnp.bfloat16), tile_rows, tile_cols, 1
    )
    out_rows = conv_first.shape[0] // groups
    grad_second = tap_gradient(
        first_out[:, 1:-1, 1:-1], decoder_second[:, 1:-1, 1:-1], out_rows
    )
    hidden_back = conv_volume(decoder_second, flipped_volume(conv_second))
    decoder_hidden = (hidden_back * silu_slope(first_pre[:, 2:-2, 2:-2])).astype(jnp.bfloat16)
    grad_first = tap_gradient(wide[:, 2:-2, 2:-2], decoder_hidden, out_rows)
    return reduce_plane(grad_first), reduce_plane(grad_second)


def solution(mesh):
    in_specs = (
        P(None, None, "row", "col", None),
        P(None, None, "col", "row", None),
        P(),
        P(),
        P(),
        P(),
        P(),
        P(),
    )
    out_specs = (P(("grp", "row", "col")), P(("grp", "row", "col")))
    return jax.shard_map(local, mesh=mesh, in_specs=in_specs, out_specs=out_specs, check_vma=False)
```

```python
import functools

import jax
import jax.numpy as jnp
from jax import lax
from jax.experimental import pallas as pl
from jax.experimental.pallas import tpu as pltpu
from jax.sharding import PartitionSpec as P

gelu_scale = 0.7978845608028654
gelu_cubic = 0.044715
plane = ("row", "col")
vmem_bytes = 62 * 2**20


def repeat(count, body, unroll=1):
    lax.fori_loop(0, count, lambda i, carry: (body(i), carry)[1], 0, unroll=unroll)


def matmul(left, right):
    return jnp.dot(left, right, preferred_element_type=jnp.float32)


def gelu_tanh(z):
    return jnp.tanh(gelu_scale * (z + gelu_cubic * z * z * z))


def gelu_slope(z, t):
    return 0.5 * (1.0 + t) + 0.5 * z * (1.0 - t * t) * gelu_scale * (
        1.0 + 3.0 * gelu_cubic * z * z
    )


def corner(rows, cols, height, width, view_rows, view_cols):
    top, left = lax.axis_index("row") * rows, lax.axis_index("col") * cols
    return (
        top,
        left,
        jnp.clip(top - 10, 0, height - view_rows),
        jnp.clip(left - 10, 0, width - view_cols),
    )


def col_mask(first_col, cols, width, slots, frames):
    at = lax.broadcasted_iota(jnp.int32, (cols * slots, 1), 0)
    col = at // slots + first_col
    return (at % slots < frames) & (col >= 0) & (col < width)


def conv_frames(source, row, cols, weight):
    slots, channels = source.shape[-2:]
    slabs = [
        source[row + dr, pl.ds(dc, cols)].reshape(cols * slots, channels)
        for dr in range(3)
        for dc in range(3)
    ]
    sums = matmul(jnp.concatenate(slabs, axis=1), weight)
    count = cols * slots
    return (
        pltpu.roll(sums[:, :channels], 1, 0)
        + sums[:, channels : 2 * channels]
        + pltpu.roll(sums[:, 2 * channels :], count - 1, 0)
    )


def frame_weight(ref):
    third = ref.shape[0] // 3
    return jnp.concatenate([ref[pl.ds(third * k, third)] for k in range(3)], axis=1)


def forward_kernel(
    frames, own, up, down, left, right, first, second, project,
    cells_out, hidden_out, slope_first, slope_second, colour, cells, hidden, spread_weight,
):
    rows, cols, slots, channels = own.shape
    half = slots // 2
    height, width = rows * lax.axis_size("row"), cols * lax.axis_size("col")
    top, left_col = lax.axis_index("row") * rows, lax.axis_index("col") * cols
    cells[3 : 3 + rows, 3 : 3 + cols] = own[...]
    cells[0:3, 3 : 3 + cols] = up[...]
    cells[3 + rows :, 3 : 3 + cols] = down[...]
    cells[:, 0:3] = left[...]
    cells[:, 3 + cols :] = right[...]
    cells_out[...] = cells[2 : 4 + rows, 2 : 4 + cols]
    spread_weight[...] = frame_weight(first)

    def first_layer(r):
        pre = conv_frames(cells, r, cols + 4, spread_weight[...])
        row = top - 2 + r
        keep = col_mask(left_col - 2, cols + 4, width, slots, frames) & (
            (row >= 0) & (row < height)
        )
        gate = 0.5 + 0.5 * jnp.tanh(0.5 * pre)
        out = jnp.where(keep, pre * gate, 0.0).astype(jnp.bfloat16)
        hidden[r] = out.reshape(cols + 4, slots, channels)
        slope = jnp.where(keep, gate * (1.0 + pre * (1.0 - gate)), 0.0)

        @pl.when((r >= 2) & (r < 2 + rows))
        def _():
            slope_first[r - 2] = slope[2 * slots : (2 + cols) * slots]

    repeat(rows + 4, first_layer, 2)
    hidden_out[...] = hidden[1 : 3 + rows, 1 : 3 + cols]
    spread_weight[...] = frame_weight(second)

    def second_layer(r):
        pre = conv_frames(hidden, r, cols + 2, spread_weight[...])
        row = top - 1 + r
        keep = col_mask(left_col - 1, cols + 2, width, slots, frames) & (
            (row >= 0) & (row < height)
        )
        gate = 0.5 + 0.5 * jnp.tanh(0.5 * pre)
        slope_second[r] = jnp.where(keep, gate * (1.0 + pre * (1.0 - gate)), 0.0)
        out = jnp.where(keep, pre * gate, 0.0)[slots : (1 + cols) * slots]
        out = out.reshape(cols, 2, half, channels)
        both = jnp.concatenate(
            [out[:, k].reshape(cols * half, channels) for k in range(2)], axis=1
        ).astype(jnp.bfloat16)

        @pl.when((r >= 1) & (r < 1 + rows))
        def _():
            colour[r - 1] = lax.dot_general(
                project[...], both, (((1,), (1,)), ((), ())),
                preferred_element_type=jnp.float32,
            ).astype(jnp.bfloat16)

    repeat(rows + 2, second_layer, 2)


def image_line(images, row, rows, cols, width, half, left):
    parts = lax.axis_size("col")
    line = jnp.concatenate(
        [images[(row // rows) * parts + k, row % rows].astype(jnp.float32) for k in range(parts)],
        axis=1,
    )
    span = width * half
    return pltpu.roll(line, lax.rem(span - left * half, span), 1)


def plane_slabs(wide, narrow, row, count, half):
    pieces = []
    for dr in range(3):
        pieces.append(wide[row + dr, pl.ds(0, count)])
        if half % 16:
            pieces.append(narrow[row + dr])
        else:
            pieces.append(wide[row + dr, pl.ds(half, count)])
        pieces.append(wide[row + dr, pl.ds(2 * half, count)])
    return jnp.concatenate(pieces, axis=1)


def store_slab(wide, narrow, row, value, half):
    wide[row] = value.astype(jnp.bfloat16)
    if half % 16:
        narrow[row] = value[half : value.shape[0] - half].astype(jnp.bfloat16)


def store_wide(wide, narrow, row, value, half):
    edge = jnp.zeros((half, value.shape[1]), jnp.float32)
    store_slab(wide, narrow, row, jnp.concatenate([edge, value, edge], axis=0), half)


def kept_row(row, first, number):
    return jnp.clip(row - first, -1, number) + 1


def clear_edges(wide, narrow):
    for ref in (wide, narrow):
        for at in (0, ref.shape[0] - 1):
            ref[at] = jnp.zeros(ref.shape[1:], ref.dtype)


def features(
    images, guides, geometry, weight_1, weight_2, weight_3,
    lines, wide_1, narrow_1, wide_3, narrow_3, on_first, on_second, on_third,
):
    rows, cols, height, width, view_rows, view_cols, half, view_top, view_left = geometry
    count = view_cols * half
    lanes = lines.shape[2]
    span = width * half
    lane = lax.broadcasted_iota(jnp.int32, (8, lanes), 1)

    def line_step(w):
        line = image_line(images, view_top + w, rows, cols, width, half, view_left)
        before = pltpu.roll(line, half, 1)[:, :lanes]
        after = pltpu.roll(line, span - half, 1)[:, :lanes]
        lines[w + 1] = jnp.concatenate(
            [
                jnp.where(lane < half, 0.0, before),
                line[:, :lanes],
                jnp.where(lane >= count - half, 0.0, after),
            ],
            axis=0,
        )

    lines[0] = jnp.zeros(lines.shape[1:], jnp.float32)
    lines[view_rows + 1] = jnp.zeros(lines.shape[1:], jnp.float32)
    repeat(view_rows, line_step, 2)
    clear_edges(wide_1, narrow_1)
    clear_edges(wide_3, narrow_3)

    def first_step(w):
        pieces = [lines[w], lines[w + 1], lines[w + 2]]
        if guides is not None:
            pieces.append(
                image_line(guides, view_top + w, rows, cols, width, half, view_left)[:, :lanes]
            )
        filled = sum(piece.shape[0] for piece in pieces)
        pieces.append(jnp.zeros((128 - filled, lanes), jnp.float32))
        patches = jnp.concatenate(pieces, axis=0).T[:count].astype(jnp.bfloat16)
        plane_1 = matmul(patches, weight_1[...])
        on_first(w, plane_1)
        z = plane_1[:, :128]
        store_wide(wide_1, narrow_1, w + 1, 0.5 * z * (1.0 + gelu_tanh(z)), half)

    repeat(view_rows, first_step, 2)

    def second_step(q):
        total = 0.0
        for part in range(2):
            w = 2 * q + part
            z = matmul(plane_slabs(wide_1, narrow_1, w, count, half), weight_2[...])
            value = 0.5 * z * (1.0 + gelu_tanh(z))
            on_second(w, z, value)
            total = total + value
        pooled = total.reshape(view_cols // 2, 2, half, 128)
        pooled = 0.25 * (pooled[:, 0] + pooled[:, 1])
        store_wide(wide_3, narrow_3, q + 1, pooled.reshape(count // 2, 128), half)

    repeat(view_rows // 2, second_step)

    def third_step(q):
        on_third(q, matmul(plane_slabs(wide_3, narrow_3, q, count // 2, half), weight_3[...]))

    repeat(view_rows // 2, third_step, 2)


def guide_kernel(
    tile, guides, weight_1, weight_2, weight_3, guide_2, guide_3,
    lines, wide_1, narrow_1, wide_3, narrow_3,
):
    rows, cols, half = tile
    height, width = rows * lax.axis_size("row"), cols * lax.axis_size("col")
    view_rows, view_cols = min(height, rows + 20), min(width, cols + 20)
    top, _, view_top, view_left = corner(rows, cols, height, width, view_rows, view_cols)

    def on_second(w, z, value):
        guide_2[kept_row(view_top + w, top - 3, rows + 6), pl.ds(3 * half, view_cols * half)] = value

    def on_third(q, z):
        guide_3[q] = 0.5 * z * (1.0 + gelu_tanh(z))

    features(
        guides, None,
        (rows, cols, height, width, view_rows, view_cols, half, view_top, view_left),
        weight_1, weight_2, weight_3, lines, wide_1, narrow_1, wide_3, narrow_3,
        lambda w, z: None, on_second, on_third,
    )


def gradient_taps(source, delta, shifted, sums, first_tap):
    rows = delta.shape[0]
    slots, channels = source.shape[-2:]
    cols = source.shape[1] - 2
    count = cols * slots

    def turn(r):
        block = delta[r].astype(jnp.float32)
        for dt in range(3):
            moved = block if dt == 1 else pltpu.roll(block, (dt - 1) % count, 0)
            shifted[dt, r] = moved.T.astype(jnp.bfloat16)

    repeat(rows, turn, 2)

    def tap_step(step):
        tap = jnp.minimum(first_tap + step, 26)
        dt, dr, dc = tap // 9, tap // 3 % 3, tap % 3
        total = 0.0
        for r in range(rows):
            slab = source[r + dr, pl.ds(dc, cols)].reshape(count, channels)
            total = total + matmul(shifted[dt, r], slab)
        sums[pl.ds(pl.multiple_of(step * channels, channels), channels)] = total.T

    repeat(sums.shape[0] // channels, tap_step)


def backward_kernel(
    frames, out_rows, images, guides, guide_2, guide_3, slope_first, slope_second, cells, hidden,
    weight_1, weight_2, weight_3, back_3, back_2, back_1, paint, back_second,
    terms,
    lines, wide_1, narrow_1, wide_3, narrow_3, plane_1, plane_2, differ, wide_g, narrow_g, spread,
    wide_b, narrow_b, wide_a, narrow_a, delta_second, delta_own, shifted, sums,
):
    slots, channels = cells.shape[-2:]
    rows, cols, half = cells.shape[0] - 2, cells.shape[1] - 2, slots // 2
    height, width = rows * lax.axis_size("row"), cols * lax.axis_size("col")
    view_rows, view_cols = min(height, rows + 20), min(width, cols + 20)
    top, left, view_top, view_left = corner(rows, cols, height, width, view_rows, view_cols)
    count = view_cols * half
    body = pl.ds(3 * half, count)

    def on_first(w, z):
        row = view_top + w
        plane_1[kept_row(row, top - 2, rows + 4), body] = z[:, :128]
        differ[kept_row(row, top - 1, rows + 2), body] = z[:, 128:]

    def on_second(w, z, value):
        plane_2[kept_row(view_top + w, top - 3, rows + 6), body] = z

    clear_edges(wide_g, narrow_g)

    def on_third(q, z):
        t = gelu_tanh(z)
        delta = (64.0 / (z.shape[1] // 2)) * (0.5 * z * (1.0 + t) - guide_3[q]) * gelu_slope(z, t)
        store_wide(wide_g, narrow_g, q + 1, delta, half)

    features(
        images, guides,
        (rows, cols, height, width, view_rows, view_cols, half, view_top, view_left),
        weight_1, weight_2, weight_3, lines, wide_1, narrow_1, wide_3, narrow_3,
        on_first, on_second, on_third,
    )

    def pool_step(q):
        grad = 0.25 * matmul(plane_slabs(wide_g, narrow_g, q, count // 2, half), back_3[...])
        grad = grad.reshape(view_cols // 2, 1, half, 128)
        grad = jnp.concatenate([grad, grad], axis=1)
        pool_row = view_top // 2 + q
        spread[kept_row(pool_row, top // 2 - 2, rows // 2 + 4), body] = grad.reshape(count, 128)

    repeat(view_rows // 2, pool_step, 2)

    def at(reach, a, number):
        row = top - reach + a
        keep = col_mask(left - reach, cols + 2 * reach, width, half, half) & (
            (row >= 0) & (row < height)
        )
        start = pl.multiple_of((left - view_left + 3 - reach) * half, half)
        return keep, pl.ds(start, number)

    def second_delta(a):
        number = (cols + 6) * half
        keep, span = at(3, a, number)
        z = plane_2[a + 1, span]
        t = gelu_tanh(z)
        value = 0.5 * z * (1.0 + t)
        delta = spread[(a + 1) // 2 + 1, span] + (16.0 / (z.shape[1] // 2)) * (value - guide_2[a + 1, span])
        delta = jnp.where(keep, delta * gelu_slope(z, t), 0.0)
        store_slab(wide_b, narrow_b, a, delta, half)

    repeat(rows + 6, second_delta)

    def first_delta(a):
        number = (cols + 4) * half
        keep, span = at(2, a, number)
        grad = matmul(plane_slabs(wide_b, narrow_b, a, number, half), back_2[...])
        z = plane_1[a + 1, span]
        delta = jnp.where(keep, grad * gelu_slope(z, gelu_tanh(z)), 0.0)
        store_slab(wide_a, narrow_a, a, delta, half)

    repeat(rows + 4, first_delta, 2)

    def pixel_step(a):
        number = (cols + 2) * half
        keep, span = at(1, a, number)
        grad = matmul(plane_slabs(wide_a, narrow_a, a, number, half), back_1[...])
        grad = jnp.where(keep, grad + (1.0 / 6.0) * differ[a + 1, span], 0.0)
        painted = matmul(grad.astype(jnp.bfloat16), paint[...])
        painted = jnp.concatenate(
            [
                painted[:, k * channels : (k + 1) * channels].reshape(cols + 2, 1, half, channels)
                for k in range(2)
            ],
            axis=1,
        ).reshape((cols + 2) * slots, channels)
        delta = (painted * slope_second[a]).astype(jnp.bfloat16)
        delta_second[a] = delta.reshape(cols + 2, slots, channels)

    repeat(rows + 2, pixel_step, 2)

    first_row = lax.axis_index("grp") * out_rows
    first_tap = first_row // channels
    skip = pl.multiple_of(first_row - first_tap * channels, 32)
    device = lax.axis_index("row") * lax.axis_size("col") + lax.axis_index("col")

    def put(which):
        value = sums[pl.ds(skip, out_rows)].astype(jnp.float32)
        if len(terms.shape) == 3:
            terms[which] = value.astype(jnp.bfloat16)
        else:
            chunks, _, size, _ = terms.shape
            for k in range(chunks):
                piece = value[k * size : (k + 1) * size].astype(jnp.bfloat16)
                terms[lax.rem(k - device + chunks, chunks), which] = piece

    def own_step(r):
        delta_own[r] = delta_second[r + 1, 1 : 1 + cols].reshape(cols * slots, channels)

    repeat(rows, own_step)
    gradient_taps(hidden, delta_own, shifted, sums, first_tap)
    put(1)

    def back_step(r):
        back = conv_frames(delta_second, r, cols, back_second[...])
        delta_own[r] = (back * slope_first[r]).astype(jnp.bfloat16)

    repeat(rows, back_step, 2)
    gradient_taps(cells, delta_own, shifted, sums, first_tap)
    put(0)


def twice(blocks):
    zero = jnp.zeros_like(blocks)
    return jnp.concatenate(
        [jnp.concatenate([blocks, zero], axis=2), jnp.concatenate([zero, blocks], axis=2)], axis=1
    )


def turned(weight):
    taps = weight.reshape(9, -1, weight.shape[1])[::-1]
    return jnp.transpose(taps, (0, 2, 1))


def plane_weights(vgg_first, vgg_second, vgg_third, rgb_weight):
    first = jnp.pad(twice(vgg_first.reshape(9, 3, -1)), ((0, 0), (0, 2), (0, 0)))
    first = jnp.pad(first.reshape(72, -1), ((0, 56), (0, 0)))
    pick = jnp.pad(jnp.eye(6, 128, dtype=jnp.bfloat16), ((0, 2), (0, 0)))
    pick = jnp.concatenate(
        [jnp.zeros((32, 128), jnp.bfloat16), pick, jnp.zeros((32, 128), jnp.bfloat16), -pick],
        axis=0,
    )
    pick = jnp.pad(pick, ((0, 48), (0, 0)))
    second = twice(vgg_second.reshape(9, 64, 64)).reshape(9 * 128, 128)
    third = twice(vgg_third.reshape(9, 64, 128)).reshape(9 * 128, 256)
    back_third = twice(turned(vgg_third)).reshape(9 * 256, 128)
    back_second = twice(turned(vgg_second)).reshape(9 * 128, 128)
    back_first = twice(turned(vgg_first))
    back_first = jnp.pad(back_first, ((0, 0), (0, 0), (0, 122))).reshape(9 * 128, 128)
    paint = twice(rgb_weight[None])[0]
    return (
        first,
        jnp.concatenate([first, pick], axis=1),
        second,
        third,
        back_third,
        back_second,
        back_first,
        jnp.pad(paint, ((0, 2), (0, 0))),
        jnp.pad(paint, ((0, 122), (0, 0))),
    )


def call(kernel, outs, scratch):
    return pl.pallas_call(
        kernel,
        out_shape=outs,
        scratch_shapes=[pltpu.VMEM(*shape) for shape in scratch],
        compiler_params=pltpu.CompilerParams(vmem_limit_bytes=vmem_bytes),
    )


def exchange(shard, axis, dim, width):
    count, length = lax.axis_size(axis), shard.shape[dim]
    last = lax.slice_in_dim(shard, length - width, length, axis=dim)
    first = lax.slice_in_dim(shard, 0, width, axis=dim)
    before = lax.ppermute(last, axis, [(i, i + 1) for i in range(count - 1)])
    after = lax.ppermute(first, axis, [(i + 1, i) for i in range(count - 1)])
    return before, after


def gather_plane(shard):
    count = lax.axis_size("row") * lax.axis_size("col")
    return lax.all_to_all(
        jnp.broadcast_to(shard[None], (count,) + shard.shape),
        plane,
        split_axis=0,
        concat_axis=0,
        tiled=True,
    )


def guide_lines(target, slots):
    row_count, col_count = lax.axis_size("row"), lax.axis_size("col")
    _, blocks, own, rows, width = target.shape
    cols, half = width // col_count, slots // 2
    frames = blocks * own * col_count
    whole = gather_plane(target)
    whole = whole.reshape(row_count, col_count, 3, blocks, own, rows, width)
    whole = jnp.transpose(whole, (2, 3, 1, 4, 0, 5, 6))
    whole = whole.reshape(3, frames, row_count, rows, col_count, cols)
    whole = jnp.pad(whole, ((0, 0), (0, slots - frames)) + ((0, 0),) * 4)
    whole = whole.reshape(3, 2, half, row_count, rows, col_count, cols)
    whole = jnp.transpose(whole, (3, 5, 4, 1, 0, 6, 2))
    whole = whole.reshape(row_count * col_count, rows, 6, cols * half)
    return jnp.pad(whole, ((0, 0), (0, 0), (0, 2), (0, 0)))


def local(dec_input, target, conv_first, conv_second, rgb_weight, vgg_first, vgg_second, vgg_third):
    f32, bf16 = jnp.float32, jnp.bfloat16
    row_count, col_count = lax.axis_size("row"), lax.axis_size("col")
    blocks, block_frames, rows, cols, channels = dec_input.shape
    frames = blocks * block_frames
    slots = -(-(frames + 1) // 16) * 16
    half = slots // 2
    height, width = rows * row_count, cols * col_count
    view_rows, view_cols = min(height, rows + 20), min(width, cols + 20)
    count = view_cols * half
    lanes = -(-count // 128) * 128

    own = jnp.transpose(dec_input.reshape(frames, rows, cols, channels), (1, 2, 0, 3))
    own = jnp.pad(own, ((0, 0), (0, 0), (0, slots - frames), (0, 0)))
    up, down = exchange(own, "row", 0, 3)
    tall = jnp.concatenate([up, own, down], axis=0)
    before, after = exchange(tall, "col", 1, 3)

    (
        first_plain, first_pick, second, third, back_third, back_second, back_first,
        project, paint,
    ) = plane_weights(vgg_first, vgg_second, vgg_third, rgb_weight)
    back_volume = conv_second.reshape(3, 9, channels, channels)[::-1, ::-1]
    back_volume = jnp.transpose(back_volume, (1, 3, 0, 2)).reshape(9 * channels, 3 * channels)

    guides = guide_lines(target, slots)
    thin = half % 16 != 0
    feature_scratch = [
        ((view_rows + 2, 24, lanes), f32),
        ((view_rows + 2, count + 2 * half, 128), bf16),
        ((view_rows + 2, count if thin else 16, 128), bf16),
        ((view_rows // 2 + 2, count // 2 + 2 * half, 128), bf16),
        ((view_rows // 2 + 2, count // 2 if thin else 16, 128), bf16),
    ]
    guide_2, guide_3 = call(
        functools.partial(guide_kernel, (rows, cols, half)),
        (
            jax.ShapeDtypeStruct((rows + 8, count + 6 * half, 128), f32),
            jax.ShapeDtypeStruct((view_rows // 2, count // 2, 256), f32),
        ),
        feature_scratch,
    )(guides, first_plain, second, third)

    cells, hidden, slope_first, slope_second, colour = call(
        functools.partial(forward_kernel, frames),
        (
            jax.ShapeDtypeStruct((rows + 2, cols + 2, slots, channels), bf16),
            jax.ShapeDtypeStruct((rows + 2, cols + 2, slots, channels), bf16),
            jax.ShapeDtypeStruct((rows, cols * slots, channels), f32),
            jax.ShapeDtypeStruct((rows + 2, (cols + 2) * slots, channels), f32),
            jax.ShapeDtypeStruct((rows, 8, cols * half), bf16),
        ),
        [
            ((rows + 6, cols + 6, slots, channels), bf16),
            ((rows + 4, cols + 4, slots, channels), bf16),
            ((9 * channels, 3 * channels), bf16),
        ],
    )(own, up, down, before, after, conv_first, conv_second, project)

    images = gather_plane(colour)
    groups, devices = lax.axis_size("grp"), row_count * col_count
    out_rows = conv_first.shape[0] // groups
    taps = max(
        -(-(g + 1) * out_rows // channels) - g * out_rows // channels for g in range(groups)
    )
    even = out_rows % devices == 0
    out_shape = (
        (devices, 2, out_rows // devices, channels) if even else (2, out_rows, channels)
    )
    wide_count = count + 6 * half
    terms = call(
        functools.partial(backward_kernel, frames, out_rows),
        jax.ShapeDtypeStruct(out_shape, bf16),
        feature_scratch
        + [
            ((rows + 6, wide_count, 128), f32),
            ((rows + 8, wide_count, 128), f32),
            ((rows + 4, wide_count, 128), f32),
            ((view_rows // 2 + 2, count // 2 + 2 * half, 256), bf16),
            ((view_rows // 2 + 2, count // 2 if thin else 16, 256), bf16),
            ((rows // 2 + 6, wide_count, 128), f32),
            ((rows + 6, (cols + 6) * half, 128), bf16),
            ((rows + 6, (cols + 4) * half if thin else 16, 128), bf16),
            ((rows + 4, (cols + 4) * half, 128), bf16),
            ((rows + 4, (cols + 2) * half if thin else 16, 128), bf16),
            ((rows + 2, cols + 2, slots, channels), bf16),
            ((rows, cols * slots, channels), bf16),
            ((3, rows, channels, cols * slots), bf16),
            ((taps * channels, channels), f32),
        ],
    )(
        images, guides, guide_2, guide_3, slope_first, slope_second, cells, hidden,
        first_pick, second, third, back_third, back_second, back_first, paint, back_volume,
    )

    if even:
        pieces = [terms[0]]
        for step in range(1, devices):
            ring = [(i, (i + step) % devices) for i in range(devices)]
            pieces.append(lax.ppermute(terms[step], plane, ring))
        total = sum(piece.astype(f32) for piece in pieces)
    else:
        pieces = jnp.swapaxes(terms.reshape(2, devices, -1), 0, 1)
        pieces = lax.all_to_all(pieces, plane, split_axis=0, concat_axis=0, tiled=True)
        total = jnp.sum(pieces.astype(f32), axis=0)
    return total[0].reshape(-1), total[1].reshape(-1)


def solution(mesh):
    in_specs = (
        P(None, None, "row", "col", None),
        P(None, None, "col", "row", None),
        P(),
        P(),
        P(),
        P(),
        P(),
        P(),
    )
    out_specs = (P(("grp", "row", "col")), P(("grp", "row", "col")))
    return jax.shard_map(local, mesh=mesh, in_specs=in_specs, out_specs=out_specs, check_vma=False)
```

```python
import functools

import jax
import jax.numpy as jnp
from jax import lax
from jax.experimental import pallas as pl
from jax.experimental.pallas import tpu as pltpu
from jax.sharding import PartitionSpec as P

gelu_scale = 0.7978845608028654
gelu_cubic = 0.044715
plane = ("row", "col")
vmem_bytes = 62 * 2**20


def repeat(count, body, unroll=1):
    lax.fori_loop(0, count, lambda i, carry: (body(i), carry)[1], 0, unroll=unroll)


def matmul(left, right):
    return jnp.dot(left, right, preferred_element_type=jnp.float32)


def gelu_tanh(z):
    return jnp.tanh(gelu_scale * (z + gelu_cubic * z * z * z))


def gelu_slope(z, t):
    return 0.5 * (1.0 + t) + 0.5 * z * (1.0 - t * t) * gelu_scale * (
        1.0 + 3.0 * gelu_cubic * z * z
    )


def split(rows, frames_own):
    small = frames_own <= 4 and lax.axis_size("row") == 2 and rows % 4 == 0
    return (2, 4) if small else (1, 8)


def corner(rows, cols):
    height, width = rows * lax.axis_size("row"), cols * lax.axis_size("col")
    view_rows, view_cols = min(height, rows + 20), min(width, cols + 20)
    top, left = lax.axis_index("row") * rows, lax.axis_index("col") * cols
    view_top = jnp.clip(top - 10, 0, height - view_rows)
    view_left = jnp.clip(left - 10, 0, width - view_cols)
    return top, left, view_top, view_left


def col_mask(first_col, cols, width, slots, frames):
    at = lax.broadcasted_iota(jnp.int32, (cols * slots, 1), 0)
    col = at // slots + first_col
    return (at % slots < frames) & (col >= 0) & (col < width)


def conv_frames(source, row, cols, weight):
    slots, channels = source.shape[-2:]
    slabs = [
        source[row + dr, pl.ds(dc, cols)].reshape(cols * slots, channels)
        for dr in range(3)
        for dc in range(3)
    ]
    sums = matmul(jnp.concatenate(slabs, axis=1), weight)
    count = cols * slots
    return (
        pltpu.roll(sums[:, :channels], 1, 0)
        + sums[:, channels : 2 * channels]
        + pltpu.roll(sums[:, 2 * channels :], count - 1, 0)
    )


def frame_weight(ref):
    third = ref.shape[0] // 3
    return jnp.concatenate([ref[pl.ds(third * k, third)] for k in range(3)], axis=1)


def weight_kernel(second, third, volume, weight_2, weight_3, back_2, back_3, back_volume):
    v1, v2, channels = second.shape[1], third.shape[1], volume.shape[1]
    zero_2 = jnp.zeros((v1, v1), jnp.bfloat16)
    zero_3 = jnp.zeros((v1, v2), jnp.bfloat16)
    for tap in range(9):
        taken = second[tap * v1 : (tap + 1) * v1]
        weight_2[tap * 2 * v1 : (tap * 2 + 1) * v1] = jnp.concatenate([taken, zero_2], axis=1)
        weight_2[(tap * 2 + 1) * v1 : (tap * 2 + 2) * v1] = jnp.concatenate(
            [zero_2, taken], axis=1
        )
        turned = jnp.concatenate([taken, zero_2], axis=0).astype(jnp.float32)
        at = (8 - tap) * 2 * v1
        turned = jnp.concatenate([turned, jnp.zeros_like(turned)], axis=1).T
        back_2[at : at + 2 * v1] = turned.astype(jnp.bfloat16)
        taken = third[tap * v1 : (tap + 1) * v1]
        weight_3[tap * 2 * v1 : (tap * 2 + 1) * v1] = jnp.concatenate([taken, zero_3], axis=1)
        weight_3[(tap * 2 + 1) * v1 : (tap * 2 + 2) * v1] = jnp.concatenate(
            [zero_3, taken], axis=1
        )
        turned = jnp.concatenate([taken, zero_3], axis=0).astype(jnp.float32).T
        back_3[(8 - tap) * v2 : (9 - tap) * v2] = turned.astype(jnp.bfloat16)
    for dt in range(3):
        for tap in range(9):
            at = (dt * 9 + tap) * channels
            turned = volume[at : at + channels].astype(jnp.float32).T.astype(jnp.bfloat16)
            back_volume[
                (8 - tap) * channels : (9 - tap) * channels,
                (2 - dt) * channels : (3 - dt) * channels,
            ] = turned


def forward_kernel(
    frames, parts, own, near, left, right, first, second, project, target,
    cells_out, hidden_out, slope_first, slope_second, payload,
    cells, hidden, spread_weight, picked, spaced, colour,
):
    rows, cols, slots, channels = own.shape
    groups, group = lax.axis_size("grp"), lax.axis_index("grp")
    height, width = rows * lax.axis_size("row"), cols * lax.axis_size("col")
    top, left_col = lax.axis_index("row") * rows, lax.axis_index("col") * cols
    cells[3 : 3 + rows, 3 : 3 + cols] = own[...]
    cells[0:3, 3 : 3 + cols] = near[0]
    cells[3 + rows :, 3 : 3 + cols] = near[1]
    cells[:, 0:3] = left[...]
    cells[:, 3 + cols :] = right[...]
    cells_out[...] = cells[2 : 4 + rows, 2 : 4 + cols]
    spread_weight[...] = frame_weight(first)

    def first_layer(r):
        pre = conv_frames(cells, r, cols + 4, spread_weight[...])
        row = top - 2 + r
        keep = col_mask(left_col - 2, cols + 4, width, slots, frames) & (
            (row >= 0) & (row < height)
        )
        gate = 0.5 + 0.5 * jnp.tanh(0.5 * pre)
        out = jnp.where(keep, pre * gate, 0.0).astype(jnp.bfloat16)
        hidden[r] = out.reshape(cols + 4, slots, channels)
        slope = jnp.where(keep, gate * (1.0 + pre * (1.0 - gate)), 0.0)

        @pl.when((r >= 2) & (r < 2 + rows))
        def _():
            slope_first[r - 2] = slope[2 * slots : (2 + cols) * slots]

    repeat(rows + 4, first_layer, 2)
    hidden_out[...] = hidden[1 : 3 + rows, 1 : 3 + cols]
    spread_weight[...] = frame_weight(second)
    own_slots = slots // groups
    spaced[...] = jnp.zeros(spaced.shape, jnp.float32)

    def second_layer(r):
        pre = conv_frames(hidden, r, cols + 2, spread_weight[...])
        row = top - 1 + r
        keep = col_mask(left_col - 1, cols + 2, width, slots, frames) & (
            (row >= 0) & (row < height)
        )
        gate = 0.5 + 0.5 * jnp.tanh(0.5 * pre)
        slope_second[r] = jnp.where(keep, gate * (1.0 + pre * (1.0 - gate)), 0.0)
        picked[...] = jnp.where(keep, pre * gate, 0.0)[slots : (1 + cols) * slots]
        mine = picked[pl.ds(group, cols * own_slots, stride=groups)]
        if parts > 1:
            part = lax.axis_index("row")
            spaced[pl.ds(part, cols * own_slots, stride=parts)] = mine
            mine = spaced[...]
        line = lax.dot_general(
            project[...], mine.astype(jnp.bfloat16), (((1,), (1,)), ((), ())),
            preferred_element_type=jnp.float32,
        )
        colour[jnp.clip(r - 1, -1, rows) + 1] = line

    repeat(rows + 2, second_layer, 2)
    lines = jnp.concatenate(
        [colour[1 : 1 + rows].reshape(rows * 8, colour.shape[2]).astype(jnp.bfloat16), target[...]],
        axis=0,
    )
    for k in range(payload.shape[0]):
        payload[k] = lines


def plane_slabs(wide, narrow, row, count, half):
    pieces = []
    for dr in range(3):
        pieces.append(wide[row + dr, pl.ds(0, count)])
        pieces.append(narrow[row + dr])
        pieces.append(wide[row + dr, pl.ds(2 * half, count)])
    return jnp.concatenate(pieces, axis=1)


def store_slab(wide, narrow, row, value, half):
    wide[row] = value.astype(jnp.bfloat16)
    narrow[row] = value[half : value.shape[0] - half].astype(jnp.bfloat16)


def store_wide(wide, narrow, row, value, half):
    edge = jnp.zeros((half, value.shape[1]), jnp.float32)
    store_slab(wide, narrow, row, jnp.concatenate([edge, value, edge], axis=0), half)


def fill_edges(parts, *refs):
    for ref in refs:
        last = ref.shape[0] - 1
        if parts == 1:
            for at in (0, last):
                ref[at] = jnp.zeros(ref.shape[1:], ref.dtype)
            continue
        part = lax.broadcasted_iota(jnp.int32, (ref.shape[1], 1), 0) % parts
        low = pltpu.roll(ref[last - 1].astype(jnp.float32), 1, 0)
        high = pltpu.roll(ref[1].astype(jnp.float32), ref.shape[1] - 1, 0)
        ref[0] = jnp.where(part > 0, low, 0.0).astype(ref.dtype)
        ref[last] = jnp.where(part < parts - 1, high, 0.0).astype(ref.dtype)


def kept_row(row, first, number):
    return jnp.clip(row - first, -1, number) + 1


def perceptual_kernel(
    shape, received, weight_1, weight_2, weight_3, back_3, back_2, back_1, pixels,
    target, strips, lines, wide_1, narrow_1, wide_3, narrow_3, wide_g, narrow_g,
    plane_1, plane_2, spread, wide_b, narrow_b, wide_a, narrow_a,
):
    rows, cols, blocks, block_frames, own, parts, own_slots, frames_own = shape
    f32, bf16 = jnp.float32, jnp.bfloat16
    half = parts * own_slots
    groups, group = lax.axis_size("grp"), lax.axis_index("grp")
    col_parts = lax.axis_size("col")
    width = cols * col_parts
    height = rows * lax.axis_size("row")
    view_rows, view_cols = min(height, rows + 20), min(width, cols + 20)
    top, left, view_top, view_left = corner(rows, cols)
    number = view_rows // parts
    count = view_cols * half
    lanes = lines.shape[2]
    span = width * half
    v1 = weight_2.shape[1] // 2
    v2 = weight_3.shape[1] // 2
    base = rows * 8
    body = pl.ds(3 * half, count)

    for device in range(received.shape[0]):
        target[device] = received[device, base:].astype(f32)
    strips[...] = jnp.zeros(strips.shape, f32)
    for j in range(frames_own):
        frame = groups * j + group
        block, rest = frame // block_frames, frame % block_frames
        for part in range(parts):
            for k in range(3):
                start = ((k * blocks + block) * own + rest % own) * rows

                def take(at, j=j, part=part, k=k, start=start, rest=rest):
                    row = view_top + part * number + at
                    device = (row // rows) * col_parts + rest // own
                    strips[j * parts + part, pl.ds(at * 8 + 3 + k, 1)] = target[
                        device, pl.ds(start + row % rows, 1)
                    ]

                if parts > 1:
                    device = part * col_parts + rest // own
                    strips[j * parts + part, pl.ds(3 + k, rows, stride=8)] = target[
                        device, pl.ds(pl.multiple_of(start, 8) if rows % 8 == 0 else start, rows)
                    ]
                else:
                    repeat(number, take)
    from_col = lax.broadcasted_iota(jnp.int32, (target.shape[2], lanes), 0) - view_left
    to_lane = lax.broadcasted_iota(jnp.int32, (target.shape[2], lanes), 1)
    guide = 0.0
    for j in range(frames_own):
        for part in range(parts):
            place = (from_col * half + (j * parts + part) == to_lane) & (to_lane < count)
            guide = guide + matmul(
                strips[j * parts + part].astype(bf16),
                jnp.where(place, 1.0, 0.0).astype(bf16),
            )
    lane = lax.broadcasted_iota(jnp.int32, (8, lanes), 1)
    strips_line = lines.at[pl.ds(1, number)]
    for at in range(number):
        strips_line[at, pl.ds(8, 8)] = guide[at * 8 : at * 8 + 8]

    def line_step(at):
        line = 0.0
        for part in range(parts):
            row = view_top + part * number + at
            source = pl.ds(pl.multiple_of(row % rows * 8, 8), 8)
            line = line + jnp.concatenate(
                [
                    received[(row // rows) * col_parts + k, source].astype(f32)[:, : cols * half]
                    for k in range(col_parts)
                ],
                axis=1,
            )
        line = pltpu.roll(line, lax.rem(span - view_left * half, span), 1)[:, :lanes]
        line = jnp.where(lane < count, line, 0.0) + lines[at + 1, pl.ds(8, 8)]
        before = jnp.where(lane < half, 0.0, pltpu.roll(line, half, 1))
        after = jnp.where(lane >= count - half, 0.0, pltpu.roll(line, lanes - half, 1))
        lines[at + 1] = jnp.concatenate([before, line, after], axis=0)

    repeat(number, line_step, 2)
    wide_lane = lax.broadcasted_iota(jnp.int32, (24, lanes), 1)
    if parts > 1:
        part = wide_lane % parts
        inside = wide_lane < count
        low = pltpu.roll(lines[number], 1, 1)
        high = pltpu.roll(lines[1], lanes - 1, 1)
        lines[0] = jnp.where((part > 0) & inside, low, 0.0)
        lines[number + 1] = jnp.where((part < parts - 1) & inside, high, 0.0)
    else:
        lines[0] = jnp.zeros((24, lanes), f32)
        lines[number + 1] = jnp.zeros((24, lanes), f32)

    def first_step(at):
        pieces = [lines[at], lines[at + 1], lines[at + 2], jnp.zeros((56, lanes), f32)]
        patches = jnp.concatenate(pieces, axis=0).T[:count].astype(bf16)
        z = matmul(patches, weight_1[...])
        plane_1[at, body] = z
        store_wide(wide_1, narrow_1, at + 1, 0.5 * z * (1.0 + gelu_tanh(z)), half)

    repeat(number, first_step, 4)
    fill_edges(parts, wide_1, narrow_1)

    def second_step(q):
        total = 0.0
        for step in range(2):
            at = 2 * q + step
            z = matmul(plane_slabs(wide_1, narrow_1, at, count, half), weight_2[...])
            plane_2[at, body] = z
            total = total + 0.5 * z * (1.0 + gelu_tanh(z))
        pooled = total.reshape(view_cols // 2, 2, half, 2 * v1)
        pooled = 0.25 * (pooled[:, 0] + pooled[:, 1])
        store_wide(wide_3, narrow_3, q + 1, pooled.reshape(count // 2, 2 * v1), half)

    repeat(number // 2, second_step, 2)
    fill_edges(parts, wide_3, narrow_3)

    def third_step(q):
        z = matmul(plane_slabs(wide_3, narrow_3, q, count // 2, half), weight_3[...])
        t = gelu_tanh(z)
        value = 0.5 * z * (1.0 + t)
        delta = (64.0 / v2) * (value[:, :v2] - value[:, v2:]) * gelu_slope(z[:, :v2], t[:, :v2])
        store_wide(wide_g, narrow_g, q + 1, delta, half)

    repeat(number // 2, third_step, 2)
    fill_edges(parts, wide_g, narrow_g)

    def pool_step(q):
        grad = 0.25 * matmul(plane_slabs(wide_g, narrow_g, q, count // 2, half), back_3[...])
        grad = grad.reshape(view_cols // 2, 1, half, 2 * v1)
        spread[q, body] = jnp.concatenate([grad, grad], axis=1).reshape(count, 2 * v1)

    repeat(number // 2, pool_step, 2)

    def near(reach):
        size = (cols + 2 * reach) * half
        keep = col_mask(left - reach, cols + 2 * reach, width, half, half)
        start = pl.multiple_of((left - view_left + 3 - reach) * half, 8)
        return keep, pl.ds(start, size), size

    def second_delta(at):
        keep, where, _ = near(3)
        z = plane_2[at, where]
        t = gelu_tanh(z)
        value = 0.5 * z * (1.0 + t)
        delta = spread[at // 2, where] + (16.0 / v1) * (value - pltpu.roll(value, v1, 1))
        store_slab(wide_b, narrow_b, at + 1, jnp.where(keep, delta * gelu_slope(z, t), 0.0), half)

    repeat(number, second_delta, 2)
    fill_edges(parts, wide_b, narrow_b)

    def first_delta(at):
        keep, where, size = near(2)
        grad = matmul(plane_slabs(wide_b, narrow_b, at, size, half), back_2[...])
        z = plane_1[at, where]
        delta = jnp.where(keep, grad * gelu_slope(z, gelu_tanh(z)), 0.0)
        store_slab(wide_a, narrow_a, at + 1, delta, half)

    repeat(number, first_delta, 2)
    fill_edges(parts, wide_a, narrow_a)

    def pixel_step(at):
        size = (cols + 2) * half
        grad = lax.dot_general(
            back_1[...], plane_slabs(wide_a, narrow_a, at, size, half), (((1,), (1,)), ((), ())),
            preferred_element_type=f32,
        )
        line = lines[at + 1, pl.ds(8, 8)]
        line = line - pltpu.roll(line, 5, 0)
        shift = lax.rem((view_left - left + 1) * half + 2 * lanes, lanes)
        line = pltpu.roll(line, shift, 1)
        pixels[at] = (grad + (1.0 / 6.0) * line[:, :size]).astype(bf16)

    repeat(number, pixel_step, 2)


def gradient_taps(source, delta, shifted, sums, first_tap):
    rows = delta.shape[0]
    slots, channels = source.shape[-2:]
    cols = source.shape[1] - 2
    count = cols * slots

    def turn(r):
        block = delta[r].astype(jnp.float32)
        for dt in range(3):
            moved = block if dt == 1 else pltpu.roll(block, (dt - 1) % count, 0)
            shifted[dt, r] = moved.T.astype(jnp.bfloat16)

    repeat(rows, turn, 2)

    def tap_step(step):
        tap = jnp.minimum(first_tap + step, 26)
        dt, dr, dc = tap // 9, tap // 3 % 3, tap % 3
        total = 0.0
        for r in range(rows):
            slab = source[r + dr, pl.ds(dc, cols)].reshape(count, channels)
            total = total + matmul(shifted[dt, r], slab)
        sums[pl.ds(pl.multiple_of(step * channels, channels), channels)] = total.T

    repeat(sums.shape[0] // channels, tap_step, 4)


def backward_kernel(*refs, parts, out_rows, groups):
    pixels = refs[:groups]
    (
        slope_first, slope_second, cells, hidden, paint, back_second, terms,
        painted, hidden_grad, delta_second, delta_own, shifted, sums,
    ) = refs[groups:]
    slots, channels = cells.shape[-2:]
    rows, cols = cells.shape[0] - 2, cells.shape[1] - 2
    height = rows * lax.axis_size("row")
    view_rows = min(height, rows + 20)
    number = view_rows // parts
    own_slots = slots // groups
    group = lax.axis_index("grp")
    top, _, view_top, _ = corner(rows, cols)
    kept = (cols + 2) * own_slots

    def paint_step(at):
        for step in range(groups):
            source = lax.rem(group - step + groups, groups)
            slot = painted.at[step]
            slot[...] = lax.dot_general(
                pixels[step][at], paint[...], (((0,), (0,)), ((), ())),
                preferred_element_type=jnp.float32,
            )
            for part in range(parts):
                row = kept_row(view_top + part * number + at, top - 1, rows + 2)
                value = slot[pl.ds(part, kept, stride=parts)] if parts > 1 else slot[...]
                hidden_grad[row, pl.ds(source, kept, stride=groups)] = value

    repeat(number, paint_step, 2)

    def delta_step(a):
        row = top - 1 + a
        inside = (row >= 0) & (row < height)
        delta = jnp.where(inside, hidden_grad[a + 1] * slope_second[a], 0.0).astype(jnp.bfloat16)
        delta_second[a] = delta.reshape(cols + 2, slots, channels)

    repeat(rows + 2, delta_step, 2)

    first_row = lax.axis_index("grp") * out_rows
    first_tap = first_row // channels
    skip = pl.multiple_of(first_row - first_tap * channels, 32)
    device = lax.axis_index("row") * lax.axis_size("col") + lax.axis_index("col")

    def put(which):
        value = sums[pl.ds(skip, out_rows)]
        if len(terms.shape) == 3:
            terms[which] = value.astype(jnp.bfloat16)
        else:
            chunks, _, size, _ = terms.shape
            for k in range(chunks):
                piece = value[k * size : (k + 1) * size].astype(jnp.bfloat16)
                terms[lax.rem(k - device + chunks, chunks), which] = piece

    def own_step(r):
        delta_own[r] = delta_second[r + 1, 1 : 1 + cols].reshape(cols * slots, channels)

    repeat(rows, own_step, 2)
    gradient_taps(hidden, delta_own, shifted, sums, first_tap)
    put(1)

    def back_step(r):
        back = conv_frames(delta_second, r, cols, back_second[...])
        delta_own[r] = (back * slope_first[r]).astype(jnp.bfloat16)

    repeat(rows, back_step, 4)
    gradient_taps(cells, delta_own, shifted, sums, first_tap)
    put(0)


def call(kernel, outs, scratch, flops=0):
    return pl.pallas_call(
        kernel,
        out_shape=outs,
        scratch_shapes=[pltpu.VMEM(*shape) for shape in scratch],
        compiler_params=pltpu.CompilerParams(vmem_limit_bytes=vmem_bytes),
        cost_estimate=pl.CostEstimate(flops=flops, bytes_accessed=2**20, transcendentals=0),
    )


def plane_first_weights(vgg_first):
    taps = vgg_first.reshape(9, 3, -1)
    v1 = taps.shape[2]
    first = jnp.concatenate(
        [jnp.pad(taps, ((0, 0), (0, 0), (0, v1))), jnp.pad(taps, ((0, 0), (0, 0), (v1, 0)))], axis=1
    )
    first = jnp.pad(first, ((0, 0), (0, 2), (0, 0))).reshape(72, 2 * v1)
    back = jnp.transpose(taps[::-1], (1, 0, 2))
    back = jnp.pad(back, ((0, 5), (0, 0), (0, v1))).reshape(8, 9 * 2 * v1)
    return jnp.pad(first, ((0, 56), (0, 0))), back


def row_halo(own, width):
    count, length = lax.axis_size("row"), own.shape[0]
    if count == 2:
        second = lax.axis_index("row")
        edge = lax.dynamic_slice_in_dim(own, (1 - second) * (length - width), width, axis=0)
        came = lax.ppermute(edge, "row", [(0, 1), (1, 0)])
        place = (jnp.arange(2) == 1 - second).reshape(2, 1, 1, 1, 1)
        return jnp.where(place, came[None], jnp.zeros_like(came)[None])
    before = lax.ppermute(own[length - width :], "row", [(i, i + 1) for i in range(count - 1)])
    after = lax.ppermute(own[:width], "row", [(i + 1, i) for i in range(count - 1)])
    return jnp.stack([before, after])


def col_halo(tall, width):
    count, length = lax.axis_size("col"), tall.shape[1]
    before = lax.ppermute(
        tall[:, length - width :], "col", [(i, i + 1) for i in range(count - 1)]
    )
    after = lax.ppermute(tall[:, :width], "col", [(i + 1, i) for i in range(count - 1)])
    return before, after


def local(dec_input, target, conv_first, conv_second, rgb_weight, vgg_first, vgg_second, vgg_third):
    f32, bf16 = jnp.float32, jnp.bfloat16
    row_count, col_count = lax.axis_size("row"), lax.axis_size("col")
    groups, devices = lax.axis_size("grp"), row_count * col_count
    blocks, block_frames, rows, cols, channels = dec_input.shape
    frames = blocks * block_frames
    frames_own = frames // groups
    parts, own_slots = split(rows, frames_own)
    slots = own_slots * groups
    half = parts * own_slots
    height, width = rows * row_count, cols * col_count
    view_rows, view_cols = min(height, rows + 20), min(width, cols + 20)
    number, count = view_rows // parts, view_cols * half
    lanes = -(-count // 128) * 128
    v1, v2 = vgg_first.shape[1], vgg_third.shape[1]

    own = jnp.transpose(dec_input.reshape(frames, rows, cols, channels), (1, 2, 0, 3))
    own = jnp.pad(own, ((0, 0), (0, 0), (0, slots - frames), (0, 0)))
    near = row_halo(own, 3)
    tall = jnp.concatenate([near[0], own, near[1]], axis=0)
    before, after = col_halo(tall, 3)

    line = max(cols * half, -(-width // 128) * 128)
    own_target = target.reshape(-1, width)
    target_rows = own_target.shape[0]
    own_target = jnp.pad(own_target, ((0, 0), (0, line - width)))
    project = jnp.pad(rgb_weight, ((0, 5), (0, 0)))
    weight_1, back_1 = plane_first_weights(vgg_first)
    weight_2, weight_3, back_2, back_3, back_volume = call(
        weight_kernel,
        (
            jax.ShapeDtypeStruct((18 * v1, 2 * v1), bf16),
            jax.ShapeDtypeStruct((18 * v1, 2 * v2), bf16),
            jax.ShapeDtypeStruct((18 * v1, 2 * v1), bf16),
            jax.ShapeDtypeStruct((9 * v2, 2 * v1), bf16),
            jax.ShapeDtypeStruct((9 * channels, 3 * channels), bf16),
        ),
        [],
        2**30,
    )(vgg_second, vgg_third, conv_second)

    cells, hidden, slope_first, slope_second, payload = call(
        functools.partial(forward_kernel, frames, parts),
        (
            jax.ShapeDtypeStruct((rows + 2, cols + 2, slots, channels), bf16),
            jax.ShapeDtypeStruct((rows + 2, cols + 2, slots, channels), bf16),
            jax.ShapeDtypeStruct((rows, cols * slots, channels), f32),
            jax.ShapeDtypeStruct((rows + 2, (cols + 2) * slots, channels), f32),
            jax.ShapeDtypeStruct((devices, rows * 8 + target_rows, line), bf16),
        ),
        [
            ((rows + 6, cols + 6, slots, channels), bf16),
            ((rows + 4, cols + 4, slots, channels), bf16),
            ((9 * channels, 3 * channels), bf16),
            ((cols * slots, channels), f32),
            ((cols * half, channels), f32),
            ((rows + 2, 8, cols * half), f32),
        ],
        2**33,
    )(own, near, before, after, conv_first, conv_second, project, own_target)

    received = lax.all_to_all(payload, plane, split_axis=0, concat_axis=0, tiled=True)

    wide_count = count + 6 * half
    pixels = call(
        functools.partial(
            perceptual_kernel,
            (
                rows, cols, blocks, block_frames, target.shape[2], parts, own_slots, frames_own,
            ),
        ),
        jax.ShapeDtypeStruct((number, 8, (cols + 2) * half), bf16),
        [
            ((devices, target_rows, line), f32),
            ((frames_own * parts, number * 8, line), f32),
            ((number + 2, 24, lanes), f32),
            ((number + 2, count + 2 * half, 2 * v1), bf16),
            ((number + 2, count, 2 * v1), bf16),
            ((number // 2 + 2, count // 2 + 2 * half, 2 * v1), bf16),
            ((number // 2 + 2, count // 2, 2 * v1), bf16),
            ((number // 2 + 2, count // 2 + 2 * half, v2), bf16),
            ((number // 2 + 2, count // 2, v2), bf16),
            ((number, wide_count, 2 * v1), f32),
            ((number, wide_count, 2 * v1), f32),
            ((number // 2, wide_count, 2 * v1), f32),
            ((number + 2, (cols + 6) * half, 2 * v1), bf16),
            ((number + 2, (cols + 4) * half, 2 * v1), bf16),
            ((number + 2, (cols + 4) * half, 2 * v1), bf16),
            ((number + 2, (cols + 2) * half, 2 * v1), bf16),
        ],
        2**32,
    )(received, weight_1, weight_2, weight_3, back_3, back_2, back_1)

    gathered = [pixels]
    for step in range(1, groups):
        ring = [(i, (i + step) % groups) for i in range(groups)]
        gathered.append(lax.ppermute(pixels, "grp", ring))

    out_rows = conv_first.shape[0] // groups
    taps = max(
        -(-(g + 1) * out_rows // channels) - g * out_rows // channels for g in range(groups)
    )
    even = out_rows % devices == 0
    out_shape = (
        (devices, 2, out_rows // devices, channels) if even else (2, out_rows, channels)
    )
    terms = call(
        functools.partial(backward_kernel, parts=parts, out_rows=out_rows, groups=groups),
        jax.ShapeDtypeStruct(out_shape, bf16),
        [
            ((groups, (cols + 2) * half, channels), f32),
            ((rows + 4, (cols + 2) * slots, channels), f32),
            ((rows + 2, cols + 2, slots, channels), bf16),
            ((rows, cols * slots, channels), bf16),
            ((3, rows, channels, cols * slots), bf16),
            ((taps * channels, channels), f32),
        ],
        2**32,
    )(*gathered, slope_first, slope_second, cells, hidden, project, back_volume)

    if even:
        pieces = [terms[0]]
        for step in range(1, devices):
            ring = [(i, (i + step) % devices) for i in range(devices)]
            pieces.append(lax.ppermute(terms[step], plane, ring))
        total = sum(piece.astype(f32) for piece in pieces)
    else:
        pieces = jnp.swapaxes(terms.reshape(2, devices, -1), 0, 1)
        pieces = lax.all_to_all(pieces, plane, split_axis=0, concat_axis=0, tiled=True)
        total = jnp.sum(pieces.astype(f32), axis=0)
    return total[0].reshape(-1), total[1].reshape(-1)


def solution(mesh):
    in_specs = (
        P(None, None, "row", "col", None),
        P(None, None, "col", "row", None),
        P(),
        P(),
        P(),
        P(),
        P(),
        P(),
    )
    out_specs = (P(("grp", "row", "col")), P(("grp", "row", "col")))
    return jax.shard_map(local, mesh=mesh, in_specs=in_specs, out_specs=out_specs, check_vma=False)
```

```python
import functools

import jax
import jax.numpy as jnp
from jax import lax
from jax.experimental import pallas as pl
from jax.experimental.pallas import tpu as pltpu
from jax.sharding import PartitionSpec as P

gelu_scale = 0.7978845608028654
gelu_cubic = 0.044715
plane = ("row", "col")


def repeat(count, body, unroll=1):
    lax.fori_loop(0, count, lambda i, carry: (body(i), carry)[1], 0, unroll=unroll)


def matmul(left, right):
    return jnp.dot(left, right, preferred_element_type=jnp.float32)


def gelu_tanh(z):
    return jnp.tanh(gelu_scale * (z + gelu_cubic * z * z * z))


def gelu_slope(z, t):
    return 0.5 * (1.0 + t) + 0.5 * z * (1.0 - t * t) * gelu_scale * (
        1.0 + 3.0 * gelu_cubic * z * z
    )


def split(rows, frames_own):
    small = frames_own <= 4 and lax.axis_size("row") == 2 and rows % 4 == 0
    return (2, 4) if small else (1, 8)


def corner(rows, cols):
    height, width = rows * lax.axis_size("row"), cols * lax.axis_size("col")
    view_rows, view_cols = min(height, rows + 20), min(width, cols + 20)
    top, left = lax.axis_index("row") * rows, lax.axis_index("col") * cols
    view_top = jnp.clip(top - 10, 0, height - view_rows)
    view_left = jnp.clip(left - 10, 0, width - view_cols)
    return top, left, view_top, view_left


def col_mask(first_col, cols, width, slots, frames):
    at = lax.broadcasted_iota(jnp.int32, (cols * slots, 1), 0)
    col = at // slots + first_col
    return (at % slots < frames) & (col >= 0) & (col < width)


def frame_weight(ref):
    third = ref.shape[0] // 3
    return jnp.concatenate([ref[pl.ds(third * k, third)] for k in range(3)], axis=1)


def conv_pairs(source, rows, cols, weight, use):
    slots, channels = source.shape[-2:]
    count = cols * slots

    def step(q):
        slabs = [
            source[pl.ds(2 * q + dr, 2), pl.ds(dc, cols)].reshape(2 * count, channels)
            for dr in range(3)
            for dc in range(3)
        ]
        sums = matmul(jnp.concatenate(slabs, axis=1), weight[...])
        total = (
            pltpu.roll(sums[:, :channels], 1, 0)
            + sums[:, channels : 2 * channels]
            + pltpu.roll(sums[:, 2 * channels :], 2 * count - 1, 0)
        )
        for k in range(2):
            use(2 * q + k, total[k * count : (k + 1) * count])

    repeat(rows // 2, step, rows // 2)


def forward_kernel(
    frames, parts, pack, own, near, left, right, first, second, rgb, target,
    cells_out, hidden_out, first_out, second_out, payload,
    cells, hidden, slope_first, slope_second, spread_weight, picked, spaced, colour, project, sems,
):
    rows, cols, slots, channels = own.shape
    f32, bf16 = jnp.float32, jnp.bfloat16
    groups, group = lax.axis_size("grp"), lax.axis_index("grp")
    height, width = rows * lax.axis_size("row"), cols * lax.axis_size("col")
    top, left_col = lax.axis_index("row") * rows, lax.axis_index("col") * cols
    cells[3 : 3 + rows, 3 : 3 + cols] = own[...]
    cells[0:3, 3 : 3 + cols] = near[0]
    cells[3 + rows :, 3 : 3 + cols] = near[1]
    cells[:, 0:3] = left[...]
    cells[:, 3 + cols :] = right[...]
    copies = [
        pltpu.make_async_copy(
            cells.at[pl.ds(2, rows + 2), pl.ds(2, cols + 2)], cells_out, sems.at[0]
        ),
        pltpu.make_async_copy(
            hidden.at[pl.ds(1, rows + 2), pl.ds(1, cols + 2)], hidden_out, sems.at[1]
        ),
        pltpu.make_async_copy(slope_first, first_out, sems.at[2]),
        pltpu.make_async_copy(slope_second, second_out, sems.at[3]),
    ]
    copies[0].start()
    spread_weight[...] = frame_weight(first)

    def first_layer(r, pre):
        row = top - 2 + r
        keep = col_mask(left_col - 2, cols + 4, width, slots, frames) & (
            (row >= 0) & (row < height)
        )
        gate = 0.5 + 0.5 * jnp.tanh(0.5 * pre)
        out = jnp.where(keep, pre * gate, 0.0).astype(bf16)
        hidden[r] = out.reshape(cols + 4, slots, channels)
        slope = jnp.where(keep, gate * (1.0 + pre * (1.0 - gate)), 0.0)

        @pl.when((r >= 2) & (r < 2 + rows))
        def _():
            slope_first[r - 2] = slope[2 * slots : (2 + cols) * slots]

    conv_pairs(cells, rows + 4, cols + 4, spread_weight, first_layer)
    copies[1].start()
    copies[2].start()
    spread_weight[...] = frame_weight(second)
    own_slots = slots // groups
    spaced[...] = jnp.zeros(spaced.shape, f32)
    project[...] = jnp.zeros(project.shape, f32)
    project[0:3] = rgb[...].astype(f32)

    def second_layer(r, pre):
        row = top - 1 + r
        keep = col_mask(left_col - 1, cols + 2, width, slots, frames) & (
            (row >= 0) & (row < height)
        )
        gate = 0.5 + 0.5 * jnp.tanh(0.5 * pre)
        slope_second[r] = jnp.where(keep, gate * (1.0 + pre * (1.0 - gate)), 0.0)
        picked[r] = jnp.where(keep, pre * gate, 0.0)[slots : (1 + cols) * slots]
        mine = picked.at[r][pl.ds(group, cols * own_slots, stride=groups)]
        if parts > 1:
            part = lax.axis_index("row")
            spaced.at[r][pl.ds(part, cols * own_slots, stride=parts)] = mine
            mine = spaced[r]
        line = lax.dot_general(
            project[...].astype(bf16), mine.astype(bf16), (((1,), (1,)), ((), ())),
            preferred_element_type=f32,
        )
        at = jnp.clip(r - 1, -1, rows) + 1
        colour[pl.ds(pl.multiple_of(at * 8, 8), 8)] = line

    conv_pairs(hidden, rows + 2, cols + 2, spread_weight, second_layer)
    copies[3].start()
    size, line = payload.shape[1:]
    pieces = [colour[pl.ds(8 + k, rows, stride=8)] for k in range(3)]
    goal = target[...].reshape(-1, rows, width).astype(f32)
    if pack > 1:
        short = rows // pack
        goal = jnp.concatenate([goal[:, k * short : (k + 1) * short] for k in range(pack)], axis=2)
    goal = goal.reshape(-1, pack * width)
    if pack * width < line:
        goal = jnp.concatenate(
            [goal, jnp.zeros((goal.shape[0], line - pack * width), f32)], axis=1
        )
    pieces.append(goal)
    filled = 3 * rows + goal.shape[0]
    if filled < size:
        pieces.append(jnp.zeros((size - filled, line), f32))
    lines = jnp.concatenate(pieces, axis=0).astype(bf16)
    for k in range(payload.shape[0]):
        payload[k] = lines
    for copy in copies:
        copy.wait()


def plane_slabs(wide, narrow, row, count, half):
    pieces = []
    for dr in range(3):
        pieces.append(wide[row + dr, pl.ds(0, count)])
        pieces.append(narrow[row + dr])
        pieces.append(wide[row + dr, pl.ds(2 * half, count)])
    return jnp.concatenate(pieces, axis=1)


def store_slab(wide, narrow, row, value, half):
    wide[row] = value.astype(jnp.bfloat16)
    narrow[row] = value[half : value.shape[0] - half].astype(jnp.bfloat16)


def store_wide(wide, narrow, row, value, half):
    edge = jnp.zeros((half, value.shape[1]), jnp.float32)
    store_slab(wide, narrow, row, jnp.concatenate([edge, value, edge], axis=0), half)


def fill_edges(parts, *refs):
    for ref in refs:
        last = ref.shape[0] - 1
        if parts == 1:
            for at in (0, last):
                ref[at] = jnp.zeros(ref.shape[1:], ref.dtype)
            continue
        part = lax.broadcasted_iota(jnp.int32, (ref.shape[1], 1), 0) % parts
        low = pltpu.roll(ref[last - 1].astype(jnp.float32), 1, 0)
        high = pltpu.roll(ref[1].astype(jnp.float32), ref.shape[1] - 1, 0)
        ref[0] = jnp.where(part > 0, low, 0.0).astype(ref.dtype)
        ref[last] = jnp.where(part < parts - 1, high, 0.0).astype(ref.dtype)


def kept_row(row, first, number):
    return jnp.clip(row - first, -1, number) + 1


def unrolled(number):
    return number if number <= 8 else 4 if number % 4 == 0 else 2


def plane_weights(
    first, second, third, weight_1, weight_2, weight_3, back_3, back_2, back_1
):
    f32, bf16 = jnp.float32, jnp.bfloat16
    v1, v2 = second.shape[1], third.shape[1]
    zero_2 = jnp.zeros((v1, v1), bf16)
    zero_3 = jnp.zeros((v1, v2), bf16)
    weight_1[...] = jnp.zeros(weight_1.shape, f32)
    back_1[...] = jnp.zeros(back_1.shape, f32)
    for tap in range(9):
        taken = first[...].astype(f32)[tap * 3 : tap * 3 + 3]
        weight_1[tap * 8 : tap * 8 + 3, 0:v1] = taken
        weight_1[tap * 8 + 3 : tap * 8 + 6, v1 : 2 * v1] = taken
        back_1[0:3, (8 - tap) * 2 * v1 : (8 - tap) * 2 * v1 + v1] = taken
        taken = second[tap * v1 : (tap + 1) * v1]
        weight_2[tap * 2 * v1 : (tap * 2 + 1) * v1] = jnp.concatenate([taken, zero_2], axis=1)
        weight_2[(tap * 2 + 1) * v1 : (tap * 2 + 2) * v1] = jnp.concatenate(
            [zero_2, taken], axis=1
        )
        turned = jnp.concatenate([taken, zero_2], axis=0).astype(f32)
        turned = jnp.concatenate([turned, jnp.zeros_like(turned)], axis=1).T
        back_2[(8 - tap) * 2 * v1 : (9 - tap) * 2 * v1] = turned.astype(bf16)
        taken = third[tap * v1 : (tap + 1) * v1]
        weight_3[tap * 2 * v1 : (tap * 2 + 1) * v1] = jnp.concatenate([taken, zero_3], axis=1)
        weight_3[(tap * 2 + 1) * v1 : (tap * 2 + 2) * v1] = jnp.concatenate(
            [zero_3, taken], axis=1
        )
        turned = jnp.concatenate([taken, zero_3], axis=0).astype(f32).T
        back_3[(8 - tap) * v2 : (9 - tap) * v2] = turned.astype(bf16)


def perceptual_kernel(
    shape, received, vgg_first, vgg_second, vgg_third, pixels,
    weight_1, weight_2, weight_3, back_3, back_2, back_1, shown, grads,
    target, strips, lines, wide_1, narrow_1, wide_3, narrow_3, wide_g, narrow_g,
    plane_1, plane_2, spread, wide_b, narrow_b, wide_a, narrow_a,
):
    rows, cols, blocks, block_frames, own, parts, own_slots, frames_own, pack = shape
    f32, bf16 = jnp.float32, jnp.bfloat16
    half = parts * own_slots
    groups, group = lax.axis_size("grp"), lax.axis_index("grp")
    col_parts = lax.axis_size("col")
    width = cols * col_parts
    height = rows * lax.axis_size("row")
    view_rows, view_cols = min(height, rows + 20), min(width, cols + 20)
    top, left, view_top, view_left = corner(rows, cols)
    number = view_rows // parts
    count = view_cols * half
    lanes = lines.shape[2]
    span = width * half
    v1 = weight_2.shape[1] // 2
    v2 = weight_3.shape[1] // 2
    body = pl.ds(3 * half, count)
    plane_weights(
        vgg_first, vgg_second, vgg_third, weight_1, weight_2, weight_3, back_3, back_2, back_1
    )

    for device in range(received.shape[0]):
        arrived = received[device].astype(f32)
        target[device] = arrived[3 * rows :]
        shown[device] = jnp.zeros(shown.shape[1:], f32)
        for k in range(3):
            shown.at[device][pl.ds(k, rows, stride=8)] = arrived[k * rows : (k + 1) * rows]
    strips[...] = jnp.zeros(strips.shape, f32)
    for j in range(frames_own):
        frame = groups * j + group
        block, rest = frame // block_frames, frame % block_frames
        for part in range(parts):
            for k in range(3):
                short = rows // pack
                start = ((k * blocks + block) * own + rest % own) * short

                def take(at, j=j, part=part, k=k, start=start, rest=rest):
                    row = view_top + part * number + at
                    device = (row // rows) * col_parts + rest // own
                    strips[j * parts + part, pl.ds(at * 8 + 3 + k, 1)] = target[
                        device, pl.ds(start + row % rows, 1)
                    ]

                if parts > 1:
                    device = part * col_parts + rest // own
                    value = target[device, pl.ds(start, short)]
                    for turn in range(pack):
                        strips[j * parts + part, pl.ds(3 + k + turn * short * 8, short, stride=8)] = (
                            pltpu.roll(value, (pack - turn) * width % value.shape[1], 1)
                        )
                else:
                    repeat(number, take)
    from_col = lax.broadcasted_iota(jnp.int32, (target.shape[2], lanes), 0) - view_left
    to_lane = lax.broadcasted_iota(jnp.int32, (target.shape[2], lanes), 1)
    guide = 0.0
    for j in range(frames_own):
        for part in range(parts):
            place = (from_col * half + (j * parts + part) == to_lane) & (to_lane < count)
            guide = guide + matmul(
                strips[j * parts + part].astype(bf16),
                jnp.where(place, 1.0, 0.0).astype(bf16),
            )
    lane = lax.broadcasted_iota(jnp.int32, (8, lanes), 1)
    strips_line = lines.at[pl.ds(1, number)]
    for at in range(number):
        strips_line[at, pl.ds(8, 8)] = guide[at * 8 : at * 8 + 8]

    def line_step(at):
        line = 0.0
        for part in range(parts):
            row = view_top + part * number + at
            source = pl.ds(pl.multiple_of(row % rows * 8, 8), 8)
            line = line + jnp.concatenate(
                [
                    shown[(row // rows) * col_parts + k, source][:, : cols * half]
                    for k in range(col_parts)
                ],
                axis=1,
            )
        line = pltpu.roll(line, lax.rem(span - view_left * half, span), 1)[:, :lanes]
        line = jnp.where(lane < count, line, 0.0) + lines[at + 1, pl.ds(8, 8)]
        before = jnp.where(lane < half, 0.0, pltpu.roll(line, half, 1))
        after = jnp.where(lane >= count - half, 0.0, pltpu.roll(line, lanes - half, 1))
        lines[at + 1] = jnp.concatenate([before, line, after], axis=0)

    repeat(number, line_step, unrolled(number))
    wide_lane = lax.broadcasted_iota(jnp.int32, (24, lanes), 1)
    if parts > 1:
        part = wide_lane % parts
        inside = wide_lane < count
        low = pltpu.roll(lines[number], 1, 1)
        high = pltpu.roll(lines[1], lanes - 1, 1)
        lines[0] = jnp.where((part > 0) & inside, low, 0.0)
        lines[number + 1] = jnp.where((part < parts - 1) & inside, high, 0.0)
    else:
        lines[0] = jnp.zeros((24, lanes), f32)
        lines[number + 1] = jnp.zeros((24, lanes), f32)

    def first_step(at):
        pieces = [lines[at], lines[at + 1], lines[at + 2], jnp.zeros((56, lanes), f32)]
        patches = jnp.concatenate(pieces, axis=0).T[:count].astype(bf16)
        z = matmul(patches, weight_1[...].astype(bf16))
        plane_1[at, body] = z
        store_wide(wide_1, narrow_1, at + 1, 0.5 * z * (1.0 + gelu_tanh(z)), half)

    repeat(number, first_step, unrolled(number))
    fill_edges(parts, wide_1, narrow_1)

    def second_step(q):
        total = 0.0
        for step in range(2):
            at = 2 * q + step
            z = matmul(plane_slabs(wide_1, narrow_1, at, count, half), weight_2[...])
            plane_2[at, body] = z
            total = total + 0.5 * z * (1.0 + gelu_tanh(z))
        pooled = total.reshape(view_cols // 2, 2, half, 2 * v1)
        pooled = 0.25 * (pooled[:, 0] + pooled[:, 1])
        store_wide(wide_3, narrow_3, q + 1, pooled.reshape(count // 2, 2 * v1), half)

    repeat(number // 2, second_step, unrolled(number // 2))
    fill_edges(parts, wide_3, narrow_3)

    def third_step(q):
        z = matmul(plane_slabs(wide_3, narrow_3, q, count // 2, half), weight_3[...])
        t = gelu_tanh(z)
        value = 0.5 * z * (1.0 + t)
        delta = (64.0 / v2) * (value[:, :v2] - value[:, v2:]) * gelu_slope(z[:, :v2], t[:, :v2])
        store_wide(wide_g, narrow_g, q + 1, delta, half)

    repeat(number // 2, third_step, unrolled(number // 2))
    fill_edges(parts, wide_g, narrow_g)

    def pool_step(q):
        grad = 0.25 * matmul(plane_slabs(wide_g, narrow_g, q, count // 2, half), back_3[...])
        grad = grad.reshape(view_cols // 2, 1, half, 2 * v1)
        spread[q, body] = jnp.concatenate([grad, grad], axis=1).reshape(count, 2 * v1)

    repeat(number // 2, pool_step, unrolled(number // 2))

    def near(reach):
        size = (cols + 2 * reach) * half
        keep = col_mask(left - reach, cols + 2 * reach, width, half, half)
        start = pl.multiple_of((left - view_left + 3 - reach) * half, 8)
        return keep, pl.ds(start, size), size

    def second_delta(at):
        keep, where, _ = near(3)
        z = plane_2[at, where]
        t = gelu_tanh(z)
        value = 0.5 * z * (1.0 + t)
        delta = spread[at // 2, where] + (16.0 / v1) * (value - pltpu.roll(value, v1, 1))
        store_slab(wide_b, narrow_b, at + 1, jnp.where(keep, delta * gelu_slope(z, t), 0.0), half)

    repeat(number, second_delta, unrolled(number))
    fill_edges(parts, wide_b, narrow_b)

    def first_delta(at):
        keep, where, size = near(2)
        grad = matmul(plane_slabs(wide_b, narrow_b, at, size, half), back_2[...])
        z = plane_1[at, where]
        delta = jnp.where(keep, grad * gelu_slope(z, gelu_tanh(z)), 0.0)
        store_slab(wide_a, narrow_a, at + 1, delta, half)

    repeat(number, first_delta, unrolled(number))
    fill_edges(parts, wide_a, narrow_a)

    def pixel_step(at):
        size = (cols + 2) * half
        grad = lax.dot_general(
            back_1[...].astype(bf16), plane_slabs(wide_a, narrow_a, at, size, half), (((1,), (1,)), ((), ())),
            preferred_element_type=f32,
        )
        line = lines[at + 1, pl.ds(8, 8)]
        line = line - pltpu.roll(line, 5, 0)
        shift = lax.rem((view_left - left + 1) * half + 2 * lanes, lanes)
        line = pltpu.roll(line, shift, 1)
        grad = grad + (1.0 / 6.0) * line[:, :size]
        for k in range(3):
            grads[pl.ds(k * number + at, 1)] = grad[k : k + 1]

    repeat(number, pixel_step, unrolled(number))
    for k in range(3):
        pixels[k] = grads[k * number : (k + 1) * number].astype(bf16)


def gradient_taps(source, delta, shifted, sums, first_tap):
    rows = delta.shape[0]
    slots, channels = source.shape[-2:]
    cols = source.shape[1] - 2
    count = cols * slots

    def turn(r):
        block = delta[r].astype(jnp.float32)
        for dt in range(3):
            moved = block if dt == 1 else pltpu.roll(block, (dt - 1) % count, 0)
            shifted[dt, r] = moved.T.astype(jnp.bfloat16)

    repeat(rows, turn, rows)

    def tap_step(step):
        tap = jnp.minimum(first_tap + step, 26)
        dt, dr, dc = tap // 9, tap // 3 % 3, tap % 3
        total = 0.0
        for r in range(rows):
            slab = source[r + dr, pl.ds(dc, cols)].reshape(count, channels)
            total = total + matmul(shifted[dt, r], slab)
        sums[pl.ds(pl.multiple_of(step * channels, channels), channels)] = total.T

    repeat(sums.shape[0] // channels, tap_step, 8)


def backward_kernel(*refs, parts, out_rows, groups):
    pixels = refs[:groups]
    (
        rgb, conv_second, first_in, second_in, cells_in, hidden_in, terms,
        slope_first, slope_second, cells, hidden, weight, back_second, paint, shown,
        painted, hidden_grad, delta_second, delta_own, shifted, sums, sems,
    ) = refs[groups:]
    copies = [
        pltpu.make_async_copy(second_in, slope_second, sems.at[0]),
        pltpu.make_async_copy(hidden_in, hidden, sems.at[1]),
        pltpu.make_async_copy(conv_second, weight, sems.at[2]),
        pltpu.make_async_copy(first_in, slope_first, sems.at[3]),
        pltpu.make_async_copy(cells_in, cells, sems.at[4]),
    ]
    for copy in copies:
        copy.start()
    slots, channels = cells.shape[-2:]
    rows, cols = cells.shape[0] - 2, cells.shape[1] - 2
    height = rows * lax.axis_size("row")
    view_rows = min(height, rows + 20)
    number = view_rows // parts
    own_slots = slots // groups
    group = lax.axis_index("grp")
    top, _, view_top, _ = corner(rows, cols)
    kept = (cols + 2) * own_slots
    paint[...] = jnp.zeros(paint.shape, jnp.float32)
    paint[0:3] = rgb[...].astype(jnp.float32)
    shown[...] = jnp.zeros(shown.shape, jnp.float32)
    for step in range(groups):
        for k in range(3):
            value = pixels[step][k].astype(jnp.float32)
            for at in range(number):
                shown[step, at * 8 + k : at * 8 + k + 1] = value[at : at + 1]

    def paint_step(at):
        for step in range(groups):
            source = lax.rem(group - step + groups, groups)
            slot = painted.at[at, step]
            slot[...] = lax.dot_general(
                shown[step, pl.ds(pl.multiple_of(at * 8, 8), 8)].astype(jnp.bfloat16),
                paint[...].astype(jnp.bfloat16),
                (((0,), (0,)), ((), ())),
                preferred_element_type=jnp.float32,
            )
            for part in range(parts):
                row = kept_row(view_top + part * number + at, top - 1, rows + 2)
                value = slot[pl.ds(part, kept, stride=parts)] if parts > 1 else slot[...]
                hidden_grad[row, pl.ds(source, kept, stride=groups)] = value

    repeat(number, paint_step, unrolled(number))
    copies[0].wait()

    def delta_step(a):
        row = top - 1 + a
        inside = (row >= 0) & (row < height)
        delta = jnp.where(inside, hidden_grad[a + 1] * slope_second[a], 0.0).astype(jnp.bfloat16)
        delta_second[a] = delta.reshape(cols + 2, slots, channels)

    repeat(rows + 2, delta_step, 5)

    first_row = lax.axis_index("grp") * out_rows
    first_tap = first_row // channels
    skip = pl.multiple_of(first_row - first_tap * channels, 32)
    device = lax.axis_index("row") * lax.axis_size("col") + lax.axis_index("col")

    def put(which):
        value = sums[pl.ds(skip, out_rows)]
        if len(terms.shape) == 3:
            terms[which] = value.astype(jnp.bfloat16)
        else:
            chunks, _, size, _ = terms.shape
            for k in range(chunks):
                piece = value[k * size : (k + 1) * size].astype(jnp.bfloat16)
                terms[lax.rem(k - device + chunks, chunks), which] = piece

    def own_step(r):
        delta_own[r] = delta_second[r + 1, 1 : 1 + cols].reshape(cols * slots, channels)

    repeat(rows, own_step, rows)
    copies[1].wait()
    gradient_taps(hidden, delta_own, shifted, sums, first_tap)
    put(1)

    copies[2].wait()
    copies[3].wait()
    copies[4].wait()
    for dt in range(3):
        for tap in range(9):
            at = (dt * 9 + tap) * channels
            turned = weight[at : at + channels].astype(jnp.float32).T.astype(jnp.bfloat16)
            back_second[
                (8 - tap) * channels : (9 - tap) * channels,
                (2 - dt) * channels : (3 - dt) * channels,
            ] = turned

    def back_row(r, back):
        delta_own[r] = (back * slope_first[r]).astype(jnp.bfloat16)

    conv_pairs(delta_second, rows, cols, back_second, back_row)
    gradient_taps(cells, delta_own, shifted, sums, first_tap)
    put(0)


def call(kernel, outs, scratch, sems, limit, hbm_in=(), hbm_out=(), operands=0, flops=0):
    def spec(at, chosen):
        return pl.BlockSpec(memory_space=pltpu.HBM if at in chosen else pltpu.VMEM)

    scratch = [pltpu.VMEM(*shape) for shape in scratch]
    if sems:
        scratch.append(pltpu.SemaphoreType.DMA((sems,)))
    several = isinstance(outs, tuple)
    return pl.pallas_call(
        kernel,
        out_shape=outs,
        in_specs=[spec(k, hbm_in) for k in range(operands)],
        out_specs=tuple(spec(k, hbm_out) for k in range(len(outs))) if several else spec(0, hbm_out),
        scratch_shapes=scratch,
        compiler_params=pltpu.CompilerParams(vmem_limit_bytes=limit * 2**20),
        cost_estimate=pl.CostEstimate(flops=flops, bytes_accessed=2**20, transcendentals=0),
    )


def row_halo(own, width):
    count, length = lax.axis_size("row"), own.shape[0]
    if count == 2:
        second = lax.axis_index("row")
        edge = lax.dynamic_slice_in_dim(own, (1 - second) * (length - width), width, axis=0)
        came = lax.ppermute(edge, "row", [(0, 1), (1, 0)])
        place = (jnp.arange(2) == 1 - second).reshape(2, 1, 1, 1, 1)
        return jnp.where(place, came[None], jnp.zeros_like(came)[None])
    before = lax.ppermute(own[length - width :], "row", [(i, i + 1) for i in range(count - 1)])
    after = lax.ppermute(own[:width], "row", [(i + 1, i) for i in range(count - 1)])
    return jnp.stack([before, after])


def col_halo(tall, width):
    count, length = lax.axis_size("col"), tall.shape[1]
    before = lax.ppermute(
        tall[:, length - width :], "col", [(i, i + 1) for i in range(count - 1)]
    )
    after = lax.ppermute(tall[:, :width], "col", [(i + 1, i) for i in range(count - 1)])
    return before, after


def local(dec_input, target, conv_first, conv_second, rgb_weight, vgg_first, vgg_second, vgg_third):
    f32, bf16 = jnp.float32, jnp.bfloat16
    row_count, col_count = lax.axis_size("row"), lax.axis_size("col")
    groups, devices = lax.axis_size("grp"), row_count * col_count
    blocks, block_frames, rows, cols, channels = dec_input.shape
    frames = blocks * block_frames
    frames_own = frames // groups
    parts, own_slots = split(rows, frames_own)
    slots = own_slots * groups
    half = parts * own_slots
    height, width = rows * row_count, cols * col_count
    view_rows, view_cols = min(height, rows + 20), min(width, cols + 20)
    number, count = view_rows // parts, view_cols * half
    lanes = -(-count // 128) * 128
    v1, v2 = vgg_first.shape[1], vgg_third.shape[1]

    own = jnp.transpose(dec_input.reshape(frames, rows, cols, channels), (1, 2, 0, 3))
    own = jnp.pad(own, ((0, 0), (0, 0), (0, slots - frames), (0, 0)))
    near = row_halo(own, 3)
    tall = jnp.concatenate([near[0], own, near[1]], axis=0)
    before, after = col_halo(tall, 3)

    line = max(cols * half, -(-width // 128) * 128)
    pack = line // width if parts > 1 and rows % (line // width) == 0 else 1
    target_rows = 3 * blocks * target.shape[2] * rows // pack
    size = -(-(3 * rows + target_rows) // 16) * 16
    big = 16 if parts > 1 else 40

    cells, hidden, slope_first, slope_second, payload = call(
        functools.partial(forward_kernel, frames, parts, pack),
        (
            jax.ShapeDtypeStruct((rows + 2, cols + 2, slots, channels), bf16),
            jax.ShapeDtypeStruct((rows + 2, cols + 2, slots, channels), bf16),
            jax.ShapeDtypeStruct((rows, cols * slots, channels), f32),
            jax.ShapeDtypeStruct((rows + 2, (cols + 2) * slots, channels), f32),
            jax.ShapeDtypeStruct((devices, size, line), bf16),
        ),
        [
            ((rows + 6, cols + 6, slots, channels), bf16),
            ((rows + 4, cols + 4, slots, channels), bf16),
            ((rows, cols * slots, channels), f32),
            ((rows + 2, (cols + 2) * slots, channels), f32),
            ((9 * channels, 3 * channels), bf16),
            ((rows + 2, cols * slots, channels), f32),
            ((rows + 2, cols * half, channels), f32),
            (((rows + 2) * 8, cols * half), f32),
            ((8, channels), f32),
        ],
        4,
        big,
        hbm_out=(0, 1, 2, 3),
        operands=8,
        flops=2**33,
    )(own, near, before, after, conv_first, conv_second, rgb_weight, target)

    received = lax.all_to_all(payload, plane, split_axis=0, concat_axis=0, tiled=True)

    wide_count = count + 6 * half
    pixels = call(
        functools.partial(
            perceptual_kernel,
            (
                rows, cols, blocks, block_frames, target.shape[2], parts, own_slots, frames_own,
                pack,
            ),
        ),
        jax.ShapeDtypeStruct((3, number, (cols + 2) * half), bf16),
        [
            ((128, 2 * v1), f32),
            ((18 * v1, 2 * v1), bf16),
            ((18 * v1, 2 * v2), bf16),
            ((9 * v2, 2 * v1), bf16),
            ((18 * v1, 2 * v1), bf16),
            ((8, 18 * v1), f32),
            ((devices, rows * 8, line), f32),
            ((number * 3, (cols + 2) * half), f32),
            ((devices, size - 3 * rows, line), f32),
            ((frames_own * parts, number * 8, line), f32),
            ((number + 2, 24, lanes), f32),
            ((number + 2, count + 2 * half, 2 * v1), bf16),
            ((number + 2, count, 2 * v1), bf16),
            ((number // 2 + 2, count // 2 + 2 * half, 2 * v1), bf16),
            ((number // 2 + 2, count // 2, 2 * v1), bf16),
            ((number // 2 + 2, count // 2 + 2 * half, v2), bf16),
            ((number // 2 + 2, count // 2, v2), bf16),
            ((number, wide_count, 2 * v1), f32),
            ((number, wide_count, 2 * v1), f32),
            ((number // 2, wide_count, 2 * v1), f32),
            ((number + 2, (cols + 6) * half, 2 * v1), bf16),
            ((number + 2, (cols + 4) * half, 2 * v1), bf16),
            ((number + 2, (cols + 4) * half, 2 * v1), bf16),
            ((number + 2, (cols + 2) * half, 2 * v1), bf16),
        ],
        0,
        big,
        operands=4,
        flops=2**32,
    )(received, vgg_first, vgg_second, vgg_third)

    gathered = [pixels]
    for step in range(1, groups):
        ring = [(i, (i + step) % groups) for i in range(groups)]
        gathered.append(lax.ppermute(pixels, "grp", ring))

    out_rows = conv_first.shape[0] // groups
    taps = max(
        -(-(g + 1) * out_rows // channels) - g * out_rows // channels for g in range(groups)
    )
    even = out_rows % devices == 0
    out_shape = (
        (devices, 2, out_rows // devices, channels) if even else (2, out_rows, channels)
    )
    terms = call(
        functools.partial(backward_kernel, parts=parts, out_rows=out_rows, groups=groups),
        jax.ShapeDtypeStruct(out_shape, bf16),
        [
            ((rows, cols * slots, channels), f32),
            ((rows + 2, (cols + 2) * slots, channels), f32),
            ((rows + 2, cols + 2, slots, channels), bf16),
            ((rows + 2, cols + 2, slots, channels), bf16),
            (conv_second.shape, bf16),
            ((9 * channels, 3 * channels), bf16),
            ((8, channels), f32),
            ((groups, number * 8, (cols + 2) * half), f32),
            ((number, groups, (cols + 2) * half, channels), f32),
            ((rows + 4, (cols + 2) * slots, channels), f32),
            ((rows + 2, cols + 2, slots, channels), bf16),
            ((rows, cols * slots, channels), bf16),
            ((3, rows, channels, cols * slots), bf16),
            ((taps * channels, channels), f32),
        ],
        5,
        big + 8,
        hbm_in=tuple(range(groups + 1, groups + 6)),
        operands=groups + 6,
        flops=2**32,
    )(
        *gathered, rgb_weight, conv_second, slope_first, slope_second, cells, hidden,
    )

    if even:
        pieces = [terms[0]]
        for step in range(1, devices):
            ring = [(i, (i + step) % devices) for i in range(devices)]
            pieces.append(lax.ppermute(terms[step], plane, ring))
        total = sum(piece.astype(f32) for piece in pieces)
    else:
        pieces = jnp.swapaxes(terms.reshape(2, devices, -1), 0, 1)
        pieces = lax.all_to_all(pieces, plane, split_axis=0, concat_axis=0, tiled=True)
        total = jnp.sum(pieces.astype(f32), axis=0)
    return total[0].reshape(-1), total[1].reshape(-1)


def solution(mesh):
    in_specs = (
        P(None, None, "row", "col", None),
        P(None, None, "col", "row", None),
        P(),
        P(),
        P(),
        P(),
        P(),
        P(),
    )
    out_specs = (P(("grp", "row", "col")), P(("grp", "row", "col")))
    return jax.shard_map(local, mesh=mesh, in_specs=in_specs, out_specs=out_specs, check_vma=False)
```

```python
import functools

import jax
import jax.numpy as jnp
from jax import lax
from jax.experimental import pallas as pl
from jax.experimental.pallas import tpu as pltpu
from jax.sharding import PartitionSpec as P

gelu_scale = 0.7978845608028654
gelu_cubic = 0.044715
plane = ("row", "col")


def repeat(count, body, unroll=1):
    lax.fori_loop(0, count, lambda i, carry: (body(i), carry)[1], 0, unroll=unroll)


def matmul(left, right):
    return jnp.dot(left, right, preferred_element_type=jnp.float32)


def gelu_tanh(z):
    return jnp.tanh(gelu_scale * (z + gelu_cubic * z * z * z))


def gelu_slope(z, t):
    return 0.5 * (1.0 + t) + 0.5 * z * (1.0 - t * t) * gelu_scale * (
        1.0 + 3.0 * gelu_cubic * z * z
    )


def split(rows, frames_own):
    small = frames_own <= 4 and lax.axis_size("row") == 2 and rows % 4 == 0
    return (2, 4) if small else (1, 8)


def corner(rows, cols):
    height, width = rows * lax.axis_size("row"), cols * lax.axis_size("col")
    view_rows, view_cols = min(height, rows + 20), min(width, cols + 20)
    top, left = lax.axis_index("row") * rows, lax.axis_index("col") * cols
    view_top = jnp.clip(top - 10, 0, height - view_rows)
    view_left = jnp.clip(left - 10, 0, width - view_cols)
    return top, left, view_top, view_left


def col_mask(first_col, cols, width, slots, frames):
    at = lax.broadcasted_iota(jnp.int32, (cols * slots, 1), 0)
    col = at // slots + first_col
    return (at % slots < frames) & (col >= 0) & (col < width)


def frame_weight(ref):
    third = ref.shape[0] // 3
    return jnp.concatenate([ref[pl.ds(third * k, third)] for k in range(3)], axis=1)


def conv_pairs(source, rows, cols, weight, use):
    slots, channels = source.shape[-2:]
    count = cols * slots

    def step(q):
        slabs = [
            source[pl.ds(2 * q + dr, 2), pl.ds(dc, cols)].reshape(2 * count, channels)
            for dr in range(3)
            for dc in range(3)
        ]
        sums = matmul(jnp.concatenate(slabs, axis=1), weight[...])
        total = (
            pltpu.roll(sums[:, :channels], 1, 0)
            + sums[:, channels : 2 * channels]
            + pltpu.roll(sums[:, 2 * channels :], 2 * count - 1, 0)
        )
        for k in range(2):
            use(2 * q + k, total[k * count : (k + 1) * count])

    repeat(rows // 2, step, rows // 2)


def forward_kernel(frames, parts, pack, places, own, *refs):
    near = refs[: len(places)]
    (
        first, second, rgb, target, cells_out, hidden_out, first_out, second_out, payload,
        cells, hidden, slope_first, slope_second, spread_weight, picked, spaced, colour, project,
        sems,
    ) = refs[len(places) :]
    rows, cols, slots, channels = own.shape
    f32, bf16 = jnp.float32, jnp.bfloat16
    groups, group = lax.axis_size("grp"), lax.axis_index("grp")
    height, width = rows * lax.axis_size("row"), cols * lax.axis_size("col")
    top, left_col = lax.axis_index("row") * rows, lax.axis_index("col") * cols
    cells[3 : 3 + rows, 3 : 3 + cols] = own[...]
    if lax.axis_size("row") == 2:
        start = jnp.where(lax.axis_index("row") == 0, 0, 3 + rows)
        cells[pl.ds(start, 3)] = jnp.zeros((3,) + cells.shape[1:], bf16)
    if lax.axis_size("col") == 2:
        start = jnp.where(lax.axis_index("col") == 0, 0, 3 + cols)
        cells[:, pl.ds(start, 3)] = jnp.zeros((rows + 6, 3) + cells.shape[2:], bf16)
    for (row_at, col_at), piece in zip(places, near):
        row, col = 3, 3
        if row_at is not None:
            row = jnp.where(lax.axis_index("row") % 2 == row_at, 3 + rows, 0)
        if col_at is not None:
            col = jnp.where(lax.axis_index("col") % 2 == col_at, 3 + cols, 0)
        cells[pl.ds(row, piece.shape[0]), pl.ds(col, piece.shape[1])] = piece[...]
    copies = [
        pltpu.make_async_copy(
            cells.at[pl.ds(2, rows + 2), pl.ds(2, cols + 2)], cells_out, sems.at[0]
        ),
        pltpu.make_async_copy(
            hidden.at[pl.ds(1, rows + 2), pl.ds(1, cols + 2)], hidden_out, sems.at[1]
        ),
        pltpu.make_async_copy(slope_first, first_out, sems.at[2]),
        pltpu.make_async_copy(slope_second, second_out, sems.at[3]),
    ]
    copies[0].start()
    spread_weight[...] = frame_weight(first)

    def first_layer(r, pre):
        row = top - 2 + r
        keep = col_mask(left_col - 2, cols + 4, width, slots, frames) & (
            (row >= 0) & (row < height)
        )
        gate = 0.5 + 0.5 * jnp.tanh(0.5 * pre)
        out = jnp.where(keep, pre * gate, 0.0).astype(bf16)
        hidden[r] = out.reshape(cols + 4, slots, channels)
        slope = jnp.where(keep, gate * (1.0 + pre * (1.0 - gate)), 0.0)

        @pl.when((r >= 2) & (r < 2 + rows))
        def _():
            slope_first[r - 2] = slope[2 * slots : (2 + cols) * slots]

    conv_pairs(cells, rows + 4, cols + 4, spread_weight, first_layer)
    copies[1].start()
    copies[2].start()
    spread_weight[...] = frame_weight(second)
    own_slots = slots // groups
    spaced[...] = jnp.zeros(spaced.shape, f32)
    project[...] = jnp.zeros(project.shape, f32)
    project[0:3] = rgb[...].astype(f32)

    def second_layer(r, pre):
        row = top - 1 + r
        keep = col_mask(left_col - 1, cols + 2, width, slots, frames) & (
            (row >= 0) & (row < height)
        )
        gate = 0.5 + 0.5 * jnp.tanh(0.5 * pre)
        slope_second[r] = jnp.where(keep, gate * (1.0 + pre * (1.0 - gate)), 0.0)
        picked[r] = jnp.where(keep, pre * gate, 0.0)[slots : (1 + cols) * slots]
        mine = picked.at[r][pl.ds(group, cols * own_slots, stride=groups)]
        if parts > 1:
            part = lax.axis_index("row")
            spaced.at[r][pl.ds(part, cols * own_slots, stride=parts)] = mine
            mine = spaced[r]
        line = lax.dot_general(
            project[...].astype(bf16), mine.astype(bf16), (((1,), (1,)), ((), ())),
            preferred_element_type=f32,
        )
        at = jnp.clip(r - 1, -1, rows) + 1
        colour[pl.ds(pl.multiple_of(at * 8, 8), 8)] = line

    conv_pairs(hidden, rows + 2, cols + 2, spread_weight, second_layer)
    copies[3].start()
    size, line = payload.shape
    pieces = [colour[pl.ds(8 + k, rows, stride=8)] for k in range(3)]
    goal = target[...].reshape(-1, rows, width).astype(f32)
    if pack > 1:
        short = rows // pack
        goal = jnp.concatenate([goal[:, k * short : (k + 1) * short] for k in range(pack)], axis=2)
    goal = goal.reshape(-1, pack * width)
    if pack * width < line:
        goal = jnp.concatenate(
            [goal, jnp.zeros((goal.shape[0], line - pack * width), f32)], axis=1
        )
    pieces.append(goal)
    filled = 3 * rows + goal.shape[0]
    if filled < size:
        pieces.append(jnp.zeros((size - filled, line), f32))
    lines = jnp.concatenate(pieces, axis=0).astype(bf16)
    payload[...] = lines
    for copy in copies:
        copy.wait()


def plane_slabs(wide, narrow, row, count, half):
    pieces = []
    for dr in range(3):
        pieces.append(wide[row + dr, pl.ds(0, count)])
        pieces.append(narrow[row + dr])
        pieces.append(wide[row + dr, pl.ds(2 * half, count)])
    return jnp.concatenate(pieces, axis=1)


def store_slab(wide, narrow, row, value, half):
    wide[row] = value.astype(jnp.bfloat16)
    narrow[row] = value[half : value.shape[0] - half].astype(jnp.bfloat16)


def store_wide(wide, narrow, row, value, half):
    edge = jnp.zeros((half, value.shape[1]), jnp.float32)
    store_slab(wide, narrow, row, jnp.concatenate([edge, value, edge], axis=0), half)


def fill_edges(parts, *refs):
    for ref in refs:
        last = ref.shape[0] - 1
        if parts == 1:
            for at in (0, last):
                ref[at] = jnp.zeros(ref.shape[1:], ref.dtype)
            continue
        part = lax.broadcasted_iota(jnp.int32, (ref.shape[1], 1), 0) % parts
        low = pltpu.roll(ref[last - 1].astype(jnp.float32), 1, 0)
        high = pltpu.roll(ref[1].astype(jnp.float32), ref.shape[1] - 1, 0)
        ref[0] = jnp.where(part > 0, low, 0.0).astype(ref.dtype)
        ref[last] = jnp.where(part < parts - 1, high, 0.0).astype(ref.dtype)


def kept_row(row, first, number):
    return jnp.clip(row - first, -1, number) + 1


def unrolled(number):
    return number if number <= 8 else 4 if number % 4 == 0 else 2


def plane_weights(
    first, second, third, weight_1, weight_2, weight_3, back_3, back_2, back_1
):
    f32, bf16 = jnp.float32, jnp.bfloat16
    v1, v2 = second.shape[0], third.shape[1]
    zero_3 = jnp.zeros((v1, v2), bf16)
    weight_1[...] = jnp.zeros(weight_1.shape, f32)
    back_1[...] = jnp.zeros(back_1.shape, f32)
    for tap in range(9):
        taken = first[...].astype(f32)[tap * 3 : tap * 3 + 3]
        weight_1[tap * 8 : tap * 8 + 3, 0:v1] = taken
        weight_1[tap * 8 + 3 : tap * 8 + 6, v1 : 2 * v1] = taken
        back_1[0:3, (8 - tap) * 2 * v1 : (8 - tap) * 2 * v1 + v1] = taken
        taken = second[...].astype(f32)[:, tap * v1 : (tap + 1) * v1]
        beside = jnp.concatenate([taken, jnp.zeros_like(taken)], axis=1)
        under = jnp.concatenate([jnp.zeros_like(taken), taken], axis=1)
        both = jnp.concatenate([beside, under], axis=0)
        weight_2[tap * 2 * v1 : (tap + 1) * 2 * v1] = both.T.astype(bf16)
        back_2[(8 - tap) * 2 * v1 : (9 - tap) * 2 * v1] = jnp.concatenate(
            [beside, jnp.zeros_like(beside)], axis=0
        ).astype(bf16)
        taken = third[tap * v1 : (tap + 1) * v1]
        weight_3[tap * 2 * v1 : (tap * 2 + 1) * v1] = jnp.concatenate([taken, zero_3], axis=1)
        weight_3[(tap * 2 + 1) * v1 : (tap * 2 + 2) * v1] = jnp.concatenate(
            [zero_3, taken], axis=1
        )
        turned = jnp.concatenate([taken, zero_3], axis=0).astype(f32).T
        back_3[(8 - tap) * v2 : (9 - tap) * v2] = turned.astype(bf16)


def perceptual_kernel(shape, sources, paired, *refs):
    received = refs[:sources]
    (
        vgg_first, vgg_second, vgg_third, pixels,
        weight_1, weight_2, weight_3, back_3, back_2, back_1, shown, grads,
        target, strips, lines, wide_1, narrow_1, wide_3, narrow_3, wide_g, narrow_g,
        plane_1, plane_2, spread, wide_b, narrow_b, wide_a, narrow_a,
    ) = refs[sources:]
    rows, cols, blocks, block_frames, own, parts, own_slots, frames_own, pack = shape
    f32, bf16 = jnp.float32, jnp.bfloat16
    half = parts * own_slots
    groups, group = lax.axis_size("grp"), lax.axis_index("grp")
    col_parts = lax.axis_size("col")
    width = cols * col_parts
    height = rows * lax.axis_size("row")
    view_rows, view_cols = min(height, rows + 20), min(width, cols + 20)
    top, left, view_top, view_left = corner(rows, cols)
    number = view_rows // parts
    count = view_cols * half
    lanes = lines.shape[2]
    span = width * half
    v1 = weight_2.shape[1] // 2
    v2 = weight_3.shape[1] // 2
    body = pl.ds(3 * half, count)
    plane_weights(
        vgg_first, vgg_second, vgg_third, weight_1, weight_2, weight_3, back_3, back_2, back_1
    )

    place = lax.axis_index("row") * col_parts + lax.axis_index("col")
    for at in range(shown.shape[0]):
        per_source = received[0].shape[0]
        device = place ^ at if paired else at
        arrived = received[at // per_source][at % per_source].astype(f32)
        target[device] = arrived[3 * rows :]
        shown[device] = jnp.zeros(shown.shape[1:], f32)
        for k in range(3):
            shown.at[device][pl.ds(k, rows, stride=8)] = arrived[k * rows : (k + 1) * rows]
    strips[...] = jnp.zeros(strips.shape, f32)
    for j in range(frames_own):
        frame = groups * j + group
        block, rest = frame // block_frames, frame % block_frames
        for part in range(parts):
            for k in range(3):
                short = rows // pack
                start = ((k * blocks + block) * own + rest % own) * short

                def take(at, j=j, part=part, k=k, start=start, rest=rest):
                    row = view_top + part * number + at
                    device = (row // rows) * col_parts + rest // own
                    strips[j * parts + part, pl.ds(at * 8 + 3 + k, 1)] = target[
                        device, pl.ds(start + row % rows, 1)
                    ]

                if parts > 1:
                    device = part * col_parts + rest // own
                    value = target[device, pl.ds(start, short)]
                    for turn in range(pack):
                        strips[j * parts + part, pl.ds(3 + k + turn * short * 8, short, stride=8)] = (
                            pltpu.roll(value, (pack - turn) * width % value.shape[1], 1)
                        )
                else:
                    repeat(number, take)
    from_col = lax.broadcasted_iota(jnp.int32, (target.shape[2], lanes), 0) - view_left
    to_lane = lax.broadcasted_iota(jnp.int32, (target.shape[2], lanes), 1)
    guide = 0.0
    for j in range(frames_own):
        for part in range(parts):
            place = (from_col * half + (j * parts + part) == to_lane) & (to_lane < count)
            guide = guide + matmul(
                strips[j * parts + part].astype(bf16),
                jnp.where(place, 1.0, 0.0).astype(bf16),
            )
    lane = lax.broadcasted_iota(jnp.int32, (8, lanes), 1)
    strips_line = lines.at[pl.ds(1, number)]
    for at in range(number):
        strips_line[at, pl.ds(8, 8)] = guide[at * 8 : at * 8 + 8]

    def line_step(at):
        line = 0.0
        for part in range(parts):
            row = view_top + part * number + at
            source = pl.ds(pl.multiple_of(row % rows * 8, 8), 8)
            line = line + jnp.concatenate(
                [
                    shown[(row // rows) * col_parts + k, source][:, : cols * half]
                    for k in range(col_parts)
                ],
                axis=1,
            )
        line = pltpu.roll(line, lax.rem(span - view_left * half, span), 1)[:, :lanes]
        line = jnp.where(lane < count, line, 0.0) + lines[at + 1, pl.ds(8, 8)]
        before = jnp.where(lane < half, 0.0, pltpu.roll(line, half, 1))
        after = jnp.where(lane >= count - half, 0.0, pltpu.roll(line, lanes - half, 1))
        lines[at + 1] = jnp.concatenate([before, line, after], axis=0)

    repeat(number, line_step, unrolled(number))
    wide_lane = lax.broadcasted_iota(jnp.int32, (24, lanes), 1)
    if parts > 1:
        part = wide_lane % parts
        inside = wide_lane < count
        low = pltpu.roll(lines[number], 1, 1)
        high = pltpu.roll(lines[1], lanes - 1, 1)
        lines[0] = jnp.where((part > 0) & inside, low, 0.0)
        lines[number + 1] = jnp.where((part < parts - 1) & inside, high, 0.0)
    else:
        lines[0] = jnp.zeros((24, lanes), f32)
        lines[number + 1] = jnp.zeros((24, lanes), f32)

    def first_step(at):
        pieces = [lines[at], lines[at + 1], lines[at + 2], jnp.zeros((56, lanes), f32)]
        patches = jnp.concatenate(pieces, axis=0).T[:count].astype(bf16)
        z = matmul(patches, weight_1[...].astype(bf16))
        plane_1[at, body] = z
        store_wide(wide_1, narrow_1, at + 1, 0.5 * z * (1.0 + gelu_tanh(z)), half)

    repeat(number, first_step, unrolled(number))
    fill_edges(parts, wide_1, narrow_1)

    def second_step(q):
        total = 0.0
        for step in range(2):
            at = 2 * q + step
            z = matmul(plane_slabs(wide_1, narrow_1, at, count, half), weight_2[...])
            plane_2[at, body] = z
            total = total + 0.5 * z * (1.0 + gelu_tanh(z))
        pooled = total.reshape(view_cols // 2, 2, half, 2 * v1)
        pooled = 0.25 * (pooled[:, 0] + pooled[:, 1])
        store_wide(wide_3, narrow_3, q + 1, pooled.reshape(count // 2, 2 * v1), half)

    repeat(number // 2, second_step, unrolled(number // 2))
    fill_edges(parts, wide_3, narrow_3)

    def third_step(q):
        z = matmul(plane_slabs(wide_3, narrow_3, q, count // 2, half), weight_3[...])
        t = gelu_tanh(z)
        value = 0.5 * z * (1.0 + t)
        delta = (64.0 / v2) * (value[:, :v2] - value[:, v2:]) * gelu_slope(z[:, :v2], t[:, :v2])
        store_wide(wide_g, narrow_g, q + 1, delta, half)

    repeat(number // 2, third_step, unrolled(number // 2))
    fill_edges(parts, wide_g, narrow_g)

    def pool_step(q):
        grad = 0.25 * matmul(plane_slabs(wide_g, narrow_g, q, count // 2, half), back_3[...])
        grad = grad.reshape(view_cols // 2, 1, half, 2 * v1)
        spread[q, body] = jnp.concatenate([grad, grad], axis=1).reshape(count, 2 * v1)

    repeat(number // 2, pool_step, unrolled(number // 2))

    def near(reach):
        size = (cols + 2 * reach) * half
        keep = col_mask(left - reach, cols + 2 * reach, width, half, half)
        start = pl.multiple_of((left - view_left + 3 - reach) * half, 8)
        return keep, pl.ds(start, size), size

    def second_delta(at):
        keep, where, _ = near(3)
        z = plane_2[at, where]
        t = gelu_tanh(z)
        value = 0.5 * z * (1.0 + t)
        delta = spread[at // 2, where] + (16.0 / v1) * (value - pltpu.roll(value, v1, 1))
        store_slab(wide_b, narrow_b, at + 1, jnp.where(keep, delta * gelu_slope(z, t), 0.0), half)

    repeat(number, second_delta, unrolled(number))
    fill_edges(parts, wide_b, narrow_b)

    def first_delta(at):
        keep, where, size = near(2)
        grad = matmul(plane_slabs(wide_b, narrow_b, at, size, half), back_2[...])
        z = plane_1[at, where]
        delta = jnp.where(keep, grad * gelu_slope(z, gelu_tanh(z)), 0.0)
        store_slab(wide_a, narrow_a, at + 1, delta, half)

    repeat(number, first_delta, unrolled(number))
    fill_edges(parts, wide_a, narrow_a)

    def pixel_step(at):
        size = (cols + 2) * half
        grad = lax.dot_general(
            back_1[...].astype(bf16), plane_slabs(wide_a, narrow_a, at, size, half), (((1,), (1,)), ((), ())),
            preferred_element_type=f32,
        )
        line = lines[at + 1, pl.ds(8, 8)]
        line = line - pltpu.roll(line, 5, 0)
        shift = lax.rem((view_left - left + 1) * half + 2 * lanes, lanes)
        line = pltpu.roll(line, shift, 1)
        grad = grad + (1.0 / 6.0) * line[:, :size]
        for k in range(3):
            grads[pl.ds(k * number + at, 1)] = grad[k : k + 1]

    repeat(number, pixel_step, unrolled(number))
    for k in range(3):
        pixels[k] = grads[k * number : (k + 1) * number].astype(bf16)


def gradient_taps(source, delta, shifted, sums, first_tap):
    rows = delta.shape[0]
    slots, channels = source.shape[-2:]
    cols = source.shape[1] - 2
    count = cols * slots

    def turn(r):
        block = delta[r].astype(jnp.float32)
        for dt in range(3):
            moved = block if dt == 1 else pltpu.roll(block, (dt - 1) % count, 0)
            shifted[dt, r] = moved.T.astype(jnp.bfloat16)

    repeat(rows, turn, rows)

    def tap_step(step):
        tap = jnp.minimum(first_tap + step, 26)
        dt, dr, dc = tap // 9, tap // 3 % 3, tap % 3
        total = 0.0
        for r in range(rows):
            slab = source[r + dr, pl.ds(dc, cols)].reshape(count, channels)
            total = total + matmul(shifted[dt, r], slab)
        sums[pl.ds(pl.multiple_of(step * channels, channels), channels)] = total.T

    repeat(sums.shape[0] // channels, tap_step, 8)


def backward_kernel(*refs, parts, out_rows, groups):
    pixels = refs[:groups]
    (
        rgb, conv_second, first_in, second_in, cells_in, hidden_in, terms,
        slope_first, slope_second, cells, hidden, weight, back_second, paint, shown,
        painted, hidden_grad, delta_second, delta_own, shifted, sums, sems,
    ) = refs[groups:]
    copies = [
        pltpu.make_async_copy(second_in, slope_second, sems.at[0]),
        pltpu.make_async_copy(hidden_in, hidden, sems.at[1]),
        pltpu.make_async_copy(conv_second, weight, sems.at[2]),
        pltpu.make_async_copy(first_in, slope_first, sems.at[3]),
        pltpu.make_async_copy(cells_in, cells, sems.at[4]),
    ]
    for copy in copies:
        copy.start()
    slots, channels = cells.shape[-2:]
    rows, cols = cells.shape[0] - 2, cells.shape[1] - 2
    height = rows * lax.axis_size("row")
    view_rows = min(height, rows + 20)
    number = view_rows // parts
    own_slots = slots // groups
    group = lax.axis_index("grp")
    top, _, view_top, _ = corner(rows, cols)
    kept = (cols + 2) * own_slots
    paint[...] = jnp.zeros(paint.shape, jnp.float32)
    paint[0:3] = rgb[...].astype(jnp.float32)
    shown[...] = jnp.zeros(shown.shape, jnp.float32)
    for step in range(groups):
        for k in range(3):
            value = pixels[step][k].astype(jnp.float32)
            for at in range(number):
                shown[step, at * 8 + k : at * 8 + k + 1] = value[at : at + 1]

    def paint_step(at):
        for step in range(groups):
            source = partner(group, step, groups)
            slot = painted.at[at, step]
            slot[...] = lax.dot_general(
                shown[step, pl.ds(pl.multiple_of(at * 8, 8), 8)].astype(jnp.bfloat16),
                paint[...].astype(jnp.bfloat16),
                (((0,), (0,)), ((), ())),
                preferred_element_type=jnp.float32,
            )
            for part in range(parts):
                row = kept_row(view_top + part * number + at, top - 1, rows + 2)
                value = slot[pl.ds(part, kept, stride=parts)] if parts > 1 else slot[...]
                hidden_grad[row, pl.ds(source, kept, stride=groups)] = value

    repeat(number, paint_step, unrolled(number))
    copies[0].wait()

    def delta_step(a):
        row = top - 1 + a
        inside = (row >= 0) & (row < height)
        delta = jnp.where(inside, hidden_grad[a + 1] * slope_second[a], 0.0).astype(jnp.bfloat16)
        delta_second[a] = delta.reshape(cols + 2, slots, channels)

    repeat(rows + 2, delta_step, 5)

    first_row = lax.axis_index("grp") * out_rows
    first_tap = first_row // channels
    skip = pl.multiple_of(first_row - first_tap * channels, 32)
    device = lax.axis_index("row") * lax.axis_size("col") + lax.axis_index("col")

    def put(which):
        value = sums[pl.ds(skip, out_rows)]
        if len(terms.shape) == 3:
            terms[which] = value.astype(jnp.bfloat16)
        else:
            chunks, _, size, _ = terms.shape
            for k in range(chunks):
                piece = value[k * size : (k + 1) * size].astype(jnp.bfloat16)
                if chunks & (chunks - 1):
                    at = lax.rem(k - device + chunks, chunks)
                else:
                    at = device ^ k
                terms[at, which] = piece

    def own_step(r):
        delta_own[r] = delta_second[r + 1, 1 : 1 + cols].reshape(cols * slots, channels)

    repeat(rows, own_step, rows)
    copies[1].wait()
    gradient_taps(hidden, delta_own, shifted, sums, first_tap)
    put(1)

    copies[2].wait()
    copies[3].wait()
    copies[4].wait()
    for dt in range(3):
        for tap in range(9):
            at = (dt * 9 + tap) * channels
            turned = weight[at : at + channels].astype(jnp.float32).T.astype(jnp.bfloat16)
            back_second[
                (8 - tap) * channels : (9 - tap) * channels,
                (2 - dt) * channels : (3 - dt) * channels,
            ] = turned

    def back_row(r, back):
        delta_own[r] = (back * slope_first[r]).astype(jnp.bfloat16)

    conv_pairs(delta_second, rows, cols, back_second, back_row)
    gradient_taps(cells, delta_own, shifted, sums, first_tap)
    put(0)


def call(kernel, outs, scratch, sems, limit, hbm_in=(), hbm_out=(), operands=0, flops=0):
    def spec(at, chosen):
        return pl.BlockSpec(memory_space=pltpu.HBM if at in chosen else pltpu.VMEM)

    scratch = [pltpu.VMEM(*shape) for shape in scratch]
    if sems:
        scratch.append(pltpu.SemaphoreType.DMA((sems,)))
    several = isinstance(outs, tuple)
    return pl.pallas_call(
        kernel,
        out_shape=outs,
        in_specs=[spec(k, hbm_in) for k in range(operands)],
        out_specs=tuple(spec(k, hbm_out) for k in range(len(outs))) if several else spec(0, hbm_out),
        scratch_shapes=scratch,
        compiler_params=pltpu.CompilerParams(vmem_limit_bytes=limit * 2**20),
        cost_estimate=pl.CostEstimate(flops=flops, bytes_accessed=2**20, transcendentals=0),
    )


def partners(step, count):
    if count & (count - 1):
        return [(i, (i + step) % count) for i in range(count)]
    return [(i, i ^ step) for i in range(count)]


def partner(index, step, count):
    if count & (count - 1):
        return lax.rem(index - step + count, count)
    return index ^ step


def matchings(axis):
    count = lax.axis_size(axis)
    pairs = []
    for first in range(2 if count > 2 else 1):
        pairs.append([(i, i + 1) for i in range(first, count - 1, 2)])
    return pairs


def exchange_pieces(field, width):
    row_pairs, col_pairs = matchings("row"), matchings("col")
    col_count = lax.axis_size("col")
    rows, cols = field.shape[1:3]
    pieces = []
    for row_at in (None, *range(len(row_pairs))):
        for col_at in (None, *range(len(col_pairs))):
            if row_at is None and col_at is None:
                continue
            edge, moves = field, []
            for axis, dim, at, length in (("row", 1, row_at, rows), ("col", 2, col_at, cols)):
                if at is not None:
                    after = (lax.axis_index(axis) % 2 == at).astype(jnp.int32)
                    edge = lax.dynamic_slice_in_dim(edge, after * (length - width), width, axis=dim)
            row_moves = [(i, i) for i in range(lax.axis_size("row"))]
            col_moves = [(i, i) for i in range(col_count)]
            if row_at is not None:
                row_moves = [pair for a, b in row_pairs[row_at] for pair in ((a, b), (b, a))]
            if col_at is not None:
                col_moves = [pair for a, b in col_pairs[col_at] for pair in ((a, b), (b, a))]
            moves = [
                (a * col_count + c, b * col_count + d) for a, b in row_moves for c, d in col_moves
            ]
            pieces.append(((row_at, col_at), edge, moves))
    return pieces


def slotted(field, slots):
    field = jnp.transpose(field, (1, 2, 0, 3))
    return jnp.pad(field, ((0, 0), (0, 0), (0, slots - field.shape[2]), (0, 0)))


def local(dec_input, target, conv_first, conv_second, rgb_weight, vgg_first, vgg_second, vgg_third):
    f32, bf16 = jnp.float32, jnp.bfloat16
    row_count, col_count = lax.axis_size("row"), lax.axis_size("col")
    groups, devices = lax.axis_size("grp"), row_count * col_count
    blocks, block_frames, rows, cols, channels = dec_input.shape
    frames = blocks * block_frames
    frames_own = frames // groups
    parts, own_slots = split(rows, frames_own)
    slots = own_slots * groups
    half = parts * own_slots
    height, width = rows * row_count, cols * col_count
    view_rows, view_cols = min(height, rows + 20), min(width, cols + 20)
    number, count = view_rows // parts, view_cols * half
    lanes = -(-count // 128) * 128
    v1, v2 = vgg_first.shape[1], vgg_third.shape[1]

    raw = dec_input.reshape(frames, rows, cols, channels)
    pieces = exchange_pieces(raw, 3)
    places = tuple(place for place, _, _ in pieces)
    near = [lax.ppermute(slotted(edge, slots), plane, moves) for _, edge, moves in pieces]
    own = slotted(raw, slots)

    line = max(cols * half, -(-width // 128) * 128)
    pack = line // width if parts > 1 and rows % (line // width) == 0 else 1
    target_rows = 3 * blocks * target.shape[2] * rows // pack
    size = -(-(3 * rows + target_rows) // 16) * 16
    big = 16 if parts > 1 else 40

    cells, hidden, slope_first, slope_second, payload = call(
        functools.partial(forward_kernel, frames, parts, pack, places),
        (
            pltpu.HBM((rows + 2, cols + 2, slots, channels), bf16),
            pltpu.HBM((rows + 2, cols + 2, slots, channels), bf16),
            pltpu.HBM((rows, cols * slots, channels), f32),
            pltpu.HBM((rows + 2, (cols + 2) * slots, channels), f32),
            jax.ShapeDtypeStruct((size, line), bf16),
        ),
        [
            ((rows + 6, cols + 6, slots, channels), bf16),
            ((rows + 4, cols + 4, slots, channels), bf16),
            ((rows, cols * slots, channels), f32),
            ((rows + 2, (cols + 2) * slots, channels), f32),
            ((9 * channels, 3 * channels), bf16),
            ((rows + 2, cols * slots, channels), f32),
            ((rows + 2, cols * half, channels), f32),
            (((rows + 2) * 8, cols * half), f32),
            ((8, channels), f32),
        ],
        4,
        big,
        hbm_out=(0, 1, 2, 3),
        operands=5 + len(near),
        flops=2**33,
    )(own, *near, conv_first, conv_second, rgb_weight, target)

    paired = devices == 8 and col_count % 2 == 0
    if paired:
        other = lax.ppermute(payload, plane, [(i, i ^ 1) for i in range(devices)])
        both = jnp.stack([payload, other])
        received = [both] + [
            lax.ppermute(both, plane, [(i, i ^ step) for i in range(devices)])
            for step in range(2, devices, 2)
        ]
    else:
        received = [
            lax.all_to_all(
                jnp.broadcast_to(payload[None], (devices,) + payload.shape),
                plane,
                split_axis=0,
                concat_axis=0,
                tiled=True,
            )
        ]

    wide_count = count + 6 * half
    pixels = call(
        functools.partial(
            perceptual_kernel,
            (
                rows, cols, blocks, block_frames, target.shape[2], parts, own_slots, frames_own,
                pack,
            ),
            len(received),
            paired,
        ),
        jax.ShapeDtypeStruct((3, number, (cols + 2) * half), bf16),
        [
            ((128, 2 * v1), f32),
            ((18 * v1, 2 * v1), bf16),
            ((18 * v1, 2 * v2), bf16),
            ((9 * v2, 2 * v1), bf16),
            ((18 * v1, 2 * v1), bf16),
            ((8, 18 * v1), f32),
            ((devices, rows * 8, line), f32),
            ((number * 3, (cols + 2) * half), f32),
            ((devices, size - 3 * rows, line), f32),
            ((frames_own * parts, number * 8, line), f32),
            ((number + 2, 24, lanes), f32),
            ((number + 2, count + 2 * half, 2 * v1), bf16),
            ((number + 2, count, 2 * v1), bf16),
            ((number // 2 + 2, count // 2 + 2 * half, 2 * v1), bf16),
            ((number // 2 + 2, count // 2, 2 * v1), bf16),
            ((number // 2 + 2, count // 2 + 2 * half, v2), bf16),
            ((number // 2 + 2, count // 2, v2), bf16),
            ((number, wide_count, 2 * v1), f32),
            ((number, wide_count, 2 * v1), f32),
            ((number // 2, wide_count, 2 * v1), f32),
            ((number + 2, (cols + 6) * half, 2 * v1), bf16),
            ((number + 2, (cols + 4) * half, 2 * v1), bf16),
            ((number + 2, (cols + 4) * half, 2 * v1), bf16),
            ((number + 2, (cols + 2) * half, 2 * v1), bf16),
        ],
        0,
        big,
        operands=3 + len(received),
        flops=2**32,
    )(*received, vgg_first, vgg_second.T, vgg_third)

    gathered = [pixels]
    for step in range(1, groups):
        gathered.append(lax.ppermute(pixels, "grp", partners(step, groups)))

    out_rows = conv_first.shape[0] // groups
    taps = max(
        -(-(g + 1) * out_rows // channels) - g * out_rows // channels for g in range(groups)
    )
    even = out_rows % devices == 0
    out_shape = (
        (devices, 2, out_rows // devices, channels) if even else (2, out_rows, channels)
    )
    terms = call(
        functools.partial(backward_kernel, parts=parts, out_rows=out_rows, groups=groups),
        jax.ShapeDtypeStruct(out_shape, bf16),
        [
            ((rows, cols * slots, channels), f32),
            ((rows + 2, (cols + 2) * slots, channels), f32),
            ((rows + 2, cols + 2, slots, channels), bf16),
            ((rows + 2, cols + 2, slots, channels), bf16),
            (conv_second.shape, bf16),
            ((9 * channels, 3 * channels), bf16),
            ((8, channels), f32),
            ((groups, number * 8, (cols + 2) * half), f32),
            ((number, groups, (cols + 2) * half, channels), f32),
            ((rows + 4, (cols + 2) * slots, channels), f32),
            ((rows + 2, cols + 2, slots, channels), bf16),
            ((rows, cols * slots, channels), bf16),
            ((3, rows, channels, cols * slots), bf16),
            ((taps * channels, channels), f32),
        ],
        5,
        big + 8,
        hbm_in=tuple(range(groups + 1, groups + 6)),
        operands=groups + 6,
        flops=2**32,
    )(
        *gathered, rgb_weight, conv_second, slope_first, slope_second, cells, hidden,
    )

    if even:
        pieces = [terms[0]]
        for step in range(1, devices):
            pieces.append(lax.ppermute(terms[step], plane, partners(step, devices)))
        total = sum(piece.astype(f32) for piece in pieces)
    else:
        pieces = jnp.swapaxes(terms.reshape(2, devices, -1), 0, 1)
        pieces = lax.all_to_all(pieces, plane, split_axis=0, concat_axis=0, tiled=True)
        total = jnp.sum(pieces.astype(f32), axis=0)
    return total[0].reshape(-1), total[1].reshape(-1)


def solution(mesh):
    in_specs = (
        P(None, None, "row", "col", None),
        P(None, None, "col", "row", None),
        P(),
        P(),
        P(),
        P(),
        P(),
        P(),
    )
    out_specs = (P(("grp", "row", "col")), P(("grp", "row", "col")))
    return jax.shard_map(local, mesh=mesh, in_specs=in_specs, out_specs=out_specs, check_vma=False)
```

```python
import functools

import jax
import jax.numpy as jnp
from jax import lax
from jax.experimental import pallas as pl
from jax.experimental.pallas import tpu as pltpu
from jax.sharding import PartitionSpec as P

gelu_scale = 0.7978845608028654
gelu_cubic = 0.044715
plane = ("row", "col")


def repeat(count, body, unroll=1):
    lax.fori_loop(0, count, lambda i, carry: (body(i), carry)[1], 0, unroll=unroll)


def matmul(left, right):
    return jnp.dot(left, right, preferred_element_type=jnp.float32)


def gelu_tanh(z):
    return jnp.tanh(gelu_scale * (z + gelu_cubic * z * z * z))


def gelu_slope(z, t):
    return 0.5 * (1.0 + t) + 0.5 * z * (1.0 - t * t) * gelu_scale * (
        1.0 + 3.0 * gelu_cubic * z * z
    )


def split(rows, frames_own):
    small = frames_own <= 4 and lax.axis_size("row") == 2 and rows % 4 == 0
    return (2, 4) if small else (1, 8)


def corner(rows, cols):
    height, width = rows * lax.axis_size("row"), cols * lax.axis_size("col")
    view_rows, view_cols = min(height, rows + 20), min(width, cols + 20)
    top, left = lax.axis_index("row") * rows, lax.axis_index("col") * cols
    view_top = jnp.clip(top - 10, 0, height - view_rows)
    view_left = jnp.clip(left - 10, 0, width - view_cols)
    return top, left, view_top, view_left


def col_mask(first_col, cols, width, slots, frames):
    at = lax.broadcasted_iota(jnp.int32, (cols * slots, 1), 0)
    col = at // slots + first_col
    return (at % slots < frames) & (col >= 0) & (col < width)


def frame_weight(ref):
    third = ref.shape[0] // 3
    return jnp.concatenate([ref[pl.ds(third * k, third)] for k in range(3)], axis=1)


def conv_pairs(source, rows, cols, weight, use):
    slots, channels = source.shape[-2:]
    count = cols * slots

    def step(q):
        slabs = [
            source[pl.ds(2 * q + dr, 2), pl.ds(dc, cols)].reshape(2 * count, channels)
            for dr in range(3)
            for dc in range(3)
        ]
        sums = matmul(jnp.concatenate(slabs, axis=1), weight[...])
        total = (
            pltpu.roll(sums[:, :channels], 1, 0)
            + sums[:, channels : 2 * channels]
            + pltpu.roll(sums[:, 2 * channels :], 2 * count - 1, 0)
        )
        for k in range(2):
            use(2 * q + k, total[k * count : (k + 1) * count])

    repeat(rows // 2, step, rows // 2)


def forward_kernel(frames, parts, pack, places, own, *refs):
    near = refs[: len(places)]
    (
        first, second, rgb, target, cells_out, hidden_out, first_out, second_out, payload,
        cells, hidden, slope_first, slope_second, spread_weight, picked, spaced, colour, project,
        unpacked, corner_rows, sems,
    ) = refs[len(places) :]
    unpacked[...] = jnp.zeros(unpacked.shape, jnp.float32)
    rows, cols, slots, channels = own.shape
    f32, bf16 = jnp.float32, jnp.bfloat16
    groups, group = lax.axis_size("grp"), lax.axis_index("grp")
    height, width = rows * lax.axis_size("row"), cols * lax.axis_size("col")
    top, left_col = lax.axis_index("row") * rows, lax.axis_index("col") * cols
    cells[3 : 3 + rows, 3 : 3 + cols] = own[...]
    if lax.axis_size("row") == 2:
        start = jnp.where(lax.axis_index("row") == 0, 0, 3 + rows)
        cells[pl.ds(start, 3)] = jnp.zeros((3,) + cells.shape[1:], bf16)
    if lax.axis_size("col") == 2:
        start = jnp.where(lax.axis_index("col") == 0, 0, 3 + cols)
        cells[:, pl.ds(start, 3)] = jnp.zeros((rows + 6, 3) + cells.shape[2:], bf16)
    for (row_at, col_at), piece in zip(places, near):
        row, col = 3, 3
        if row_at is not None:
            row = jnp.where(lax.axis_index("row") % 2 == row_at, 3 + rows, 0)
        if col_at is not None:
            col = jnp.where(lax.axis_index("col") % 2 == col_at, 3 + cols, 0)
        if row_at is None:
            for f in range(frames):
                for c in range(3):
                    unpacked[pl.ds(c * rows * slots + f, rows, stride=slots)] = piece[f, c].astype(
                        f32
                    )
            for c in range(3):
                line = unpacked[c * rows * slots : (c + 1) * rows * slots].astype(bf16)
                cells[3 : 3 + rows, col + c] = line.reshape(rows, slots, channels)
        elif col_at is None:
            for f in range(frames):
                for r in range(3):
                    unpacked[pl.ds(r * cols * slots + f, cols, stride=slots)] = piece[f, r].astype(
                        f32
                    )
            for r in range(3):
                line = unpacked[r * cols * slots : (r + 1) * cols * slots].astype(bf16)
                cells[row + r, 3 : 3 + cols] = line.reshape(cols, slots, channels)
        else:
            corner_rows[...] = piece[...].astype(f32)
            for r in range(3):
                for c in range(3):
                    unpacked[0:frames] = corner_rows[pl.ds(r * 3 + c, frames, stride=9)]
                    cells[row + r, col + c] = unpacked[0:slots].astype(bf16)
    copies = [
        pltpu.make_async_copy(
            cells.at[pl.ds(2, rows + 2), pl.ds(2, cols + 2)], cells_out, sems.at[0]
        ),
        pltpu.make_async_copy(
            hidden.at[pl.ds(1, rows + 2), pl.ds(1, cols + 2)], hidden_out, sems.at[1]
        ),
        pltpu.make_async_copy(slope_first, first_out, sems.at[2]),
        pltpu.make_async_copy(slope_second, second_out, sems.at[3]),
    ]
    copies[0].start()
    spread_weight[...] = frame_weight(first)

    def first_layer(r, pre):
        row = top - 2 + r
        keep = col_mask(left_col - 2, cols + 4, width, slots, frames) & (
            (row >= 0) & (row < height)
        )
        gate = 0.5 + 0.5 * jnp.tanh(0.5 * pre)
        out = jnp.where(keep, pre * gate, 0.0).astype(bf16)
        hidden[r] = out.reshape(cols + 4, slots, channels)
        slope = jnp.where(keep, gate * (1.0 + pre * (1.0 - gate)), 0.0)

        @pl.when((r >= 2) & (r < 2 + rows))
        def _():
            slope_first[r - 2] = slope[2 * slots : (2 + cols) * slots]

    conv_pairs(cells, rows + 4, cols + 4, spread_weight, first_layer)
    copies[1].start()
    copies[2].start()
    spread_weight[...] = frame_weight(second)
    own_slots = slots // groups
    spaced[...] = jnp.zeros(spaced.shape, f32)
    project[...] = jnp.zeros(project.shape, f32)
    project[0:3] = rgb[...].astype(f32)

    def second_layer(r, pre):
        row = top - 1 + r
        keep = col_mask(left_col - 1, cols + 2, width, slots, frames) & (
            (row >= 0) & (row < height)
        )
        gate = 0.5 + 0.5 * jnp.tanh(0.5 * pre)
        slope_second[r] = jnp.where(keep, gate * (1.0 + pre * (1.0 - gate)), 0.0)
        picked[r] = jnp.where(keep, pre * gate, 0.0)[slots : (1 + cols) * slots]
        mine = picked.at[r][pl.ds(group, cols * own_slots, stride=groups)]
        if parts > 1:
            part = lax.axis_index("row")
            spaced.at[r][pl.ds(part, cols * own_slots, stride=parts)] = mine
            mine = spaced[r]
        line = lax.dot_general(
            project[...].astype(bf16), mine.astype(bf16), (((1,), (1,)), ((), ())),
            preferred_element_type=f32,
        )
        at = jnp.clip(r - 1, -1, rows) + 1
        colour[pl.ds(pl.multiple_of(at * 8, 8), 8)] = line

    conv_pairs(hidden, rows + 2, cols + 2, spread_weight, second_layer)
    copies[3].start()
    size, line = payload.shape
    pieces = [colour[pl.ds(8 + k, rows, stride=8)] for k in range(3)]
    goal = target[...].reshape(-1, rows, width).astype(f32)
    if pack > 1:
        short = rows // pack
        goal = jnp.concatenate([goal[:, k * short : (k + 1) * short] for k in range(pack)], axis=2)
    goal = goal.reshape(-1, pack * width)
    if pack * width < line:
        goal = jnp.concatenate(
            [goal, jnp.zeros((goal.shape[0], line - pack * width), f32)], axis=1
        )
    pieces.append(goal)
    filled = 3 * rows + goal.shape[0]
    if filled < size:
        pieces.append(jnp.zeros((size - filled, line), f32))
    lines = jnp.concatenate(pieces, axis=0).astype(bf16)
    payload[...] = lines
    for copy in copies:
        copy.wait()


def plane_slabs(wide, narrow, row, count, half):
    pieces = []
    for dr in range(3):
        pieces.append(wide[row + dr, pl.ds(0, count)])
        pieces.append(narrow[row + dr])
        pieces.append(wide[row + dr, pl.ds(2 * half, count)])
    return jnp.concatenate(pieces, axis=1)


def store_slab(wide, narrow, row, value, half):
    wide[row] = value.astype(jnp.bfloat16)
    narrow[row] = value[half : value.shape[0] - half].astype(jnp.bfloat16)


def store_wide(wide, narrow, row, value, half):
    edge = jnp.zeros((half, value.shape[1]), jnp.float32)
    store_slab(wide, narrow, row, jnp.concatenate([edge, value, edge], axis=0), half)


def fill_edges(parts, *refs):
    for ref in refs:
        last = ref.shape[0] - 1
        if parts == 1:
            for at in (0, last):
                ref[at] = jnp.zeros(ref.shape[1:], ref.dtype)
            continue
        part = lax.broadcasted_iota(jnp.int32, (ref.shape[1], 1), 0) % parts
        low = pltpu.roll(ref[last - 1].astype(jnp.float32), 1, 0)
        high = pltpu.roll(ref[1].astype(jnp.float32), ref.shape[1] - 1, 0)
        ref[0] = jnp.where(part > 0, low, 0.0).astype(ref.dtype)
        ref[last] = jnp.where(part < parts - 1, high, 0.0).astype(ref.dtype)


def kept_row(row, first, number):
    return jnp.clip(row - first, -1, number) + 1


def unrolled(number):
    return number if number <= 8 else 4 if number % 4 == 0 else 2


def plane_weights(
    first, second, third, weight_1, weight_2, weight_3, back_3, back_2, back_1
):
    f32, bf16 = jnp.float32, jnp.bfloat16
    v1, v2 = second.shape[0], third.shape[1]
    zero_3 = jnp.zeros((v1, v2), bf16)
    weight_1[...] = jnp.zeros(weight_1.shape, f32)
    back_1[...] = jnp.zeros(back_1.shape, f32)
    for tap in range(9):
        taken = first[...].astype(f32)[tap * 3 : tap * 3 + 3]
        weight_1[tap * 8 : tap * 8 + 3, 0:v1] = taken
        weight_1[tap * 8 + 3 : tap * 8 + 6, v1 : 2 * v1] = taken
        back_1[0:3, (8 - tap) * 2 * v1 : (8 - tap) * 2 * v1 + v1] = taken
        taken = second[...].astype(f32)[:, tap * v1 : (tap + 1) * v1]
        beside = jnp.concatenate([taken, jnp.zeros_like(taken)], axis=1)
        under = jnp.concatenate([jnp.zeros_like(taken), taken], axis=1)
        both = jnp.concatenate([beside, under], axis=0)
        weight_2[tap * 2 * v1 : (tap + 1) * 2 * v1] = both.T.astype(bf16)
        back_2[(8 - tap) * 2 * v1 : (9 - tap) * 2 * v1] = jnp.concatenate(
            [beside, jnp.zeros_like(beside)], axis=0
        ).astype(bf16)
        taken = third[tap * v1 : (tap + 1) * v1]
        weight_3[tap * 2 * v1 : (tap * 2 + 1) * v1] = jnp.concatenate([taken, zero_3], axis=1)
        weight_3[(tap * 2 + 1) * v1 : (tap * 2 + 2) * v1] = jnp.concatenate(
            [zero_3, taken], axis=1
        )
        turned = jnp.concatenate([taken, zero_3], axis=0).astype(f32).T
        back_3[(8 - tap) * v2 : (9 - tap) * v2] = turned.astype(bf16)


def perceptual_kernel(shape, sources, paired, *refs):
    received = refs[:sources]
    (
        vgg_first, vgg_second, vgg_third, pixels,
        weight_1, weight_2, weight_3, back_3, back_2, back_1, shown, grads,
        target, strips, lines, wide_1, narrow_1, wide_3, narrow_3, wide_g, narrow_g,
        plane_1, plane_2, spread, wide_b, narrow_b, wide_a, narrow_a,
    ) = refs[sources:]
    rows, cols, blocks, block_frames, own, parts, own_slots, frames_own, pack = shape
    f32, bf16 = jnp.float32, jnp.bfloat16
    half = parts * own_slots
    groups, group = lax.axis_size("grp"), lax.axis_index("grp")
    col_parts = lax.axis_size("col")
    width = cols * col_parts
    height = rows * lax.axis_size("row")
    view_rows, view_cols = min(height, rows + 20), min(width, cols + 20)
    top, left, view_top, view_left = corner(rows, cols)
    number = view_rows // parts
    count = view_cols * half
    lanes = lines.shape[2]
    span = width * half
    v1 = weight_2.shape[1] // 2
    v2 = weight_3.shape[1] // 2
    body = pl.ds(3 * half, count)
    plane_weights(
        vgg_first, vgg_second, vgg_third, weight_1, weight_2, weight_3, back_3, back_2, back_1
    )

    place = lax.axis_index("row") * col_parts + lax.axis_index("col")
    for at in range(shown.shape[0]):
        per_source = received[0].shape[0]
        device = place ^ at if paired else at
        arrived = received[at // per_source][at % per_source].astype(f32)
        target[device] = arrived[3 * rows :]
        shown[device] = jnp.zeros(shown.shape[1:], f32)
        for k in range(3):
            shown.at[device][pl.ds(k, rows, stride=8)] = arrived[k * rows : (k + 1) * rows]
    strips[...] = jnp.zeros(strips.shape, f32)
    for j in range(frames_own):
        frame = groups * j + group
        block, rest = frame // block_frames, frame % block_frames
        for part in range(parts):
            for k in range(3):
                short = rows // pack
                start = ((k * blocks + block) * own + rest % own) * short

                def take(at, j=j, part=part, k=k, start=start, rest=rest):
                    row = view_top + part * number + at
                    device = (row // rows) * col_parts + rest // own
                    strips[j * parts + part, pl.ds(at * 8 + 3 + k, 1)] = target[
                        device, pl.ds(start + row % rows, 1)
                    ]

                if parts > 1:
                    device = part * col_parts + rest // own
                    value = target[device, pl.ds(start, short)]
                    for turn in range(pack):
                        strips[j * parts + part, pl.ds(3 + k + turn * short * 8, short, stride=8)] = (
                            pltpu.roll(value, (pack - turn) * width % value.shape[1], 1)
                        )
                else:
                    repeat(number, take)
    from_col = lax.broadcasted_iota(jnp.int32, (target.shape[2], lanes), 0) - view_left
    to_lane = lax.broadcasted_iota(jnp.int32, (target.shape[2], lanes), 1)
    guide = 0.0
    for j in range(frames_own):
        for part in range(parts):
            place = (from_col * half + (j * parts + part) == to_lane) & (to_lane < count)
            guide = guide + matmul(
                strips[j * parts + part].astype(bf16),
                jnp.where(place, 1.0, 0.0).astype(bf16),
            )
    lane = lax.broadcasted_iota(jnp.int32, (8, lanes), 1)
    strips_line = lines.at[pl.ds(1, number)]
    for at in range(number):
        strips_line[at, pl.ds(8, 8)] = guide[at * 8 : at * 8 + 8]

    def line_step(at):
        line = 0.0
        for part in range(parts):
            row = view_top + part * number + at
            source = pl.ds(pl.multiple_of(row % rows * 8, 8), 8)
            line = line + jnp.concatenate(
                [
                    shown[(row // rows) * col_parts + k, source][:, : cols * half]
                    for k in range(col_parts)
                ],
                axis=1,
            )
        line = pltpu.roll(line, lax.rem(span - view_left * half, span), 1)[:, :lanes]
        line = jnp.where(lane < count, line, 0.0) + lines[at + 1, pl.ds(8, 8)]
        before = jnp.where(lane < half, 0.0, pltpu.roll(line, half, 1))
        after = jnp.where(lane >= count - half, 0.0, pltpu.roll(line, lanes - half, 1))
        lines[at + 1] = jnp.concatenate([before, line, after], axis=0)

    repeat(number, line_step, unrolled(number))
    wide_lane = lax.broadcasted_iota(jnp.int32, (24, lanes), 1)
    if parts > 1:
        part = wide_lane % parts
        inside = wide_lane < count
        low = pltpu.roll(lines[number], 1, 1)
        high = pltpu.roll(lines[1], lanes - 1, 1)
        lines[0] = jnp.where((part > 0) & inside, low, 0.0)
        lines[number + 1] = jnp.where((part < parts - 1) & inside, high, 0.0)
    else:
        lines[0] = jnp.zeros((24, lanes), f32)
        lines[number + 1] = jnp.zeros((24, lanes), f32)

    def first_step(at):
        pieces = [lines[at], lines[at + 1], lines[at + 2], jnp.zeros((56, lanes), f32)]
        patches = jnp.concatenate(pieces, axis=0).T[:count].astype(bf16)
        z = matmul(patches, weight_1[...].astype(bf16))
        plane_1[at, body] = z
        store_wide(wide_1, narrow_1, at + 1, 0.5 * z * (1.0 + gelu_tanh(z)), half)

    repeat(number, first_step, unrolled(number))
    fill_edges(parts, wide_1, narrow_1)

    def second_step(q):
        total = 0.0
        for step in range(2):
            at = 2 * q + step
            z = matmul(plane_slabs(wide_1, narrow_1, at, count, half), weight_2[...])
            plane_2[at, body] = z
            total = total + 0.5 * z * (1.0 + gelu_tanh(z))
        pooled = total.reshape(view_cols // 2, 2, half, 2 * v1)
        pooled = 0.25 * (pooled[:, 0] + pooled[:, 1])
        store_wide(wide_3, narrow_3, q + 1, pooled.reshape(count // 2, 2 * v1), half)

    repeat(number // 2, second_step, unrolled(number // 2))
    fill_edges(parts, wide_3, narrow_3)

    def third_step(q):
        z = matmul(plane_slabs(wide_3, narrow_3, q, count // 2, half), weight_3[...])
        t = gelu_tanh(z)
        value = 0.5 * z * (1.0 + t)
        delta = (64.0 / v2) * (value[:, :v2] - value[:, v2:]) * gelu_slope(z[:, :v2], t[:, :v2])
        store_wide(wide_g, narrow_g, q + 1, delta, half)

    repeat(number // 2, third_step, unrolled(number // 2))
    fill_edges(parts, wide_g, narrow_g)

    def pool_step(q):
        grad = 0.25 * matmul(plane_slabs(wide_g, narrow_g, q, count // 2, half), back_3[...])
        grad = grad.reshape(view_cols // 2, 1, half, 2 * v1)
        spread[q, body] = jnp.concatenate([grad, grad], axis=1).reshape(count, 2 * v1)

    repeat(number // 2, pool_step, unrolled(number // 2))

    def near(reach):
        size = (cols + 2 * reach) * half
        keep = col_mask(left - reach, cols + 2 * reach, width, half, half)
        start = pl.multiple_of((left - view_left + 3 - reach) * half, 8)
        return keep, pl.ds(start, size), size

    def second_delta(at):
        keep, where, _ = near(3)
        z = plane_2[at, where]
        t = gelu_tanh(z)
        value = 0.5 * z * (1.0 + t)
        delta = spread[at // 2, where] + (16.0 / v1) * (value - pltpu.roll(value, v1, 1))
        store_slab(wide_b, narrow_b, at + 1, jnp.where(keep, delta * gelu_slope(z, t), 0.0), half)

    repeat(number, second_delta, unrolled(number))
    fill_edges(parts, wide_b, narrow_b)

    def first_delta(at):
        keep, where, size = near(2)
        grad = matmul(plane_slabs(wide_b, narrow_b, at, size, half), back_2[...])
        z = plane_1[at, where]
        delta = jnp.where(keep, grad * gelu_slope(z, gelu_tanh(z)), 0.0)
        store_slab(wide_a, narrow_a, at + 1, delta, half)

    repeat(number, first_delta, unrolled(number))
    fill_edges(parts, wide_a, narrow_a)

    def pixel_step(at):
        size = (cols + 2) * half
        grad = lax.dot_general(
            back_1[...].astype(bf16), plane_slabs(wide_a, narrow_a, at, size, half), (((1,), (1,)), ((), ())),
            preferred_element_type=f32,
        )
        line = lines[at + 1, pl.ds(8, 8)]
        line = line - pltpu.roll(line, 5, 0)
        shift = lax.rem((view_left - left + 1) * half + 2 * lanes, lanes)
        line = pltpu.roll(line, shift, 1)
        grad = grad + (1.0 / 6.0) * line[:, :size]
        for k in range(3):
            grads[pl.ds(k * number + at, 1)] = grad[k : k + 1]

    repeat(number, pixel_step, unrolled(number))
    for k in range(3):
        pixels[k] = grads[k * number : (k + 1) * number].astype(bf16)


def gradient_taps(source, delta, shifted, sums, first_tap):
    rows = delta.shape[0]
    slots, channels = source.shape[-2:]
    cols = source.shape[1] - 2
    count = cols * slots

    def turn(r):
        block = delta[r].astype(jnp.float32)
        for dt in range(3):
            moved = block if dt == 1 else pltpu.roll(block, (dt - 1) % count, 0)
            shifted[dt, r] = moved.T.astype(jnp.bfloat16)

    repeat(rows, turn, rows)

    def tap_step(step):
        tap = jnp.minimum(first_tap + step, 26)
        dt, dr, dc = tap // 9, tap // 3 % 3, tap % 3
        total = 0.0
        for r in range(rows):
            slab = source[r + dr, pl.ds(dc, cols)].reshape(count, channels)
            total = total + matmul(shifted[dt, r], slab)
        sums[pl.ds(pl.multiple_of(step * channels, channels), channels)] = total.T

    repeat(sums.shape[0] // channels, tap_step, 8)


def backward_kernel(*refs, parts, out_rows, groups, outs):
    pixels = refs[:groups]
    (
        rgb, conv_second, first_in, second_in, cells_in, hidden_in,
    ) = refs[groups : groups + 6]
    terms = refs[groups + 6 : groups + 6 + outs]
    (
        slope_first, slope_second, cells, hidden, weight, back_second, paint, shown,
        painted, hidden_grad, delta_second, delta_own, shifted, sums, sems,
    ) = refs[groups + 6 + outs :]
    copies = [
        pltpu.make_async_copy(second_in, slope_second, sems.at[0]),
        pltpu.make_async_copy(hidden_in, hidden, sems.at[1]),
        pltpu.make_async_copy(conv_second, weight, sems.at[2]),
        pltpu.make_async_copy(first_in, slope_first, sems.at[3]),
        pltpu.make_async_copy(cells_in, cells, sems.at[4]),
    ]
    for copy in copies:
        copy.start()
    slots, channels = cells.shape[-2:]
    rows, cols = cells.shape[0] - 2, cells.shape[1] - 2
    height = rows * lax.axis_size("row")
    view_rows = min(height, rows + 20)
    number = view_rows // parts
    own_slots = slots // groups
    group = lax.axis_index("grp")
    top, _, view_top, _ = corner(rows, cols)
    kept = (cols + 2) * own_slots
    paint[...] = jnp.zeros(paint.shape, jnp.float32)
    paint[0:3] = rgb[...].astype(jnp.float32)
    shown[...] = jnp.zeros(shown.shape, jnp.float32)
    for step in range(groups):
        for k in range(3):
            value = pixels[step][k].astype(jnp.float32)
            for at in range(number):
                shown[step, at * 8 + k : at * 8 + k + 1] = value[at : at + 1]

    def paint_step(at):
        for step in range(groups):
            source = partner(group, step, groups)
            slot = painted.at[at, step]
            slot[...] = lax.dot_general(
                shown[step, pl.ds(pl.multiple_of(at * 8, 8), 8)].astype(jnp.bfloat16),
                paint[...].astype(jnp.bfloat16),
                (((0,), (0,)), ((), ())),
                preferred_element_type=jnp.float32,
            )
            for part in range(parts):
                row = kept_row(view_top + part * number + at, top - 1, rows + 2)
                value = slot[pl.ds(part, kept, stride=parts)] if parts > 1 else slot[...]
                hidden_grad[row, pl.ds(source, kept, stride=groups)] = value

    repeat(number, paint_step, unrolled(number))
    copies[0].wait()

    def delta_step(a):
        row = top - 1 + a
        inside = (row >= 0) & (row < height)
        delta = jnp.where(inside, hidden_grad[a + 1] * slope_second[a], 0.0).astype(jnp.bfloat16)
        delta_second[a] = delta.reshape(cols + 2, slots, channels)

    repeat(rows + 2, delta_step, 5)

    first_row = lax.axis_index("grp") * out_rows
    first_tap = first_row // channels
    skip = pl.multiple_of(first_row - first_tap * channels, 32)
    device = lax.axis_index("row") * lax.axis_size("col") + lax.axis_index("col")

    def put(which):
        value = sums[pl.ds(skip, out_rows)]
        if len(terms[0].shape) == 3:
            terms[0][which] = value.astype(jnp.bfloat16)
            return
        chunks, _, size, _ = terms[0].shape
        chunks = chunks * outs
        for k in range(chunks):
            piece = value[k * size : (k + 1) * size].astype(jnp.bfloat16)
            if chunks & (chunks - 1):
                terms[0][lax.rem(k - device + chunks, chunks), which] = piece
            elif outs == 1:
                terms[0][device ^ k, which] = piece
            else:
                at = device ^ k

                @pl.when(at % 2 == 0)
                def _():
                    terms[0][at // 2, which] = piece

                @pl.when(at % 2 == 1)
                def _():
                    terms[1][at // 2, which] = piece

    def own_step(r):
        delta_own[r] = delta_second[r + 1, 1 : 1 + cols].reshape(cols * slots, channels)

    repeat(rows, own_step, rows)
    copies[1].wait()
    gradient_taps(hidden, delta_own, shifted, sums, first_tap)
    put(1)

    copies[2].wait()
    copies[3].wait()
    copies[4].wait()
    for dt in range(3):
        for tap in range(9):
            at = (dt * 9 + tap) * channels
            turned = weight[at : at + channels].astype(jnp.float32).T.astype(jnp.bfloat16)
            back_second[
                (8 - tap) * channels : (9 - tap) * channels,
                (2 - dt) * channels : (3 - dt) * channels,
            ] = turned

    def back_row(r, back):
        delta_own[r] = (back * slope_first[r]).astype(jnp.bfloat16)

    conv_pairs(delta_second, rows, cols, back_second, back_row)
    gradient_taps(cells, delta_own, shifted, sums, first_tap)
    put(0)


def call(kernel, outs, scratch, sems, limit, hbm_in=(), hbm_out=(), operands=0, flops=0):
    def spec(at, chosen):
        return pl.BlockSpec(memory_space=pltpu.HBM if at in chosen else pltpu.VMEM)

    scratch = [pltpu.VMEM(*shape) for shape in scratch]
    if sems:
        scratch.append(pltpu.SemaphoreType.DMA((sems,)))
    several = isinstance(outs, tuple)
    return pl.pallas_call(
        kernel,
        out_shape=outs,
        in_specs=[spec(k, hbm_in) for k in range(operands)],
        out_specs=tuple(spec(k, hbm_out) for k in range(len(outs))) if several else spec(0, hbm_out),
        scratch_shapes=scratch,
        compiler_params=pltpu.CompilerParams(vmem_limit_bytes=limit * 2**20),
        cost_estimate=pl.CostEstimate(flops=flops, bytes_accessed=2**20, transcendentals=0),
    )


def partners(step, count):
    if count & (count - 1):
        return [(i, (i + step) % count) for i in range(count)]
    return [(i, i ^ step) for i in range(count)]


def partner(index, step, count):
    if count & (count - 1):
        return lax.rem(index - step + count, count)
    return index ^ step


def matchings(axis):
    count = lax.axis_size(axis)
    pairs = []
    for first in range(2 if count > 2 else 1):
        pairs.append([(i, i + 1) for i in range(first, count - 1, 2)])
    return pairs


def exchange_pieces(field, width):
    row_pairs, col_pairs = matchings("row"), matchings("col")
    col_count = lax.axis_size("col")
    rows, cols = field.shape[1:3]
    pieces = []
    for row_at in (None, *range(len(row_pairs))):
        for col_at in (None, *range(len(col_pairs))):
            if row_at is None and col_at is None:
                continue
            edge, moves = field, []
            for axis, dim, at, length in (("row", 1, row_at, rows), ("col", 2, col_at, cols)):
                if at is not None:
                    after = (lax.axis_index(axis) % 2 == at).astype(jnp.int32)
                    edge = lax.dynamic_slice_in_dim(edge, after * (length - width), width, axis=dim)
            row_moves = [(i, i) for i in range(lax.axis_size("row"))]
            col_moves = [(i, i) for i in range(col_count)]
            if row_at is not None:
                row_moves = [pair for a, b in row_pairs[row_at] for pair in ((a, b), (b, a))]
            if col_at is not None:
                col_moves = [pair for a, b in col_pairs[col_at] for pair in ((a, b), (b, a))]
            moves = [
                (a * col_count + c, b * col_count + d) for a, b in row_moves for c, d in col_moves
            ]
            pieces.append(((row_at, col_at), edge, moves))
    return pieces


def packed_edge(place, edge):
    row_at, col_at = place
    if row_at is None:
        return jnp.swapaxes(edge, 1, 2)
    if col_at is None:
        return edge
    return edge.reshape(-1, edge.shape[3])


def slotted(field, slots):
    field = jnp.transpose(field, (1, 2, 0, 3))
    return jnp.pad(field, ((0, 0), (0, 0), (0, slots - field.shape[2]), (0, 0)))


def local(dec_input, target, conv_first, conv_second, rgb_weight, vgg_first, vgg_second, vgg_third):
    f32, bf16 = jnp.float32, jnp.bfloat16
    row_count, col_count = lax.axis_size("row"), lax.axis_size("col")
    groups, devices = lax.axis_size("grp"), row_count * col_count
    blocks, block_frames, rows, cols, channels = dec_input.shape
    frames = blocks * block_frames
    frames_own = frames // groups
    parts, own_slots = split(rows, frames_own)
    slots = own_slots * groups
    half = parts * own_slots
    height, width = rows * row_count, cols * col_count
    view_rows, view_cols = min(height, rows + 20), min(width, cols + 20)
    number, count = view_rows // parts, view_cols * half
    lanes = -(-count // 128) * 128
    v1, v2 = vgg_first.shape[1], vgg_third.shape[1]

    raw = dec_input.reshape(frames, rows, cols, channels)
    pieces = exchange_pieces(raw, 3)
    places = tuple(place for place, _, _ in pieces)
    near = [
        lax.ppermute(packed_edge(place, edge), plane, moves) for place, edge, moves in pieces
    ]
    own = slotted(raw, slots)

    line = max(cols * half, -(-width // 128) * 128)
    pack = line // width if parts > 1 and rows % (line // width) == 0 else 1
    target_rows = 3 * blocks * target.shape[2] * rows // pack
    size = -(-(3 * rows + target_rows) // 16) * 16
    big = 16 if parts > 1 else 40

    cells, hidden, slope_first, slope_second, payload = call(
        functools.partial(forward_kernel, frames, parts, pack, places),
        (
            pltpu.HBM((rows + 2, cols + 2, slots, channels), bf16),
            pltpu.HBM((rows + 2, cols + 2, slots, channels), bf16),
            pltpu.HBM((rows, cols * slots, channels), f32),
            pltpu.HBM((rows + 2, (cols + 2) * slots, channels), f32),
            jax.ShapeDtypeStruct((size, line), bf16),
        ),
        [
            ((rows + 6, cols + 6, slots, channels), bf16),
            ((rows + 4, cols + 4, slots, channels), bf16),
            ((rows, cols * slots, channels), f32),
            ((rows + 2, (cols + 2) * slots, channels), f32),
            ((9 * channels, 3 * channels), bf16),
            ((rows + 2, cols * slots, channels), f32),
            ((rows + 2, cols * half, channels), f32),
            (((rows + 2) * 8, cols * half), f32),
            ((8, channels), f32),
            ((3 * max(rows, cols) * slots, channels), f32),
            ((9 * frames, channels), f32),
        ],
        4,
        big,
        hbm_out=(0, 1, 2, 3),
        operands=5 + len(near),
        flops=2**33,
    )(own, *near, conv_first, conv_second, rgb_weight, target)

    paired = devices == 8 and col_count % 2 == 0
    if paired:
        other = lax.ppermute(payload, plane, [(i, i ^ 1) for i in range(devices)])
        both = jnp.stack([payload, other])
        received = [both] + [
            lax.ppermute(both, plane, [(i, i ^ step) for i in range(devices)])
            for step in range(2, devices, 2)
        ]
    else:
        received = [
            lax.all_to_all(
                jnp.broadcast_to(payload[None], (devices,) + payload.shape),
                plane,
                split_axis=0,
                concat_axis=0,
                tiled=True,
            )
        ]

    wide_count = count + 6 * half
    pixels = call(
        functools.partial(
            perceptual_kernel,
            (
                rows, cols, blocks, block_frames, target.shape[2], parts, own_slots, frames_own,
                pack,
            ),
            len(received),
            paired,
        ),
        jax.ShapeDtypeStruct((3, number, (cols + 2) * half), bf16),
        [
            ((128, 2 * v1), f32),
            ((18 * v1, 2 * v1), bf16),
            ((18 * v1, 2 * v2), bf16),
            ((9 * v2, 2 * v1), bf16),
            ((18 * v1, 2 * v1), bf16),
            ((8, 18 * v1), f32),
            ((devices, rows * 8, line), f32),
            ((number * 3, (cols + 2) * half), f32),
            ((devices, size - 3 * rows, line), f32),
            ((frames_own * parts, number * 8, line), f32),
            ((number + 2, 24, lanes), f32),
            ((number + 2, count + 2 * half, 2 * v1), bf16),
            ((number + 2, count, 2 * v1), bf16),
            ((number // 2 + 2, count // 2 + 2 * half, 2 * v1), bf16),
            ((number // 2 + 2, count // 2, 2 * v1), bf16),
            ((number // 2 + 2, count // 2 + 2 * half, v2), bf16),
            ((number // 2 + 2, count // 2, v2), bf16),
            ((number, wide_count, 2 * v1), f32),
            ((number, wide_count, 2 * v1), f32),
            ((number // 2, wide_count, 2 * v1), f32),
            ((number + 2, (cols + 6) * half, 2 * v1), bf16),
            ((number + 2, (cols + 4) * half, 2 * v1), bf16),
            ((number + 2, (cols + 4) * half, 2 * v1), bf16),
            ((number + 2, (cols + 2) * half, 2 * v1), bf16),
        ],
        0,
        big,
        operands=3 + len(received),
        flops=2**32,
    )(*received, vgg_first, vgg_second.T, vgg_third)

    gathered = [pixels]
    for step in range(1, groups):
        gathered.append(lax.ppermute(pixels, "grp", partners(step, groups)))

    out_rows = conv_first.shape[0] // groups
    taps = max(
        -(-(g + 1) * out_rows // channels) - g * out_rows // channels for g in range(groups)
    )
    even = out_rows % devices == 0
    out_shape = jax.ShapeDtypeStruct((2, out_rows, channels), bf16)
    if even:
        count_out = devices // 2 if paired else devices
        out_shape = jax.ShapeDtypeStruct((count_out, 2, out_rows // devices, channels), bf16)
    if even and paired:
        out_shape = (out_shape, out_shape)
    terms = call(
        functools.partial(
            backward_kernel, parts=parts, out_rows=out_rows, groups=groups,
            outs=2 if even and paired else 1,
        ),
        out_shape,
        [
            ((rows, cols * slots, channels), f32),
            ((rows + 2, (cols + 2) * slots, channels), f32),
            ((rows + 2, cols + 2, slots, channels), bf16),
            ((rows + 2, cols + 2, slots, channels), bf16),
            (conv_second.shape, bf16),
            ((9 * channels, 3 * channels), bf16),
            ((8, channels), f32),
            ((groups, number * 8, (cols + 2) * half), f32),
            ((number, groups, (cols + 2) * half, channels), f32),
            ((rows + 4, (cols + 2) * slots, channels), f32),
            ((rows + 2, cols + 2, slots, channels), bf16),
            ((rows, cols * slots, channels), bf16),
            ((3, rows, channels, cols * slots), bf16),
            ((taps * channels, channels), f32),
        ],
        5,
        big + 8,
        hbm_in=tuple(range(groups + 1, groups + 6)),
        operands=groups + 6,
        flops=2**32,
    )(
        *gathered, rgb_weight, conv_second, slope_first, slope_second, cells, hidden,
    )

    if even and paired:
        kept, given = terms
        came = lax.ppermute(given, plane, partners(1, devices))
        halves = [kept[k].astype(f32) + came[k].astype(f32) for k in range(devices // 2)]
        total = halves[0]
        for k in range(1, devices // 2):
            half_sum = lax.ppermute(halves[k].astype(bf16), plane, partners(2 * k, devices))
            total = total + half_sum.astype(f32)
    elif even:
        pieces = [terms[0]]
        for step in range(1, devices):
            pieces.append(lax.ppermute(terms[step], plane, partners(step, devices)))
        total = sum(piece.astype(f32) for piece in pieces)
    else:
        pieces = jnp.swapaxes(terms.reshape(2, devices, -1), 0, 1)
        pieces = lax.all_to_all(pieces, plane, split_axis=0, concat_axis=0, tiled=True)
        total = jnp.sum(pieces.astype(f32), axis=0)
    return total[0].reshape(-1), total[1].reshape(-1)


def solution(mesh):
    in_specs = (
        P(None, None, "row", "col", None),
        P(None, None, "col", "row", None),
        P(),
        P(),
        P(),
        P(),
        P(),
        P(),
    )
    out_specs = (P(("grp", "row", "col")), P(("grp", "row", "col")))
    return jax.shard_map(local, mesh=mesh, in_specs=in_specs, out_specs=out_specs, check_vma=False)
```

```python
import functools

import jax
import jax.numpy as jnp
from jax import lax
from jax.experimental import pallas as pl
from jax.experimental.pallas import tpu as pltpu
from jax.sharding import PartitionSpec as P

gelu_scale = 0.7978845608028654
gelu_cubic = 0.044715
plane = ("row", "col")


def repeat(count, body, unroll=1):
    lax.fori_loop(0, count, lambda i, carry: (body(i), carry)[1], 0, unroll=unroll)


def matmul(left, right):
    return jnp.dot(left, right, preferred_element_type=jnp.float32)


def gelu_tanh(z):
    return jnp.tanh(gelu_scale * (z + gelu_cubic * z * z * z))


def gelu_slope(z, t):
    return 0.5 * (1.0 + t) + 0.5 * z * (1.0 - t * t) * gelu_scale * (
        1.0 + 3.0 * gelu_cubic * z * z
    )


def split(rows, frames_own):
    small = frames_own <= 4 and lax.axis_size("row") == 2 and rows % 4 == 0
    return (2, 4) if small else (1, 8)


def corner(rows, cols):
    height, width = rows * lax.axis_size("row"), cols * lax.axis_size("col")
    view_rows, view_cols = min(height, rows + 20), min(width, cols + 20)
    top, left = lax.axis_index("row") * rows, lax.axis_index("col") * cols
    view_top = jnp.clip(top - 10, 0, height - view_rows)
    view_left = jnp.clip(left - 10, 0, width - view_cols)
    return top, left, view_top, view_left


def col_mask(first_col, cols, width, slots, frames):
    at = lax.broadcasted_iota(jnp.int32, (cols * slots, 1), 0)
    col = at // slots + first_col
    return (at % slots < frames) & (col >= 0) & (col < width)


def frame_weight(ref):
    third = ref.shape[0] // 3
    return jnp.concatenate([ref[pl.ds(third * k, third)] for k in range(3)], axis=1)


def conv_pairs(source, rows, cols, weight, use):
    slots, channels = source.shape[-2:]
    count = cols * slots

    def step(q):
        slabs = [
            source[pl.ds(2 * q + dr, 2), pl.ds(dc, cols)].reshape(2 * count, channels)
            for dr in range(3)
            for dc in range(3)
        ]
        sums = matmul(jnp.concatenate(slabs, axis=1), weight[...])
        total = (
            pltpu.roll(sums[:, :channels], 1, 0)
            + sums[:, channels : 2 * channels]
            + pltpu.roll(sums[:, 2 * channels :], 2 * count - 1, 0)
        )
        for k in range(2):
            use(2 * q + k, total[k * count : (k + 1) * count])

    repeat(rows // 2, step, rows // 2)


def forward_kernel(frames, parts, pack, places, own, *refs):
    near = refs[: len(places)]
    (
        first, second, rgb, target, cells_out, hidden_out, first_out, second_out, payload,
        cells, hidden, slope_first, slope_second, spread_weight, picked, spaced, colour, project,
        sems,
    ) = refs[len(places) :]
    rows, cols, slots, channels = own.shape
    f32, bf16 = jnp.float32, jnp.bfloat16
    groups, group = lax.axis_size("grp"), lax.axis_index("grp")
    height, width = rows * lax.axis_size("row"), cols * lax.axis_size("col")
    top, left_col = lax.axis_index("row") * rows, lax.axis_index("col") * cols
    cells[3 : 3 + rows, 3 : 3 + cols] = own[...]
    if lax.axis_size("row") == 2:
        start = jnp.where(lax.axis_index("row") == 0, 0, 3 + rows)
        cells[pl.ds(start, 3)] = jnp.zeros((3,) + cells.shape[1:], bf16)
    if lax.axis_size("col") == 2:
        start = jnp.where(lax.axis_index("col") == 0, 0, 3 + cols)
        cells[:, pl.ds(start, 3)] = jnp.zeros((rows + 6, 3) + cells.shape[2:], bf16)
    for (row_at, col_at), piece in zip(places, near):
        row, col = 3, 3
        if row_at is not None:
            row = jnp.where(lax.axis_index("row") % 2 == row_at, 3 + rows, 0)
        if col_at is not None:
            col = jnp.where(lax.axis_index("col") % 2 == col_at, 3 + cols, 0)
        cells[pl.ds(row, piece.shape[0]), pl.ds(col, piece.shape[1])] = piece[...]
    copies = [
        pltpu.make_async_copy(
            cells.at[pl.ds(2, rows + 2), pl.ds(2, cols + 2)], cells_out, sems.at[0]
        ),
        pltpu.make_async_copy(
            hidden.at[pl.ds(1, rows + 2), pl.ds(1, cols + 2)], hidden_out, sems.at[1]
        ),
        pltpu.make_async_copy(slope_first, first_out, sems.at[2]),
        pltpu.make_async_copy(slope_second, second_out, sems.at[3]),
    ]
    copies[0].start()
    spread_weight[...] = frame_weight(first)

    def first_layer(r, pre):
        row = top - 2 + r
        keep = col_mask(left_col - 2, cols + 4, width, slots, frames) & (
            (row >= 0) & (row < height)
        )
        gate = 0.5 + 0.5 * jnp.tanh(0.5 * pre)
        out = jnp.where(keep, pre * gate, 0.0).astype(bf16)
        hidden[r] = out.reshape(cols + 4, slots, channels)
        slope = jnp.where(keep, gate * (1.0 + pre * (1.0 - gate)), 0.0)

        @pl.when((r >= 2) & (r < 2 + rows))
        def _():
            slope_first[r - 2] = slope[2 * slots : (2 + cols) * slots]

    conv_pairs(cells, rows + 4, cols + 4, spread_weight, first_layer)
    copies[1].start()
    copies[2].start()
    spread_weight[...] = frame_weight(second)
    own_slots = slots // groups
    spaced[...] = jnp.zeros(spaced.shape, f32)
    project[...] = jnp.zeros(project.shape, f32)
    project[0:3] = rgb[...].astype(f32)

    def second_layer(r, pre):
        row = top - 1 + r
        keep = col_mask(left_col - 1, cols + 2, width, slots, frames) & (
            (row >= 0) & (row < height)
        )
        gate = 0.5 + 0.5 * jnp.tanh(0.5 * pre)
        slope_second[r] = jnp.where(keep, gate * (1.0 + pre * (1.0 - gate)), 0.0)
        picked[r] = jnp.where(keep, pre * gate, 0.0)[slots : (1 + cols) * slots]
        mine = picked.at[r][pl.ds(group, cols * own_slots, stride=groups)]
        if parts > 1:
            part = lax.axis_index("row")
            spaced.at[r][pl.ds(part, cols * own_slots, stride=parts)] = mine
            mine = spaced[r]
        line = lax.dot_general(
            project[...].astype(bf16), mine.astype(bf16), (((1,), (1,)), ((), ())),
            preferred_element_type=f32,
        )
        at = jnp.clip(r - 1, -1, rows) + 1
        colour[pl.ds(pl.multiple_of(at * 8, 8), 8)] = line

    conv_pairs(hidden, rows + 2, cols + 2, spread_weight, second_layer)
    copies[3].start()
    size, line = payload.shape
    pieces = [colour[pl.ds(8 + k, rows, stride=8)] for k in range(3)]
    goal = target[...].reshape(-1, rows, width).astype(f32)
    if pack > 1:
        short = rows // pack
        goal = jnp.concatenate([goal[:, k * short : (k + 1) * short] for k in range(pack)], axis=2)
    goal = goal.reshape(-1, pack * width)
    if pack * width < line:
        goal = jnp.concatenate(
            [goal, jnp.zeros((goal.shape[0], line - pack * width), f32)], axis=1
        )
    pieces.append(goal)
    filled = 3 * rows + goal.shape[0]
    if filled < size:
        pieces.append(jnp.zeros((size - filled, line), f32))
    lines = jnp.concatenate(pieces, axis=0).astype(bf16)
    payload[...] = lines
    for copy in copies:
        copy.wait()


def plane_slabs(wide, narrow, row, count, half):
    pieces = []
    for dr in range(3):
        pieces.append(wide[row + dr, pl.ds(0, count)])
        pieces.append(narrow[row + dr])
        pieces.append(wide[row + dr, pl.ds(2 * half, count)])
    return jnp.concatenate(pieces, axis=1)


def store_slab(wide, narrow, row, value, half):
    wide[row] = value.astype(jnp.bfloat16)
    narrow[row] = value[half : value.shape[0] - half].astype(jnp.bfloat16)


def store_wide(wide, narrow, row, value, half):
    edge = jnp.zeros((half, value.shape[1]), jnp.float32)
    store_slab(wide, narrow, row, jnp.concatenate([edge, value, edge], axis=0), half)


def fill_edges(parts, *refs):
    for ref in refs:
        last = ref.shape[0] - 1
        if parts == 1:
            for at in (0, last):
                ref[at] = jnp.zeros(ref.shape[1:], ref.dtype)
            continue
        part = lax.broadcasted_iota(jnp.int32, (ref.shape[1], 1), 0) % parts
        low = pltpu.roll(ref[last - 1].astype(jnp.float32), 1, 0)
        high = pltpu.roll(ref[1].astype(jnp.float32), ref.shape[1] - 1, 0)
        ref[0] = jnp.where(part > 0, low, 0.0).astype(ref.dtype)
        ref[last] = jnp.where(part < parts - 1, high, 0.0).astype(ref.dtype)


def kept_row(row, first, number):
    return jnp.clip(row - first, -1, number) + 1


def unrolled(number):
    return number if number <= 8 else 4 if number % 4 == 0 else 2


def plane_weights(
    first, second, third, weight_1, weight_2, weight_3, back_3, back_2, back_1
):
    f32, bf16 = jnp.float32, jnp.bfloat16
    v1, v2 = second.shape[0], third.shape[1]
    zero_3 = jnp.zeros((v1, v2), bf16)
    weight_1[...] = jnp.zeros(weight_1.shape, f32)
    back_1[...] = jnp.zeros(back_1.shape, f32)
    for tap in range(9):
        taken = first[...].astype(f32)[tap * 3 : tap * 3 + 3]
        weight_1[tap * 8 : tap * 8 + 3, 0:v1] = taken
        weight_1[tap * 8 + 3 : tap * 8 + 6, v1 : 2 * v1] = taken
        back_1[0:3, (8 - tap) * 2 * v1 : (8 - tap) * 2 * v1 + v1] = taken
        taken = second[...].astype(f32)[:, tap * v1 : (tap + 1) * v1]
        beside = jnp.concatenate([taken, jnp.zeros_like(taken)], axis=1)
        under = jnp.concatenate([jnp.zeros_like(taken), taken], axis=1)
        both = jnp.concatenate([beside, under], axis=0)
        weight_2[tap * 2 * v1 : (tap + 1) * 2 * v1] = both.T.astype(bf16)
        back_2[(8 - tap) * 2 * v1 : (9 - tap) * 2 * v1] = jnp.concatenate(
            [beside, jnp.zeros_like(beside)], axis=0
        ).astype(bf16)
        taken = third[tap * v1 : (tap + 1) * v1]
        weight_3[tap * 2 * v1 : (tap * 2 + 1) * v1] = jnp.concatenate([taken, zero_3], axis=1)
        weight_3[(tap * 2 + 1) * v1 : (tap * 2 + 2) * v1] = jnp.concatenate(
            [zero_3, taken], axis=1
        )
        turned = jnp.concatenate([taken, zero_3], axis=0).astype(f32).T
        back_3[(8 - tap) * v2 : (9 - tap) * v2] = turned.astype(bf16)


def perceptual_kernel(shape, sources, paired, *refs):
    received = refs[:sources]
    (
        vgg_first, vgg_second, vgg_third, pixels,
        weight_1, weight_2, weight_3, back_3, back_2, back_1, shown, grads,
        target, strips, lines, wide_1, narrow_1, wide_3, narrow_3, wide_g, narrow_g,
        plane_1, plane_2, spread, wide_b, narrow_b, wide_a, narrow_a,
    ) = refs[sources:]
    rows, cols, blocks, block_frames, own, parts, own_slots, frames_own, pack = shape
    f32, bf16 = jnp.float32, jnp.bfloat16
    half = parts * own_slots
    groups, group = lax.axis_size("grp"), lax.axis_index("grp")
    col_parts = lax.axis_size("col")
    width = cols * col_parts
    height = rows * lax.axis_size("row")
    view_rows, view_cols = min(height, rows + 20), min(width, cols + 20)
    top, left, view_top, view_left = corner(rows, cols)
    number = view_rows // parts
    count = view_cols * half
    lanes = lines.shape[2]
    span = width * half
    v1 = weight_2.shape[1] // 2
    v2 = weight_3.shape[1] // 2
    body = pl.ds(3 * half, count)
    plane_weights(
        vgg_first, vgg_second, vgg_third, weight_1, weight_2, weight_3, back_3, back_2, back_1
    )

    place = lax.axis_index("row") * col_parts + lax.axis_index("col")
    for at in range(shown.shape[0]):
        per_source = received[0].shape[0]
        device = place ^ at if paired else at
        arrived = received[at // per_source][at % per_source].astype(f32)
        target[device] = arrived[3 * rows :]
        shown[device] = jnp.zeros(shown.shape[1:], f32)
        for k in range(3):
            shown.at[device][pl.ds(k, rows, stride=8)] = arrived[k * rows : (k + 1) * rows]
    strips[...] = jnp.zeros(strips.shape, f32)
    for j in range(frames_own):
        frame = groups * j + group
        block, rest = frame // block_frames, frame % block_frames
        for part in range(parts):
            for k in range(3):
                short = rows // pack
                start = ((k * blocks + block) * own + rest % own) * short

                def take(at, j=j, part=part, k=k, start=start, rest=rest):
                    row = view_top + part * number + at
                    device = (row // rows) * col_parts + rest // own
                    strips[j * parts + part, pl.ds(at * 8 + 3 + k, 1)] = target[
                        device, pl.ds(start + row % rows, 1)
                    ]

                if parts > 1:
                    device = part * col_parts + rest // own
                    value = target[device, pl.ds(start, short)]
                    for turn in range(pack):
                        strips[j * parts + part, pl.ds(3 + k + turn * short * 8, short, stride=8)] = (
                            pltpu.roll(value, (pack - turn) * width % value.shape[1], 1)
                        )
                else:
                    repeat(number, take)
    from_col = lax.broadcasted_iota(jnp.int32, (target.shape[2], lanes), 0) - view_left
    to_lane = lax.broadcasted_iota(jnp.int32, (target.shape[2], lanes), 1)
    guide = 0.0
    for j in range(frames_own):
        for part in range(parts):
            place = (from_col * half + (j * parts + part) == to_lane) & (to_lane < count)
            guide = guide + matmul(
                strips[j * parts + part].astype(bf16),
                jnp.where(place, 1.0, 0.0).astype(bf16),
            )
    lane = lax.broadcasted_iota(jnp.int32, (8, lanes), 1)
    strips_line = lines.at[pl.ds(1, number)]
    for at in range(number):
        strips_line[at, pl.ds(8, 8)] = guide[at * 8 : at * 8 + 8]

    def line_step(at):
        line = 0.0
        for part in range(parts):
            row = view_top + part * number + at
            source = pl.ds(pl.multiple_of(row % rows * 8, 8), 8)
            line = line + jnp.concatenate(
                [
                    shown[(row // rows) * col_parts + k, source][:, : cols * half]
                    for k in range(col_parts)
                ],
                axis=1,
            )
        line = pltpu.roll(line, lax.rem(span - view_left * half, span), 1)[:, :lanes]
        line = jnp.where(lane < count, line, 0.0) + lines[at + 1, pl.ds(8, 8)]
        before = jnp.where(lane < half, 0.0, pltpu.roll(line, half, 1))
        after = jnp.where(lane >= count - half, 0.0, pltpu.roll(line, lanes - half, 1))
        lines[at + 1] = jnp.concatenate([before, line, after], axis=0)

    repeat(number, line_step, unrolled(number))
    wide_lane = lax.broadcasted_iota(jnp.int32, (24, lanes), 1)
    if parts > 1:
        part = wide_lane % parts
        inside = wide_lane < count
        low = pltpu.roll(lines[number], 1, 1)
        high = pltpu.roll(lines[1], lanes - 1, 1)
        lines[0] = jnp.where((part > 0) & inside, low, 0.0)
        lines[number + 1] = jnp.where((part < parts - 1) & inside, high, 0.0)
    else:
        lines[0] = jnp.zeros((24, lanes), f32)
        lines[number + 1] = jnp.zeros((24, lanes), f32)

    def first_step(at):
        pieces = [lines[at], lines[at + 1], lines[at + 2], jnp.zeros((56, lanes), f32)]
        patches = jnp.concatenate(pieces, axis=0).T[:count].astype(bf16)
        z = matmul(patches, weight_1[...].astype(bf16))
        plane_1[at, body] = z
        store_wide(wide_1, narrow_1, at + 1, 0.5 * z * (1.0 + gelu_tanh(z)), half)

    repeat(number, first_step, unrolled(number))
    fill_edges(parts, wide_1, narrow_1)

    def second_step(q):
        total = 0.0
        for step in range(2):
            at = 2 * q + step
            z = matmul(plane_slabs(wide_1, narrow_1, at, count, half), weight_2[...])
            plane_2[at, body] = z
            total = total + 0.5 * z * (1.0 + gelu_tanh(z))
        pooled = total.reshape(view_cols // 2, 2, half, 2 * v1)
        pooled = 0.25 * (pooled[:, 0] + pooled[:, 1])
        store_wide(wide_3, narrow_3, q + 1, pooled.reshape(count // 2, 2 * v1), half)

    repeat(number // 2, second_step, unrolled(number // 2))
    fill_edges(parts, wide_3, narrow_3)

    def third_step(q):
        z = matmul(plane_slabs(wide_3, narrow_3, q, count // 2, half), weight_3[...])
        t = gelu_tanh(z)
        value = 0.5 * z * (1.0 + t)
        delta = (64.0 / v2) * (value[:, :v2] - value[:, v2:]) * gelu_slope(z[:, :v2], t[:, :v2])
        store_wide(wide_g, narrow_g, q + 1, delta, half)

    repeat(number // 2, third_step, unrolled(number // 2))
    fill_edges(parts, wide_g, narrow_g)

    def pool_step(q):
        grad = 0.25 * matmul(plane_slabs(wide_g, narrow_g, q, count // 2, half), back_3[...])
        grad = grad.reshape(view_cols // 2, 1, half, 2 * v1)
        spread[q, body] = jnp.concatenate([grad, grad], axis=1).reshape(count, 2 * v1)

    repeat(number // 2, pool_step, unrolled(number // 2))

    def near(reach):
        size = (cols + 2 * reach) * half
        keep = col_mask(left - reach, cols + 2 * reach, width, half, half)
        start = pl.multiple_of((left - view_left + 3 - reach) * half, 8)
        return keep, pl.ds(start, size), size

    def second_delta(at):
        keep, where, _ = near(3)
        z = plane_2[at, where]
        t = gelu_tanh(z)
        value = 0.5 * z * (1.0 + t)
        delta = spread[at // 2, where] + (16.0 / v1) * (value - pltpu.roll(value, v1, 1))
        store_slab(wide_b, narrow_b, at + 1, jnp.where(keep, delta * gelu_slope(z, t), 0.0), half)

    repeat(number, second_delta, unrolled(number))
    fill_edges(parts, wide_b, narrow_b)

    def first_delta(at):
        keep, where, size = near(2)
        grad = matmul(plane_slabs(wide_b, narrow_b, at, size, half), back_2[...])
        z = plane_1[at, where]
        delta = jnp.where(keep, grad * gelu_slope(z, gelu_tanh(z)), 0.0)
        store_slab(wide_a, narrow_a, at + 1, delta, half)

    repeat(number, first_delta, unrolled(number))
    fill_edges(parts, wide_a, narrow_a)

    def pixel_step(at):
        size = (cols + 2) * half
        grad = lax.dot_general(
            back_1[...].astype(bf16), plane_slabs(wide_a, narrow_a, at, size, half), (((1,), (1,)), ((), ())),
            preferred_element_type=f32,
        )
        line = lines[at + 1, pl.ds(8, 8)]
        line = line - pltpu.roll(line, 5, 0)
        shift = lax.rem((view_left - left + 1) * half + 2 * lanes, lanes)
        line = pltpu.roll(line, shift, 1)
        grad = grad + (1.0 / 6.0) * line[:, :size]
        for k in range(3):
            grads[pl.ds(k * number + at, 1)] = grad[k : k + 1]

    repeat(number, pixel_step, unrolled(number))
    for k in range(3):
        pixels[k] = grads[k * number : (k + 1) * number].astype(bf16)


def gradient_taps(source, delta, shifted, sums, first_tap):
    rows = delta.shape[0]
    slots, channels = source.shape[-2:]
    cols = source.shape[1] - 2
    count = cols * slots

    def turn(r):
        block = delta[r].astype(jnp.float32)
        for dt in range(3):
            moved = block if dt == 1 else pltpu.roll(block, (dt - 1) % count, 0)
            shifted[dt, r] = moved.T.astype(jnp.bfloat16)

    repeat(rows, turn, rows)

    def tap_step(step):
        tap = jnp.minimum(first_tap + step, 26)
        dt, dr, dc = tap // 9, tap // 3 % 3, tap % 3
        total = 0.0
        for r in range(rows):
            slab = source[r + dr, pl.ds(dc, cols)].reshape(count, channels)
            total = total + matmul(shifted[dt, r], slab)
        sums[pl.ds(pl.multiple_of(step * channels, channels), channels)] = total.T

    repeat(sums.shape[0] // channels, tap_step, 8)


def backward_kernel(*refs, parts, out_rows, groups, outs):
    pixels = refs[:groups]
    (
        rgb, conv_second, first_in, second_in, cells_in, hidden_in,
    ) = refs[groups : groups + 6]
    terms = refs[groups + 6 : groups + 6 + outs]
    (
        slope_first, slope_second, cells, hidden, weight, back_second, paint, shown,
        painted, hidden_grad, delta_second, delta_own, shifted, sums, sems,
    ) = refs[groups + 6 + outs :]
    copies = [
        pltpu.make_async_copy(second_in, slope_second, sems.at[0]),
        pltpu.make_async_copy(hidden_in, hidden, sems.at[1]),
        pltpu.make_async_copy(conv_second, weight, sems.at[2]),
        pltpu.make_async_copy(first_in, slope_first, sems.at[3]),
        pltpu.make_async_copy(cells_in, cells, sems.at[4]),
    ]
    for copy in copies:
        copy.start()
    slots, channels = cells.shape[-2:]
    rows, cols = cells.shape[0] - 2, cells.shape[1] - 2
    height = rows * lax.axis_size("row")
    view_rows = min(height, rows + 20)
    number = view_rows // parts
    own_slots = slots // groups
    group = lax.axis_index("grp")
    top, _, view_top, _ = corner(rows, cols)
    kept = (cols + 2) * own_slots
    paint[...] = jnp.zeros(paint.shape, jnp.float32)
    paint[0:3] = rgb[...].astype(jnp.float32)
    shown[...] = jnp.zeros(shown.shape, jnp.float32)
    for step in range(groups):
        for k in range(3):
            value = pixels[step][k].astype(jnp.float32)
            for at in range(number):
                shown[step, at * 8 + k : at * 8 + k + 1] = value[at : at + 1]

    def paint_step(at):
        for step in range(groups):
            source = partner(group, step, groups)
            slot = painted.at[at, step]
            slot[...] = lax.dot_general(
                shown[step, pl.ds(pl.multiple_of(at * 8, 8), 8)].astype(jnp.bfloat16),
                paint[...].astype(jnp.bfloat16),
                (((0,), (0,)), ((), ())),
                preferred_element_type=jnp.float32,
            )
            for part in range(parts):
                row = kept_row(view_top + part * number + at, top - 1, rows + 2)
                value = slot[pl.ds(part, kept, stride=parts)] if parts > 1 else slot[...]
                hidden_grad[row, pl.ds(source, kept, stride=groups)] = value

    repeat(number, paint_step, unrolled(number))
    copies[0].wait()

    def delta_step(a):
        row = top - 1 + a
        inside = (row >= 0) & (row < height)
        delta = jnp.where(inside, hidden_grad[a + 1] * slope_second[a], 0.0).astype(jnp.bfloat16)
        delta_second[a] = delta.reshape(cols + 2, slots, channels)

    repeat(rows + 2, delta_step, 5)

    first_row = lax.axis_index("grp") * out_rows
    first_tap = first_row // channels
    skip = pl.multiple_of(first_row - first_tap * channels, 32)
    device = lax.axis_index("row") * lax.axis_size("col") + lax.axis_index("col")

    def put(which):
        value = sums[pl.ds(skip, out_rows)]
        if len(terms[0].shape) == 3:
            terms[0][which] = value.astype(jnp.bfloat16)
            return
        chunks, _, size, _ = terms[0].shape
        chunks = chunks * outs
        for k in range(chunks):
            piece = value[k * size : (k + 1) * size].astype(jnp.bfloat16)
            if chunks & (chunks - 1):
                terms[0][lax.rem(k - device + chunks, chunks), which] = piece
            elif outs == 1:
                terms[0][device ^ k, which] = piece
            else:
                at = device ^ k

                @pl.when(at % 2 == 0)
                def _():
                    terms[0][at // 2, which] = piece

                @pl.when(at % 2 == 1)
                def _():
                    terms[1][at // 2, which] = piece

    def own_step(r):
        delta_own[r] = delta_second[r + 1, 1 : 1 + cols].reshape(cols * slots, channels)

    repeat(rows, own_step, rows)
    copies[1].wait()
    gradient_taps(hidden, delta_own, shifted, sums, first_tap)
    put(1)

    copies[2].wait()
    copies[3].wait()
    copies[4].wait()
    for dt in range(3):
        for tap in range(9):
            at = (dt * 9 + tap) * channels
            turned = weight[at : at + channels].astype(jnp.float32).T.astype(jnp.bfloat16)
            back_second[
                (8 - tap) * channels : (9 - tap) * channels,
                (2 - dt) * channels : (3 - dt) * channels,
            ] = turned

    def back_row(r, back):
        delta_own[r] = (back * slope_first[r]).astype(jnp.bfloat16)

    conv_pairs(delta_second, rows, cols, back_second, back_row)
    gradient_taps(cells, delta_own, shifted, sums, first_tap)
    put(0)


def call(kernel, outs, scratch, sems, limit, hbm_in=(), hbm_out=(), operands=0, flops=0):
    def spec(at, chosen):
        return pl.BlockSpec(memory_space=pltpu.HBM if at in chosen else pltpu.VMEM)

    scratch = [pltpu.VMEM(*shape) for shape in scratch]
    if sems:
        scratch.append(pltpu.SemaphoreType.DMA((sems,)))
    several = isinstance(outs, tuple)
    return pl.pallas_call(
        kernel,
        out_shape=outs,
        in_specs=[spec(k, hbm_in) for k in range(operands)],
        out_specs=tuple(spec(k, hbm_out) for k in range(len(outs))) if several else spec(0, hbm_out),
        scratch_shapes=scratch,
        compiler_params=pltpu.CompilerParams(vmem_limit_bytes=limit * 2**20),
        cost_estimate=pl.CostEstimate(flops=flops, bytes_accessed=2**20, transcendentals=0),
    )


def partners(step, count):
    if count & (count - 1):
        return [(i, (i + step) % count) for i in range(count)]
    return [(i, i ^ step) for i in range(count)]


def partner(index, step, count):
    if count & (count - 1):
        return lax.rem(index - step + count, count)
    return index ^ step


def matchings(axis):
    count = lax.axis_size(axis)
    pairs = []
    for first in range(2 if count > 2 else 1):
        pairs.append([(i, i + 1) for i in range(first, count - 1, 2)])
    return pairs


def exchange_pieces(field, width):
    row_pairs, col_pairs = matchings("row"), matchings("col")
    col_count = lax.axis_size("col")
    rows, cols = field.shape[1:3]
    pieces = []
    for row_at in (None, *range(len(row_pairs))):
        for col_at in (None, *range(len(col_pairs))):
            if row_at is None and col_at is None:
                continue
            edge, moves = field, []
            for axis, dim, at, length in (("row", 1, row_at, rows), ("col", 2, col_at, cols)):
                if at is not None:
                    after = (lax.axis_index(axis) % 2 == at).astype(jnp.int32)
                    edge = lax.dynamic_slice_in_dim(edge, after * (length - width), width, axis=dim)
            row_moves = [(i, i) for i in range(lax.axis_size("row"))]
            col_moves = [(i, i) for i in range(col_count)]
            if row_at is not None:
                row_moves = [pair for a, b in row_pairs[row_at] for pair in ((a, b), (b, a))]
            if col_at is not None:
                col_moves = [pair for a, b in col_pairs[col_at] for pair in ((a, b), (b, a))]
            moves = [
                (a * col_count + c, b * col_count + d) for a, b in row_moves for c, d in col_moves
            ]
            pieces.append(((row_at, col_at), edge, moves))
    return pieces


def slotted(field, slots):
    field = jnp.transpose(field, (1, 2, 0, 3))
    return jnp.pad(field, ((0, 0), (0, 0), (0, slots - field.shape[2]), (0, 0)))


def local(dec_input, target, conv_first, conv_second, rgb_weight, vgg_first, vgg_second, vgg_third):
    f32, bf16 = jnp.float32, jnp.bfloat16
    row_count, col_count = lax.axis_size("row"), lax.axis_size("col")
    groups, devices = lax.axis_size("grp"), row_count * col_count
    blocks, block_frames, rows, cols, channels = dec_input.shape
    frames = blocks * block_frames
    frames_own = frames // groups
    parts, own_slots = split(rows, frames_own)
    slots = own_slots * groups
    half = parts * own_slots
    height, width = rows * row_count, cols * col_count
    view_rows, view_cols = min(height, rows + 20), min(width, cols + 20)
    number, count = view_rows // parts, view_cols * half
    lanes = -(-count // 128) * 128
    v1, v2 = vgg_first.shape[1], vgg_third.shape[1]

    raw = dec_input.reshape(frames, rows, cols, channels)
    pieces = exchange_pieces(raw, 3)
    places = tuple(place for place, _, _ in pieces)
    near = [lax.ppermute(slotted(edge, slots), plane, moves) for _, edge, moves in pieces]
    own = slotted(raw, slots)

    line = max(cols * half, -(-width // 128) * 128)
    pack = line // width if parts > 1 and rows % (line // width) == 0 else 1
    target_rows = 3 * blocks * target.shape[2] * rows // pack
    size = -(-(3 * rows + target_rows) // 16) * 16
    big = 16 if parts > 1 else 40

    cells, hidden, slope_first, slope_second, payload = call(
        functools.partial(forward_kernel, frames, parts, pack, places),
        (
            pltpu.HBM((rows + 2, cols + 2, slots, channels), bf16),
            pltpu.HBM((rows + 2, cols + 2, slots, channels), bf16),
            pltpu.HBM((rows, cols * slots, channels), f32),
            pltpu.HBM((rows + 2, (cols + 2) * slots, channels), f32),
            jax.ShapeDtypeStruct((size, line), bf16),
        ),
        [
            ((rows + 6, cols + 6, slots, channels), bf16),
            ((rows + 4, cols + 4, slots, channels), bf16),
            ((rows, cols * slots, channels), f32),
            ((rows + 2, (cols + 2) * slots, channels), f32),
            ((9 * channels, 3 * channels), bf16),
            ((rows + 2, cols * slots, channels), f32),
            ((rows + 2, cols * half, channels), f32),
            (((rows + 2) * 8, cols * half), f32),
            ((8, channels), f32),
        ],
        4,
        big,
        hbm_out=(0, 1, 2, 3),
        operands=5 + len(near),
        flops=2**33,
    )(own, *near, conv_first, conv_second, rgb_weight, target)

    paired = devices == 8 and col_count % 2 == 0
    if paired:
        other = lax.ppermute(payload, plane, [(i, i ^ 1) for i in range(devices)])
        both = jnp.stack([payload, other])
        received = [both] + [
            lax.ppermute(both, plane, [(i, i ^ step) for i in range(devices)])
            for step in range(2, devices, 2)
        ]
    else:
        received = [
            lax.all_to_all(
                jnp.broadcast_to(payload[None], (devices,) + payload.shape),
                plane,
                split_axis=0,
                concat_axis=0,
                tiled=True,
            )
        ]

    wide_count = count + 6 * half
    pixels = call(
        functools.partial(
            perceptual_kernel,
            (
                rows, cols, blocks, block_frames, target.shape[2], parts, own_slots, frames_own,
                pack,
            ),
            len(received),
            paired,
        ),
        jax.ShapeDtypeStruct((3, number, (cols + 2) * half), bf16),
        [
            ((128, 2 * v1), f32),
            ((18 * v1, 2 * v1), bf16),
            ((18 * v1, 2 * v2), bf16),
            ((9 * v2, 2 * v1), bf16),
            ((18 * v1, 2 * v1), bf16),
            ((8, 18 * v1), f32),
            ((devices, rows * 8, line), f32),
            ((number * 3, (cols + 2) * half), f32),
            ((devices, size - 3 * rows, line), f32),
            ((frames_own * parts, number * 8, line), f32),
            ((number + 2, 24, lanes), f32),
            ((number + 2, count + 2 * half, 2 * v1), bf16),
            ((number + 2, count, 2 * v1), bf16),
            ((number // 2 + 2, count // 2 + 2 * half, 2 * v1), bf16),
            ((number // 2 + 2, count // 2, 2 * v1), bf16),
            ((number // 2 + 2, count // 2 + 2 * half, v2), bf16),
            ((number // 2 + 2, count // 2, v2), bf16),
            ((number, wide_count, 2 * v1), f32),
            ((number, wide_count, 2 * v1), f32),
            ((number // 2, wide_count, 2 * v1), f32),
            ((number + 2, (cols + 6) * half, 2 * v1), bf16),
            ((number + 2, (cols + 4) * half, 2 * v1), bf16),
            ((number + 2, (cols + 4) * half, 2 * v1), bf16),
            ((number + 2, (cols + 2) * half, 2 * v1), bf16),
        ],
        0,
        big,
        operands=3 + len(received),
        flops=2**32,
    )(*received, vgg_first, vgg_second.T, vgg_third)

    gathered = [pixels]
    for step in range(1, groups):
        gathered.append(lax.ppermute(pixels, "grp", partners(step, groups)))

    out_rows = conv_first.shape[0] // groups
    taps = max(
        -(-(g + 1) * out_rows // channels) - g * out_rows // channels for g in range(groups)
    )
    even = out_rows % devices == 0
    out_shape = jax.ShapeDtypeStruct((2, out_rows, channels), bf16)
    if even:
        count_out = devices // 2 if paired else devices
        out_shape = jax.ShapeDtypeStruct((count_out, 2, out_rows // devices, channels), bf16)
    if even and paired:
        out_shape = (out_shape, out_shape)
    terms = call(
        functools.partial(
            backward_kernel, parts=parts, out_rows=out_rows, groups=groups,
            outs=2 if even and paired else 1,
        ),
        out_shape,
        [
            ((rows, cols * slots, channels), f32),
            ((rows + 2, (cols + 2) * slots, channels), f32),
            ((rows + 2, cols + 2, slots, channels), bf16),
            ((rows + 2, cols + 2, slots, channels), bf16),
            (conv_second.shape, bf16),
            ((9 * channels, 3 * channels), bf16),
            ((8, channels), f32),
            ((groups, number * 8, (cols + 2) * half), f32),
            ((number, groups, (cols + 2) * half, channels), f32),
            ((rows + 4, (cols + 2) * slots, channels), f32),
            ((rows + 2, cols + 2, slots, channels), bf16),
            ((rows, cols * slots, channels), bf16),
            ((3, rows, channels, cols * slots), bf16),
            ((taps * channels, channels), f32),
        ],
        5,
        big + 8,
        hbm_in=tuple(range(groups + 1, groups + 6)),
        operands=groups + 6,
        flops=2**32,
    )(
        *gathered, rgb_weight, conv_second, slope_first, slope_second, cells, hidden,
    )

    if even and paired:
        kept, given = terms
        came = lax.ppermute(given, plane, partners(1, devices))
        halves = [kept[k].astype(f32) + came[k].astype(f32) for k in range(devices // 2)]
        total = halves[0]
        for k in range(1, devices // 2):
            half_sum = lax.ppermute(halves[k].astype(bf16), plane, partners(2 * k, devices))
            total = total + half_sum.astype(f32)
    elif even:
        pieces = [terms[0]]
        for step in range(1, devices):
            pieces.append(lax.ppermute(terms[step], plane, partners(step, devices)))
        total = sum(piece.astype(f32) for piece in pieces)
    else:
        pieces = jnp.swapaxes(terms.reshape(2, devices, -1), 0, 1)
        pieces = lax.all_to_all(pieces, plane, split_axis=0, concat_axis=0, tiled=True)
        total = jnp.sum(pieces.astype(f32), axis=0)
    return total[0].reshape(-1), total[1].reshape(-1)


def solution(mesh):
    in_specs = (
        P(None, None, "row", "col", None),
        P(None, None, "col", "row", None),
        P(),
        P(),
        P(),
        P(),
        P(),
        P(),
    )
    out_specs = (P(("grp", "row", "col")), P(("grp", "row", "col")))
    return jax.shard_map(local, mesh=mesh, in_specs=in_specs, out_specs=out_specs, check_vma=False)
```

```python
import functools

import jax
import jax.numpy as jnp
from jax import lax
from jax.experimental import pallas as pl
from jax.experimental.pallas import tpu as pltpu
from jax.sharding import PartitionSpec as P

gelu_scale = 0.7978845608028654
gelu_cubic = 0.044715
plane = ("row", "col")


def repeat(count, body, unroll=1):
    lax.fori_loop(0, count, lambda i, carry: (body(i), carry)[1], 0, unroll=unroll)


def matmul(left, right):
    return jnp.dot(left, right, preferred_element_type=jnp.float32)


def gelu_tanh(z):
    return jnp.tanh(gelu_scale * (z + gelu_cubic * z * z * z))


def gelu_slope(z, t):
    return 0.5 * (1.0 + t) + 0.5 * z * (1.0 - t * t) * gelu_scale * (
        1.0 + 3.0 * gelu_cubic * z * z
    )


def split(rows, frames_own):
    small = frames_own <= 4 and lax.axis_size("row") == 2 and rows % 4 == 0
    return (2, 4) if small else (1, 8)


def corner(rows, cols):
    height, width = rows * lax.axis_size("row"), cols * lax.axis_size("col")
    view_rows, view_cols = min(height, rows + 20), min(width, cols + 20)
    top, left = lax.axis_index("row") * rows, lax.axis_index("col") * cols
    view_top = jnp.clip(top - 10, 0, height - view_rows)
    view_left = jnp.clip(left - 10, 0, width - view_cols)
    return top, left, view_top, view_left


def col_mask(first_col, cols, width, slots, frames):
    at = lax.broadcasted_iota(jnp.int32, (cols * slots, 1), 0)
    col = at // slots + first_col
    return (at % slots < frames) & (col >= 0) & (col < width)


def frame_weight(ref):
    third = ref.shape[0] // 3
    return jnp.concatenate([ref[pl.ds(third * k, third)] for k in range(2)], axis=1)


def last_weight(ref):
    third = ref.shape[0] // 3
    size = third // 9
    rows = []
    for dr in range(3):
        near = [ref[pl.ds(2 * third + (3 * dr + dc) * size, size)] for dc in range(3)]
        rows.append(jnp.concatenate([near[1], near[0]], axis=1))
        rows.append(jnp.concatenate([near[2], jnp.zeros_like(near[2])], axis=1))
    return jnp.concatenate(rows, axis=0)


def conv_pairs(source, rows, cols, weight, shifted_weight, use):
    slots, channels = source.shape[-2:]
    count = cols * slots

    def step(q):
        slabs = [
            source[pl.ds(2 * q + dr, 2), pl.ds(dc, cols)].reshape(2 * count, channels)
            for dr in range(3)
            for dc in range(3)
        ]
        sums = matmul(jnp.concatenate(slabs, axis=1), weight[...])
        more = [
            source[pl.ds(2 * q + dr, 2), pl.ds(dc, cols + 1)].reshape(-1, channels)
            for dr in range(3)
            for dc in range(2)
        ]
        last = matmul(jnp.concatenate(more, axis=1), shifted_weight[...])
        last = last.reshape(2, count + slots, 2 * channels)
        last = last[:, slots:, :channels] + last[:, :count, channels:]
        total = (
            pltpu.roll(sums[:, :channels], 1, 0)
            + sums[:, channels:]
            + pltpu.roll(last.reshape(2 * count, channels), 2 * count - 1, 0)
        )
        for k in range(2):
            use(2 * q + k, total[k * count : (k + 1) * count])

    repeat(rows // 2, step, rows // 2)


def forward_kernel(frames, parts, pack, places, own, *refs):
    near = refs[: len(places)]
    (
        first, second, rgb, target, cells_out, hidden_out, first_out, second_out, payload,
        cells, hidden, slope_first, slope_second, spread_weight, shifted_weight, picked, spaced, colour, project,
        sems,
    ) = refs[len(places) :]
    rows, cols, slots, channels = own.shape
    f32, bf16 = jnp.float32, jnp.bfloat16
    groups, group = lax.axis_size("grp"), lax.axis_index("grp")
    height, width = rows * lax.axis_size("row"), cols * lax.axis_size("col")
    top, left_col = lax.axis_index("row") * rows, lax.axis_index("col") * cols
    cells[3 : 3 + rows, 3 : 3 + cols] = own[...]
    if lax.axis_size("row") == 2:
        start = jnp.where(lax.axis_index("row") == 0, 0, 3 + rows)
        cells[pl.ds(start, 3)] = jnp.zeros((3,) + cells.shape[1:], bf16)
    if lax.axis_size("col") == 2:
        start = jnp.where(lax.axis_index("col") == 0, 0, 3 + cols)
        cells[:, pl.ds(start, 3)] = jnp.zeros((rows + 6, 3) + cells.shape[2:], bf16)
    for (row_at, col_at), piece in zip(places, near):
        row, col = 3, 3
        if row_at is not None:
            row = jnp.where(lax.axis_index("row") % 2 == row_at, 3 + rows, 0)
        if col_at is not None:
            col = jnp.where(lax.axis_index("col") % 2 == col_at, 3 + cols, 0)
        cells[pl.ds(row, piece.shape[0]), pl.ds(col, piece.shape[1])] = piece[...]
    copies = [
        pltpu.make_async_copy(
            cells.at[pl.ds(2, rows + 2), pl.ds(2, cols + 2)], cells_out, sems.at[0]
        ),
        pltpu.make_async_copy(
            hidden.at[pl.ds(1, rows + 2), pl.ds(1, cols + 2)], hidden_out, sems.at[1]
        ),
        pltpu.make_async_copy(slope_first, first_out, sems.at[2]),
        pltpu.make_async_copy(slope_second, second_out, sems.at[3]),
    ]
    copies[0].start()
    spread_weight[...] = frame_weight(first)
    shifted_weight[...] = last_weight(first)

    def first_layer(r, pre):
        row = top - 2 + r
        keep = col_mask(left_col - 2, cols + 4, width, slots, frames) & (
            (row >= 0) & (row < height)
        )
        gate = 0.5 + 0.5 * jnp.tanh(0.5 * pre)
        out = jnp.where(keep, pre * gate, 0.0).astype(bf16)
        hidden[r] = out.reshape(cols + 4, slots, channels)
        slope = jnp.where(keep, gate * (1.0 + pre * (1.0 - gate)), 0.0)

        @pl.when((r >= 2) & (r < 2 + rows))
        def _():
            slope_first[r - 2] = slope[2 * slots : (2 + cols) * slots]

    conv_pairs(cells, rows + 4, cols + 4, spread_weight, shifted_weight, first_layer)
    copies[1].start()
    copies[2].start()
    spread_weight[...] = frame_weight(second)
    shifted_weight[...] = last_weight(second)
    own_slots = slots // groups
    spaced[...] = jnp.zeros(spaced.shape, f32)
    project[...] = jnp.zeros(project.shape, f32)
    project[0:3] = rgb[...].astype(f32)

    def second_layer(r, pre):
        row = top - 1 + r
        keep = col_mask(left_col - 1, cols + 2, width, slots, frames) & (
            (row >= 0) & (row < height)
        )
        gate = 0.5 + 0.5 * jnp.tanh(0.5 * pre)
        slope_second[r] = jnp.where(keep, gate * (1.0 + pre * (1.0 - gate)), 0.0)
        picked[r] = jnp.where(keep, pre * gate, 0.0)[slots : (1 + cols) * slots]
        mine = picked.at[r][pl.ds(group, cols * own_slots, stride=groups)]
        if parts > 1:
            part = lax.axis_index("row")
            spaced.at[r][pl.ds(part, cols * own_slots, stride=parts)] = mine
            mine = spaced[r]
        line = lax.dot_general(
            project[...].astype(bf16), mine.astype(bf16), (((1,), (1,)), ((), ())),
            preferred_element_type=f32,
        )
        at = jnp.clip(r - 1, -1, rows) + 1
        colour[pl.ds(pl.multiple_of(at * 8, 8), 8)] = line

    conv_pairs(hidden, rows + 2, cols + 2, spread_weight, shifted_weight, second_layer)
    copies[3].start()
    size, line = payload.shape
    pieces = [colour[pl.ds(8 + k, rows, stride=8)] for k in range(3)]
    goal = target[...].reshape(-1, rows, width).astype(f32)
    if pack > 1:
        short = rows // pack
        goal = jnp.concatenate([goal[:, k * short : (k + 1) * short] for k in range(pack)], axis=2)
    goal = goal.reshape(-1, pack * width)
    if pack * width < line:
        goal = jnp.concatenate(
            [goal, jnp.zeros((goal.shape[0], line - pack * width), f32)], axis=1
        )
    pieces.append(goal)
    filled = 3 * rows + goal.shape[0]
    if filled < size:
        pieces.append(jnp.zeros((size - filled, line), f32))
    lines = jnp.concatenate(pieces, axis=0).astype(bf16)
    payload[...] = lines
    for copy in copies:
        copy.wait()


def plane_slabs(wide, narrow, row, count, half):
    pieces = []
    for dr in range(3):
        pieces.append(wide[row + dr, pl.ds(0, count)])
        pieces.append(narrow[row + dr])
        pieces.append(wide[row + dr, pl.ds(2 * half, count)])
    return jnp.concatenate(pieces, axis=1)


def store_slab(wide, narrow, row, value, half):
    wide[row] = value.astype(jnp.bfloat16)
    narrow[row] = value[half : value.shape[0] - half].astype(jnp.bfloat16)


def store_wide(wide, narrow, row, value, half):
    edge = jnp.zeros((half, value.shape[1]), jnp.float32)
    store_slab(wide, narrow, row, jnp.concatenate([edge, value, edge], axis=0), half)


def fill_edges(parts, *refs):
    for ref in refs:
        last = ref.shape[0] - 1
        if parts == 1:
            for at in (0, last):
                ref[at] = jnp.zeros(ref.shape[1:], ref.dtype)
            continue
        part = lax.broadcasted_iota(jnp.int32, (ref.shape[1], 1), 0) % parts
        low = pltpu.roll(ref[last - 1].astype(jnp.float32), 1, 0)
        high = pltpu.roll(ref[1].astype(jnp.float32), ref.shape[1] - 1, 0)
        ref[0] = jnp.where(part > 0, low, 0.0).astype(ref.dtype)
        ref[last] = jnp.where(part < parts - 1, high, 0.0).astype(ref.dtype)


def kept_row(row, first, number):
    return jnp.clip(row - first, -1, number) + 1


def unrolled(number):
    return number if number <= 8 else 4 if number % 4 == 0 else 2


def plane_weights(
    first, second, third, weight_1, weight_2, weight_3, back_3, back_2, back_1
):
    f32, bf16 = jnp.float32, jnp.bfloat16
    v1, v2 = second.shape[0], third.shape[1]
    zero_3 = jnp.zeros((v1, v2), bf16)
    weight_1[...] = jnp.zeros(weight_1.shape, f32)
    back_1[...] = jnp.zeros(back_1.shape, f32)
    for tap in range(9):
        taken = first[...].astype(f32)[tap * 3 : tap * 3 + 3]
        weight_1[tap * 8 : tap * 8 + 3, 0:v1] = taken
        weight_1[tap * 8 + 3 : tap * 8 + 6, v1 : 2 * v1] = taken
        back_1[0:3, (8 - tap) * 2 * v1 : (8 - tap) * 2 * v1 + v1] = taken
        taken = second[...].astype(f32)[:, tap * v1 : (tap + 1) * v1]
        beside = jnp.concatenate([taken, jnp.zeros_like(taken)], axis=1)
        under = jnp.concatenate([jnp.zeros_like(taken), taken], axis=1)
        both = jnp.concatenate([beside, under], axis=0)
        weight_2[tap * 2 * v1 : (tap + 1) * 2 * v1] = both.T.astype(bf16)
        back_2[(8 - tap) * 2 * v1 : (9 - tap) * 2 * v1] = jnp.concatenate(
            [beside, jnp.zeros_like(beside)], axis=0
        ).astype(bf16)
        taken = third[tap * v1 : (tap + 1) * v1]
        weight_3[tap * 2 * v1 : (tap * 2 + 1) * v1] = jnp.concatenate([taken, zero_3], axis=1)
        weight_3[(tap * 2 + 1) * v1 : (tap * 2 + 2) * v1] = jnp.concatenate(
            [zero_3, taken], axis=1
        )
        turned = jnp.concatenate([taken, zero_3], axis=0).astype(f32).T
        back_3[(8 - tap) * v2 : (9 - tap) * v2] = turned.astype(bf16)


def perceptual_kernel(shape, sources, paired, *refs):
    received = refs[:sources]
    (
        vgg_first, vgg_second, vgg_third, pixels,
        weight_1, weight_2, weight_3, back_3, back_2, back_1, shown, grads,
        target, strips, lines, wide_1, narrow_1, wide_3, narrow_3, wide_g, narrow_g,
        plane_1, plane_2, spread, wide_b, narrow_b, wide_a, narrow_a,
    ) = refs[sources:]
    rows, cols, blocks, block_frames, own, parts, own_slots, frames_own, pack = shape
    f32, bf16 = jnp.float32, jnp.bfloat16
    half = parts * own_slots
    groups, group = lax.axis_size("grp"), lax.axis_index("grp")
    col_parts = lax.axis_size("col")
    width = cols * col_parts
    height = rows * lax.axis_size("row")
    view_rows, view_cols = min(height, rows + 20), min(width, cols + 20)
    top, left, view_top, view_left = corner(rows, cols)
    number = view_rows // parts
    count = view_cols * half
    lanes = lines.shape[2]
    span = width * half
    v1 = weight_2.shape[1] // 2
    v2 = weight_3.shape[1] // 2
    body = pl.ds(3 * half, count)
    plane_weights(
        vgg_first, vgg_second, vgg_third, weight_1, weight_2, weight_3, back_3, back_2, back_1
    )

    place = lax.axis_index("row") * col_parts + lax.axis_index("col")
    for at in range(shown.shape[0]):
        per_source = received[0].shape[0]
        device = place ^ at if paired else at
        arrived = received[at // per_source][at % per_source].astype(f32)
        target[device] = arrived[3 * rows :]
        shown[device] = jnp.zeros(shown.shape[1:], f32)
        for k in range(3):
            shown.at[device][pl.ds(k, rows, stride=8)] = arrived[k * rows : (k + 1) * rows]
    strips[...] = jnp.zeros(strips.shape, f32)
    for j in range(frames_own):
        frame = groups * j + group
        block, rest = frame // block_frames, frame % block_frames
        for part in range(parts):
            for k in range(3):
                short = rows // pack
                start = ((k * blocks + block) * own + rest % own) * short

                def take(at, j=j, part=part, k=k, start=start, rest=rest):
                    row = view_top + part * number + at
                    device = (row // rows) * col_parts + rest // own
                    strips[j * parts + part, pl.ds(at * 8 + 3 + k, 1)] = target[
                        device, pl.ds(start + row % rows, 1)
                    ]

                if parts > 1:
                    device = part * col_parts + rest // own
                    value = target[device, pl.ds(start, short)]
                    for turn in range(pack):
                        strips[j * parts + part, pl.ds(3 + k + turn * short * 8, short, stride=8)] = (
                            pltpu.roll(value, (pack - turn) * width % value.shape[1], 1)
                        )
                else:
                    repeat(number, take)
    from_col = lax.broadcasted_iota(jnp.int32, (target.shape[2], lanes), 0) - view_left
    to_lane = lax.broadcasted_iota(jnp.int32, (target.shape[2], lanes), 1)
    guide = 0.0
    for j in range(frames_own):
        for part in range(parts):
            place = (from_col * half + (j * parts + part) == to_lane) & (to_lane < count)
            guide = guide + matmul(
                strips[j * parts + part].astype(bf16),
                jnp.where(place, 1.0, 0.0).astype(bf16),
            )
    lane = lax.broadcasted_iota(jnp.int32, (8, lanes), 1)
    strips_line = lines.at[pl.ds(1, number)]
    for at in range(number):
        strips_line[at, pl.ds(8, 8)] = guide[at * 8 : at * 8 + 8]

    def line_step(at):
        line = 0.0
        for part in range(parts):
            row = view_top + part * number + at
            source = pl.ds(pl.multiple_of(row % rows * 8, 8), 8)
            line = line + jnp.concatenate(
                [
                    shown[(row // rows) * col_parts + k, source][:, : cols * half]
                    for k in range(col_parts)
                ],
                axis=1,
            )
        line = pltpu.roll(line, lax.rem(span - view_left * half, span), 1)[:, :lanes]
        line = jnp.where(lane < count, line, 0.0) + lines[at + 1, pl.ds(8, 8)]
        before = jnp.where(lane < half, 0.0, pltpu.roll(line, half, 1))
        after = jnp.where(lane >= count - half, 0.0, pltpu.roll(line, lanes - half, 1))
        lines[at + 1] = jnp.concatenate([before, line, after], axis=0)

    repeat(number, line_step, unrolled(number))
    wide_lane = lax.broadcasted_iota(jnp.int32, (24, lanes), 1)
    if parts > 1:
        part = wide_lane % parts
        inside = wide_lane < count
        low = pltpu.roll(lines[number], 1, 1)
        high = pltpu.roll(lines[1], lanes - 1, 1)
        lines[0] = jnp.where((part > 0) & inside, low, 0.0)
        lines[number + 1] = jnp.where((part < parts - 1) & inside, high, 0.0)
    else:
        lines[0] = jnp.zeros((24, lanes), f32)
        lines[number + 1] = jnp.zeros((24, lanes), f32)

    def first_step(at):
        pieces = [lines[at], lines[at + 1], lines[at + 2], jnp.zeros((56, lanes), f32)]
        patches = jnp.concatenate(pieces, axis=0).T[:count].astype(bf16)
        z = matmul(patches, weight_1[...].astype(bf16))
        plane_1[at, body] = z
        store_wide(wide_1, narrow_1, at + 1, 0.5 * z * (1.0 + gelu_tanh(z)), half)

    repeat(number, first_step, unrolled(number))
    fill_edges(parts, wide_1, narrow_1)

    def second_step(q):
        total = 0.0
        for step in range(2):
            at = 2 * q + step
            z = matmul(plane_slabs(wide_1, narrow_1, at, count, half), weight_2[...])
            plane_2[at, body] = z
            total = total + 0.5 * z * (1.0 + gelu_tanh(z))
        pooled = total.reshape(view_cols // 2, 2, half, 2 * v1)
        pooled = 0.25 * (pooled[:, 0] + pooled[:, 1])
        store_wide(wide_3, narrow_3, q + 1, pooled.reshape(count // 2, 2 * v1), half)

    repeat(number // 2, second_step, unrolled(number // 2))
    fill_edges(parts, wide_3, narrow_3)

    def third_step(q):
        z = matmul(plane_slabs(wide_3, narrow_3, q, count // 2, half), weight_3[...])
        t = gelu_tanh(z)
        value = 0.5 * z * (1.0 + t)
        delta = (64.0 / v2) * (value[:, :v2] - value[:, v2:]) * gelu_slope(z[:, :v2], t[:, :v2])
        store_wide(wide_g, narrow_g, q + 1, delta, half)

    repeat(number // 2, third_step, unrolled(number // 2))
    fill_edges(parts, wide_g, narrow_g)

    def pool_step(q):
        grad = 0.25 * matmul(plane_slabs(wide_g, narrow_g, q, count // 2, half), back_3[...])
        grad = grad.reshape(view_cols // 2, 1, half, 2 * v1)
        spread[q, body] = jnp.concatenate([grad, grad], axis=1).reshape(count, 2 * v1)

    repeat(number // 2, pool_step, unrolled(number // 2))

    def near(reach):
        size = (cols + 2 * reach) * half
        keep = col_mask(left - reach, cols + 2 * reach, width, half, half)
        start = pl.multiple_of((left - view_left + 3 - reach) * half, 8)
        return keep, pl.ds(start, size), size

    def second_delta(at):
        keep, where, _ = near(3)
        z = plane_2[at, where]
        t = gelu_tanh(z)
        value = 0.5 * z * (1.0 + t)
        delta = spread[at // 2, where] + (16.0 / v1) * (value - pltpu.roll(value, v1, 1))
        store_slab(wide_b, narrow_b, at + 1, jnp.where(keep, delta * gelu_slope(z, t), 0.0), half)

    repeat(number, second_delta, unrolled(number))
    fill_edges(parts, wide_b, narrow_b)

    def first_delta(at):
        keep, where, size = near(2)
        grad = matmul(plane_slabs(wide_b, narrow_b, at, size, half), back_2[...])
        z = plane_1[at, where]
        delta = jnp.where(keep, grad * gelu_slope(z, gelu_tanh(z)), 0.0)
        store_slab(wide_a, narrow_a, at + 1, delta, half)

    repeat(number, first_delta, unrolled(number))
    fill_edges(parts, wide_a, narrow_a)

    def pixel_step(at):
        size = (cols + 2) * half
        grad = lax.dot_general(
            back_1[...].astype(bf16), plane_slabs(wide_a, narrow_a, at, size, half), (((1,), (1,)), ((), ())),
            preferred_element_type=f32,
        )
        line = lines[at + 1, pl.ds(8, 8)]
        line = line - pltpu.roll(line, 5, 0)
        shift = lax.rem((view_left - left + 1) * half + 2 * lanes, lanes)
        line = pltpu.roll(line, shift, 1)
        grad = grad + (1.0 / 6.0) * line[:, :size]
        for k in range(3):
            grads[pl.ds(k * number + at, 1)] = grad[k : k + 1]

    repeat(number, pixel_step, unrolled(number))
    for k in range(3):
        pixels[k] = grads[k * number : (k + 1) * number].astype(bf16)


def gradient_taps(source, delta, shifted, sums, first_tap):
    rows = delta.shape[0]
    slots, channels = source.shape[-2:]
    cols = source.shape[1] - 2
    count = cols * slots

    def turn(r):
        block = delta[r].astype(jnp.float32)
        for dt in range(3):
            moved = block if dt == 1 else pltpu.roll(block, (dt - 1) % count, 0)
            shifted[dt, r] = moved.T.astype(jnp.bfloat16)

    repeat(rows, turn, rows)

    def tap_step(step):
        tap = jnp.minimum(first_tap + step, 26)
        dt, dr, dc = tap // 9, tap // 3 % 3, tap % 3
        total = 0.0
        for r in range(rows):
            slab = source[r + dr, pl.ds(dc, cols)].reshape(count, channels)
            total = total + matmul(shifted[dt, r], slab)
        sums[pl.ds(pl.multiple_of(step * channels, channels), channels)] = total.T

    repeat(sums.shape[0] // channels, tap_step, 8)


def backward_kernel(*refs, parts, out_rows, groups, outs):
    pixels = refs[:groups]
    (
        rgb, conv_second, first_in, second_in, cells_in, hidden_in,
    ) = refs[groups : groups + 6]
    terms = refs[groups + 6 : groups + 6 + outs]
    (
        slope_first, slope_second, cells, hidden, weight, back_second, back_last, paint, shown,
        painted, hidden_grad, delta_second, delta_own, shifted, sums, sems,
    ) = refs[groups + 6 + outs :]
    copies = [
        pltpu.make_async_copy(second_in, slope_second, sems.at[0]),
        pltpu.make_async_copy(hidden_in, hidden, sems.at[1]),
        pltpu.make_async_copy(conv_second, weight, sems.at[2]),
        pltpu.make_async_copy(first_in, slope_first, sems.at[3]),
        pltpu.make_async_copy(cells_in, cells, sems.at[4]),
    ]
    for copy in copies:
        copy.start()
    slots, channels = cells.shape[-2:]
    rows, cols = cells.shape[0] - 2, cells.shape[1] - 2
    height = rows * lax.axis_size("row")
    view_rows = min(height, rows + 20)
    number = view_rows // parts
    own_slots = slots // groups
    group = lax.axis_index("grp")
    top, _, view_top, _ = corner(rows, cols)
    kept = (cols + 2) * own_slots
    paint[...] = jnp.zeros(paint.shape, jnp.float32)
    paint[0:3] = rgb[...].astype(jnp.float32)
    shown[...] = jnp.zeros(shown.shape, jnp.float32)
    for step in range(groups):
        for k in range(3):
            value = pixels[step][k].astype(jnp.float32)
            for at in range(number):
                shown[step, at * 8 + k : at * 8 + k + 1] = value[at : at + 1]

    def paint_step(at):
        for step in range(groups):
            source = partner(group, step, groups)
            slot = painted.at[at, step]
            slot[...] = lax.dot_general(
                shown[step, pl.ds(pl.multiple_of(at * 8, 8), 8)].astype(jnp.bfloat16),
                paint[...].astype(jnp.bfloat16),
                (((0,), (0,)), ((), ())),
                preferred_element_type=jnp.float32,
            )
            for part in range(parts):
                row = kept_row(view_top + part * number + at, top - 1, rows + 2)
                value = slot[pl.ds(part, kept, stride=parts)] if parts > 1 else slot[...]
                hidden_grad[row, pl.ds(source, kept, stride=groups)] = value

    repeat(number, paint_step, unrolled(number))
    copies[0].wait()

    def delta_step(a):
        row = top - 1 + a
        inside = (row >= 0) & (row < height)
        delta = jnp.where(inside, hidden_grad[a + 1] * slope_second[a], 0.0).astype(jnp.bfloat16)
        delta_second[a] = delta.reshape(cols + 2, slots, channels)

    repeat(rows + 2, delta_step, 5)

    first_row = lax.axis_index("grp") * out_rows
    first_tap = first_row // channels
    skip = pl.multiple_of(first_row - first_tap * channels, 32)
    device = lax.axis_index("row") * lax.axis_size("col") + lax.axis_index("col")

    def put(which):
        value = sums[pl.ds(skip, out_rows)]
        if len(terms[0].shape) == 3:
            terms[0][which] = value.astype(jnp.bfloat16)
            return
        chunks, _, size, _ = terms[0].shape
        chunks = chunks * outs
        for k in range(chunks):
            piece = value[k * size : (k + 1) * size].astype(jnp.bfloat16)
            if chunks & (chunks - 1):
                terms[0][lax.rem(k - device + chunks, chunks), which] = piece
            elif outs == 1:
                terms[0][device ^ k, which] = piece
            else:
                at = device ^ k

                @pl.when(at % 2 == 0)
                def _():
                    terms[0][at // 2, which] = piece

                @pl.when(at % 2 == 1)
                def _():
                    terms[1][at // 2, which] = piece

    def own_step(r):
        delta_own[r] = delta_second[r + 1, 1 : 1 + cols].reshape(cols * slots, channels)

    repeat(rows, own_step, rows)
    copies[1].wait()
    gradient_taps(hidden, delta_own, shifted, sums, first_tap)
    put(1)

    copies[2].wait()
    copies[3].wait()
    copies[4].wait()
    for dt in range(3):
        for tap in range(9):
            at = (dt * 9 + tap) * channels
            turned = weight[at : at + channels].astype(jnp.float32).T.astype(jnp.bfloat16)
            at, dr, dc = 8 - tap, (8 - tap) // 3, (8 - tap) % 3
            if dt > 0:
                back_second[
                    at * channels : (at + 1) * channels,
                    (2 - dt) * channels : (3 - dt) * channels,
                ] = turned
                continue
            into = (2 * dr + (dc == 2)) * channels
            side = channels if dc == 0 else 0
            back_last[into : into + channels, side : side + channels] = turned
            if dc == 2:
                back_last[into : into + channels, channels : 2 * channels] = jnp.zeros_like(turned)

    def back_row(r, back):
        delta_own[r] = (back * slope_first[r]).astype(jnp.bfloat16)

    conv_pairs(delta_second, rows, cols, back_second, back_last, back_row)
    gradient_taps(cells, delta_own, shifted, sums, first_tap)
    put(0)


def call(kernel, outs, scratch, sems, limit, hbm_in=(), hbm_out=(), operands=0, flops=0):
    def spec(at, chosen):
        return pl.BlockSpec(memory_space=pltpu.HBM if at in chosen else pltpu.VMEM)

    scratch = [pltpu.VMEM(*shape) for shape in scratch]
    if sems:
        scratch.append(pltpu.SemaphoreType.DMA((sems,)))
    several = isinstance(outs, tuple)
    return pl.pallas_call(
        kernel,
        out_shape=outs,
        in_specs=[spec(k, hbm_in) for k in range(operands)],
        out_specs=tuple(spec(k, hbm_out) for k in range(len(outs))) if several else spec(0, hbm_out),
        scratch_shapes=scratch,
        compiler_params=pltpu.CompilerParams(vmem_limit_bytes=limit * 2**20),
        cost_estimate=pl.CostEstimate(flops=flops, bytes_accessed=2**20, transcendentals=0),
    )


def partners(step, count):
    if count & (count - 1):
        return [(i, (i + step) % count) for i in range(count)]
    return [(i, i ^ step) for i in range(count)]


def partner(index, step, count):
    if count & (count - 1):
        return lax.rem(index - step + count, count)
    return index ^ step


def matchings(axis):
    count = lax.axis_size(axis)
    pairs = []
    for first in range(2 if count > 2 else 1):
        pairs.append([(i, i + 1) for i in range(first, count - 1, 2)])
    return pairs


def exchange_pieces(field, width):
    row_pairs, col_pairs = matchings("row"), matchings("col")
    col_count = lax.axis_size("col")
    rows, cols = field.shape[1:3]
    pieces = []
    for row_at in (None, *range(len(row_pairs))):
        for col_at in (None, *range(len(col_pairs))):
            if row_at is None and col_at is None:
                continue
            edge, moves = field, []
            for axis, dim, at, length in (("row", 1, row_at, rows), ("col", 2, col_at, cols)):
                if at is not None:
                    after = (lax.axis_index(axis) % 2 == at).astype(jnp.int32)
                    edge = lax.dynamic_slice_in_dim(edge, after * (length - width), width, axis=dim)
            row_moves = [(i, i) for i in range(lax.axis_size("row"))]
            col_moves = [(i, i) for i in range(col_count)]
            if row_at is not None:
                row_moves = [pair for a, b in row_pairs[row_at] for pair in ((a, b), (b, a))]
            if col_at is not None:
                col_moves = [pair for a, b in col_pairs[col_at] for pair in ((a, b), (b, a))]
            moves = [
                (a * col_count + c, b * col_count + d) for a, b in row_moves for c, d in col_moves
            ]
            pieces.append(((row_at, col_at), edge, moves))
    return pieces


def slotted(field, slots):
    field = jnp.transpose(field, (1, 2, 0, 3))
    return jnp.pad(field, ((0, 0), (0, 0), (0, slots - field.shape[2]), (0, 0)))


def local(dec_input, target, conv_first, conv_second, rgb_weight, vgg_first, vgg_second, vgg_third):
    f32, bf16 = jnp.float32, jnp.bfloat16
    row_count, col_count = lax.axis_size("row"), lax.axis_size("col")
    groups, devices = lax.axis_size("grp"), row_count * col_count
    blocks, block_frames, rows, cols, channels = dec_input.shape
    frames = blocks * block_frames
    frames_own = frames // groups
    parts, own_slots = split(rows, frames_own)
    slots = own_slots * groups
    half = parts * own_slots
    height, width = rows * row_count, cols * col_count
    view_rows, view_cols = min(height, rows + 20), min(width, cols + 20)
    number, count = view_rows // parts, view_cols * half
    lanes = -(-count // 128) * 128
    v1, v2 = vgg_first.shape[1], vgg_third.shape[1]

    raw = dec_input.reshape(frames, rows, cols, channels)
    pieces = exchange_pieces(raw, 3)
    places = tuple(place for place, _, _ in pieces)
    near = [lax.ppermute(slotted(edge, slots), plane, moves) for _, edge, moves in pieces]
    own = slotted(raw, slots)

    line = max(cols * half, -(-width // 128) * 128)
    pack = line // width if parts > 1 and rows % (line // width) == 0 else 1
    target_rows = 3 * blocks * target.shape[2] * rows // pack
    size = -(-(3 * rows + target_rows) // 16) * 16
    big = 16 if parts > 1 else 40

    cells, hidden, slope_first, slope_second, payload = call(
        functools.partial(forward_kernel, frames, parts, pack, places),
        (
            pltpu.HBM((rows + 2, cols + 2, slots, channels), bf16),
            pltpu.HBM((rows + 2, cols + 2, slots, channels), bf16),
            pltpu.HBM((rows, cols * slots, channels), f32),
            pltpu.HBM((rows + 2, (cols + 2) * slots, channels), f32),
            jax.ShapeDtypeStruct((size, line), bf16),
        ),
        [
            ((rows + 6, cols + 6, slots, channels), bf16),
            ((rows + 4, cols + 4, slots, channels), bf16),
            ((rows, cols * slots, channels), f32),
            ((rows + 2, (cols + 2) * slots, channels), f32),
            ((9 * channels, 2 * channels), bf16),
            ((6 * channels, 2 * channels), bf16),
            ((rows + 2, cols * slots, channels), f32),
            ((rows + 2, cols * half, channels), f32),
            (((rows + 2) * 8, cols * half), f32),
            ((8, channels), f32),
        ],
        4,
        big,
        hbm_out=(0, 1, 2, 3),
        operands=5 + len(near),
        flops=2**33,
    )(own, *near, conv_first, conv_second, rgb_weight, target)

    paired = devices == 8 and col_count % 2 == 0
    if paired:
        other = lax.ppermute(payload, plane, [(i, i ^ 1) for i in range(devices)])
        both = jnp.stack([payload, other])
        received = [both] + [
            lax.ppermute(both, plane, [(i, i ^ step) for i in range(devices)])
            for step in range(2, devices, 2)
        ]
    else:
        received = [
            lax.all_to_all(
                jnp.broadcast_to(payload[None], (devices,) + payload.shape),
                plane,
                split_axis=0,
                concat_axis=0,
                tiled=True,
            )
        ]

    wide_count = count + 6 * half
    pixels = call(
        functools.partial(
            perceptual_kernel,
            (
                rows, cols, blocks, block_frames, target.shape[2], parts, own_slots, frames_own,
                pack,
            ),
            len(received),
            paired,
        ),
        jax.ShapeDtypeStruct((3, number, (cols + 2) * half), bf16),
        [
            ((128, 2 * v1), f32),
            ((18 * v1, 2 * v1), bf16),
            ((18 * v1, 2 * v2), bf16),
            ((9 * v2, 2 * v1), bf16),
            ((18 * v1, 2 * v1), bf16),
            ((8, 18 * v1), f32),
            ((devices, rows * 8, line), f32),
            ((number * 3, (cols + 2) * half), f32),
            ((devices, size - 3 * rows, line), f32),
            ((frames_own * parts, number * 8, line), f32),
            ((number + 2, 24, lanes), f32),
            ((number + 2, count + 2 * half, 2 * v1), bf16),
            ((number + 2, count, 2 * v1), bf16),
            ((number // 2 + 2, count // 2 + 2 * half, 2 * v1), bf16),
            ((number // 2 + 2, count // 2, 2 * v1), bf16),
            ((number // 2 + 2, count // 2 + 2 * half, v2), bf16),
            ((number // 2 + 2, count // 2, v2), bf16),
            ((number, wide_count, 2 * v1), f32),
            ((number, wide_count, 2 * v1), f32),
            ((number // 2, wide_count, 2 * v1), f32),
            ((number + 2, (cols + 6) * half, 2 * v1), bf16),
            ((number + 2, (cols + 4) * half, 2 * v1), bf16),
            ((number + 2, (cols + 4) * half, 2 * v1), bf16),
            ((number + 2, (cols + 2) * half, 2 * v1), bf16),
        ],
        0,
        big,
        operands=3 + len(received),
        flops=2**32,
    )(*received, vgg_first, vgg_second.T, vgg_third)

    gathered = [pixels]
    for step in range(1, groups):
        gathered.append(lax.ppermute(pixels, "grp", partners(step, groups)))

    out_rows = conv_first.shape[0] // groups
    taps = max(
        -(-(g + 1) * out_rows // channels) - g * out_rows // channels for g in range(groups)
    )
    even = out_rows % devices == 0
    out_shape = jax.ShapeDtypeStruct((2, out_rows, channels), bf16)
    if even:
        count_out = devices // 2 if paired else devices
        out_shape = jax.ShapeDtypeStruct((count_out, 2, out_rows // devices, channels), bf16)
    if even and paired:
        out_shape = (out_shape, out_shape)
    terms = call(
        functools.partial(
            backward_kernel, parts=parts, out_rows=out_rows, groups=groups,
            outs=2 if even and paired else 1,
        ),
        out_shape,
        [
            ((rows, cols * slots, channels), f32),
            ((rows + 2, (cols + 2) * slots, channels), f32),
            ((rows + 2, cols + 2, slots, channels), bf16),
            ((rows + 2, cols + 2, slots, channels), bf16),
            (conv_second.shape, bf16),
            ((9 * channels, 2 * channels), bf16),
            ((6 * channels, 2 * channels), bf16),
            ((8, channels), f32),
            ((groups, number * 8, (cols + 2) * half), f32),
            ((number, groups, (cols + 2) * half, channels), f32),
            ((rows + 4, (cols + 2) * slots, channels), f32),
            ((rows + 2, cols + 2, slots, channels), bf16),
            ((rows, cols * slots, channels), bf16),
            ((3, rows, channels, cols * slots), bf16),
            ((taps * channels, channels), f32),
        ],
        5,
        big + 8,
        hbm_in=tuple(range(groups + 1, groups + 6)),
        operands=groups + 6,
        flops=2**32,
    )(
        *gathered, rgb_weight, conv_second, slope_first, slope_second, cells, hidden,
    )

    if even and paired:
        kept, given = terms
        came = lax.ppermute(given, plane, partners(1, devices))
        halves = [kept[k].astype(f32) + came[k].astype(f32) for k in range(devices // 2)]
        total = halves[0]
        for k in range(1, devices // 2):
            half_sum = lax.ppermute(halves[k].astype(bf16), plane, partners(2 * k, devices))
            total = total + half_sum.astype(f32)
    elif even:
        pieces = [terms[0]]
        for step in range(1, devices):
            pieces.append(lax.ppermute(terms[step], plane, partners(step, devices)))
        total = sum(piece.astype(f32) for piece in pieces)
    else:
        pieces = jnp.swapaxes(terms.reshape(2, devices, -1), 0, 1)
        pieces = lax.all_to_all(pieces, plane, split_axis=0, concat_axis=0, tiled=True)
        total = jnp.sum(pieces.astype(f32), axis=0)
    return total[0].reshape(-1), total[1].reshape(-1)


def solution(mesh):
    in_specs = (
        P(None, None, "row", "col", None),
        P(None, None, "col", "row", None),
        P(),
        P(),
        P(),
        P(),
        P(),
        P(),
    )
    out_specs = (P(("grp", "row", "col")), P(("grp", "row", "col")))
    return jax.shard_map(local, mesh=mesh, in_specs=in_specs, out_specs=out_specs, check_vma=False)
```

```python
import functools

import jax
import jax.numpy as jnp
from jax import lax
from jax.experimental import pallas as pl
from jax.experimental.pallas import tpu as pltpu
from jax.sharding import PartitionSpec as P

gelu_scale = 0.7978845608028654
gelu_cubic = 0.044715
plane = ("row", "col")


def repeat(count, body, unroll=1):
    lax.fori_loop(0, count, lambda i, carry: (body(i), carry)[1], 0, unroll=unroll)


def matmul(left, right):
    return jnp.dot(left, right, preferred_element_type=jnp.float32)


def gelu_tanh(z):
    return jnp.tanh(gelu_scale * (z + gelu_cubic * z * z * z))


def gelu_slope(z, t):
    return 0.5 * (1.0 + t) + 0.5 * z * (1.0 - t * t) * gelu_scale * (
        1.0 + 3.0 * gelu_cubic * z * z
    )


def split(rows, frames_own):
    small = frames_own <= 4 and lax.axis_size("row") == 2 and rows % 4 == 0
    return (2, 4) if small else (1, 8)


def corner(rows, cols):
    height, width = rows * lax.axis_size("row"), cols * lax.axis_size("col")
    view_rows, view_cols = min(height, rows + 20), min(width, cols + 20)
    top, left = lax.axis_index("row") * rows, lax.axis_index("col") * cols
    view_top = jnp.clip(top - 10, 0, height - view_rows)
    view_left = jnp.clip(left - 10, 0, width - view_cols)
    return top, left, view_top, view_left


def col_mask(first_col, cols, width, slots, frames):
    at = lax.broadcasted_iota(jnp.int32, (cols * slots, 1), 0)
    col = at // slots + first_col
    return (at % slots < frames) & (col >= 0) & (col < width)


def frame_weight(ref):
    third = ref.shape[0] // 3
    return jnp.concatenate([ref[pl.ds(third * k, third)] for k in range(2)], axis=1)


def last_weight(ref):
    third = ref.shape[0] // 3
    size = third // 9
    rows = []
    for dr in range(3):
        near = [ref[pl.ds(2 * third + (3 * dr + dc) * size, size)] for dc in range(3)]
        rows.append(jnp.concatenate([near[1], near[0]], axis=1))
        rows.append(jnp.concatenate([near[2], jnp.zeros_like(near[2])], axis=1))
    return jnp.concatenate(rows, axis=0)


def conv_pairs(source, rows, cols, weight, shifted_weight, use):
    slots, channels = source.shape[-2:]
    count = cols * slots

    def step(q):
        slabs = [
            source[pl.ds(2 * q + dr, 2), pl.ds(dc, cols)].reshape(2 * count, channels)
            for dr in range(3)
            for dc in range(3)
        ]
        sums = matmul(jnp.concatenate(slabs, axis=1), weight[...])
        more = [
            source[pl.ds(2 * q + dr, 2), pl.ds(dc, cols + 1)].reshape(-1, channels)
            for dr in range(3)
            for dc in range(2)
        ]
        last = matmul(jnp.concatenate(more, axis=1), shifted_weight[...])
        last = last.reshape(2, count + slots, 2 * channels)
        last = last[:, slots:, :channels] + last[:, :count, channels:]
        total = (
            pltpu.roll(sums[:, :channels], 1, 0)
            + sums[:, channels:]
            + pltpu.roll(last.reshape(2 * count, channels), 2 * count - 1, 0)
        )
        for k in range(2):
            use(2 * q + k, total[k * count : (k + 1) * count])

    repeat(rows // 2, step, rows // 2)


def forward_kernel(frames, parts, pack, places, own, *refs):
    near = refs[: len(places)]
    (
        first, second, rgb, target, cells_out, hidden_out, first_out, second_out, payload,
        cells, hidden, slope_first, slope_second, spread_weight, shifted_weight, picked, spaced, colour, project,
        sems,
    ) = refs[len(places) :]
    rows, cols, slots, channels = own.shape
    f32, bf16 = jnp.float32, jnp.bfloat16
    groups, group = lax.axis_size("grp"), lax.axis_index("grp")
    height, width = rows * lax.axis_size("row"), cols * lax.axis_size("col")
    top, left_col = lax.axis_index("row") * rows, lax.axis_index("col") * cols
    cells[3 : 3 + rows, 3 : 3 + cols] = own[...]
    if lax.axis_size("row") == 2:
        start = jnp.where(lax.axis_index("row") == 0, 0, 3 + rows)
        cells[pl.ds(start, 3)] = jnp.zeros((3,) + cells.shape[1:], bf16)
    if lax.axis_size("col") == 2:
        start = jnp.where(lax.axis_index("col") == 0, 0, 3 + cols)
        cells[:, pl.ds(start, 3)] = jnp.zeros((rows + 6, 3) + cells.shape[2:], bf16)
    for (row_at, col_at), piece in zip(places, near):
        row, col = 3, 3
        if row_at is not None:
            row = jnp.where(lax.axis_index("row") % 2 == row_at, 3 + rows, 0)
        if col_at is not None:
            col = jnp.where(lax.axis_index("col") % 2 == col_at, 3 + cols, 0)
        cells[pl.ds(row, piece.shape[0]), pl.ds(col, piece.shape[1])] = piece[...]
    copies = [
        pltpu.make_async_copy(
            cells.at[pl.ds(2, rows + 2), pl.ds(2, cols + 2)], cells_out, sems.at[0]
        ),
        pltpu.make_async_copy(
            hidden.at[pl.ds(1, rows + 2), pl.ds(1, cols + 2)], hidden_out, sems.at[1]
        ),
        pltpu.make_async_copy(slope_first, first_out, sems.at[2]),
        pltpu.make_async_copy(slope_second, second_out, sems.at[3]),
    ]
    copies[0].start()
    spread_weight[...] = frame_weight(first)
    shifted_weight[...] = last_weight(first)

    def first_layer(r, pre):
        row = top - 2 + r
        keep = col_mask(left_col - 2, cols + 4, width, slots, frames) & (
            (row >= 0) & (row < height)
        )
        gate = 0.5 + 0.5 * jnp.tanh(0.5 * pre)
        out = jnp.where(keep, pre * gate, 0.0).astype(bf16)
        hidden[r] = out.reshape(cols + 4, slots, channels)
        slope = jnp.where(keep, gate * (1.0 + pre * (1.0 - gate)), 0.0)

        @pl.when((r >= 2) & (r < 2 + rows))
        def _():
            slope_first[r - 2] = slope[2 * slots : (2 + cols) * slots]

    conv_pairs(cells, rows + 4, cols + 4, spread_weight, shifted_weight, first_layer)
    copies[1].start()
    copies[2].start()
    spread_weight[...] = frame_weight(second)
    shifted_weight[...] = last_weight(second)
    own_slots = slots // groups
    spaced[...] = jnp.zeros(spaced.shape, f32)
    project[...] = jnp.zeros(project.shape, f32)
    project[0:3] = rgb[...].astype(f32)

    def second_layer(r, pre):
        row = top - 1 + r
        keep = col_mask(left_col - 1, cols + 2, width, slots, frames) & (
            (row >= 0) & (row < height)
        )
        gate = 0.5 + 0.5 * jnp.tanh(0.5 * pre)
        slope_second[r] = jnp.where(keep, gate * (1.0 + pre * (1.0 - gate)), 0.0)
        picked[r] = jnp.where(keep, pre * gate, 0.0)[slots : (1 + cols) * slots]
        mine = picked.at[r][pl.ds(group, cols * own_slots, stride=groups)]
        if parts > 1:
            part = lax.axis_index("row")
            spaced.at[r][pl.ds(part, cols * own_slots, stride=parts)] = mine
            mine = spaced[r]
        line = lax.dot_general(
            project[...].astype(bf16), mine.astype(bf16), (((1,), (1,)), ((), ())),
            preferred_element_type=f32,
        )
        at = jnp.clip(r - 1, -1, rows) + 1
        colour[pl.ds(pl.multiple_of(at * 8, 8), 8)] = line

    conv_pairs(hidden, rows + 2, cols + 2, spread_weight, shifted_weight, second_layer)
    copies[3].start()
    size, line = payload.shape
    pieces = [colour[pl.ds(8 + k, rows, stride=8)] for k in range(3)]
    goal = target[...].reshape(-1, rows, width).astype(f32)
    if pack > 1:
        short = rows // pack
        goal = jnp.concatenate([goal[:, k * short : (k + 1) * short] for k in range(pack)], axis=2)
    goal = goal.reshape(-1, pack * width)
    if pack * width < line:
        goal = jnp.concatenate(
            [goal, jnp.zeros((goal.shape[0], line - pack * width), f32)], axis=1
        )
    pieces.append(goal)
    filled = 3 * rows + goal.shape[0]
    if filled < size:
        pieces.append(jnp.zeros((size - filled, line), f32))
    lines = jnp.concatenate(pieces, axis=0).astype(bf16)
    payload[...] = lines
    for copy in copies:
        copy.wait()


def plane_slabs(wide, narrow, row, count, half):
    pieces = []
    for dr in range(3):
        pieces.append(wide[row + dr, pl.ds(0, count)])
        pieces.append(narrow[row + dr])
        pieces.append(wide[row + dr, pl.ds(2 * half, count)])
    return jnp.concatenate(pieces, axis=1)


def store_slab(wide, narrow, row, value, half):
    wide[row] = value.astype(jnp.bfloat16)
    narrow[row] = value[half : value.shape[0] - half].astype(jnp.bfloat16)


def store_wide(wide, narrow, row, value, half):
    edge = jnp.zeros((half, value.shape[1]), jnp.float32)
    store_slab(wide, narrow, row, jnp.concatenate([edge, value, edge], axis=0), half)


def fill_edges(parts, *refs):
    for ref in refs:
        last = ref.shape[0] - 1
        if parts == 1:
            for at in (0, last):
                ref[at] = jnp.zeros(ref.shape[1:], ref.dtype)
            continue
        part = lax.broadcasted_iota(jnp.int32, (ref.shape[1], 1), 0) % parts
        low = pltpu.roll(ref[last - 1].astype(jnp.float32), 1, 0)
        high = pltpu.roll(ref[1].astype(jnp.float32), ref.shape[1] - 1, 0)
        ref[0] = jnp.where(part > 0, low, 0.0).astype(ref.dtype)
        ref[last] = jnp.where(part < parts - 1, high, 0.0).astype(ref.dtype)


def kept_row(row, first, number):
    return jnp.clip(row - first, -1, number) + 1


def unrolled(number):
    return number if number <= 8 else 4 if number % 4 == 0 else 2


def plane_weights(
    first, second, third, weight_1, weight_2, weight_3, back_3, back_2, back_1
):
    f32, bf16 = jnp.float32, jnp.bfloat16
    v1, v2 = second.shape[0], third.shape[1]
    zero_3 = jnp.zeros((v1, v2), bf16)
    weight_1[...] = jnp.zeros(weight_1.shape, f32)
    back_1[...] = jnp.zeros(back_1.shape, f32)
    for tap in range(9):
        taken = first[...].astype(f32)[tap * 3 : tap * 3 + 3]
        weight_1[tap * 8 : tap * 8 + 3, 0:v1] = taken
        weight_1[tap * 8 + 3 : tap * 8 + 6, v1 : 2 * v1] = taken
        back_1[0:3, (8 - tap) * 2 * v1 : (8 - tap) * 2 * v1 + v1] = taken
        taken = second[...].astype(f32)[:, tap * v1 : (tap + 1) * v1]
        beside = jnp.concatenate([taken, jnp.zeros_like(taken)], axis=1)
        under = jnp.concatenate([jnp.zeros_like(taken), taken], axis=1)
        both = jnp.concatenate([beside, under], axis=0)
        weight_2[tap * 2 * v1 : (tap + 1) * 2 * v1] = both.T.astype(bf16)
        back_2[(8 - tap) * 2 * v1 : (9 - tap) * 2 * v1] = jnp.concatenate(
            [beside, jnp.zeros_like(beside)], axis=0
        ).astype(bf16)
        taken = third[tap * v1 : (tap + 1) * v1]
        weight_3[tap * 2 * v1 : (tap * 2 + 1) * v1] = jnp.concatenate([taken, zero_3], axis=1)
        weight_3[(tap * 2 + 1) * v1 : (tap * 2 + 2) * v1] = jnp.concatenate(
            [zero_3, taken], axis=1
        )
        turned = jnp.concatenate([taken, zero_3], axis=0).astype(f32).T
        back_3[(8 - tap) * v2 : (9 - tap) * v2] = turned.astype(bf16)


def perceptual_kernel(shape, sources, paired, *refs):
    received = refs[:sources]
    (
        vgg_first, vgg_second, vgg_third, pixels,
        weight_1, weight_2, weight_3, back_3, back_2, back_1, shown, grads,
        target, strips, lines, wide_1, narrow_1, wide_3, narrow_3, wide_g, narrow_g,
        plane_1, plane_2, spread, wide_b, narrow_b, wide_a, narrow_a,
    ) = refs[sources:]
    rows, cols, blocks, block_frames, own, parts, own_slots, frames_own, pack = shape
    f32, bf16 = jnp.float32, jnp.bfloat16
    half = parts * own_slots
    groups, group = lax.axis_size("grp"), lax.axis_index("grp")
    col_parts = lax.axis_size("col")
    width = cols * col_parts
    height = rows * lax.axis_size("row")
    view_rows, view_cols = min(height, rows + 20), min(width, cols + 20)
    top, left, view_top, view_left = corner(rows, cols)
    number = view_rows // parts
    count = view_cols * half
    lanes = lines.shape[2]
    span = width * half
    v1 = weight_2.shape[1] // 2
    v2 = weight_3.shape[1] // 2
    body = pl.ds(3 * half, count)
    plane_weights(
        vgg_first, vgg_second, vgg_third, weight_1, weight_2, weight_3, back_3, back_2, back_1
    )

    place = lax.axis_index("row") * col_parts + lax.axis_index("col")
    for at in range(shown.shape[0]):
        per_source = received[0].shape[0]
        device = place ^ at if paired else at
        arrived = received[at // per_source][at % per_source].astype(f32)
        target[device] = arrived[3 * rows :]
        shown[device] = jnp.zeros(shown.shape[1:], f32)
        for k in range(3):
            shown.at[device][pl.ds(k, rows, stride=8)] = arrived[k * rows : (k + 1) * rows]
    strips[...] = jnp.zeros(strips.shape, f32)
    for j in range(frames_own):
        frame = groups * j + group
        block, rest = frame // block_frames, frame % block_frames
        for part in range(parts):
            for k in range(3):
                short = rows // pack
                start = ((k * blocks + block) * own + rest % own) * short

                def take(at, j=j, part=part, k=k, start=start, rest=rest):
                    row = view_top + part * number + at
                    device = (row // rows) * col_parts + rest // own
                    strips[j * parts + part, pl.ds(at * 8 + 3 + k, 1)] = target[
                        device, pl.ds(start + row % rows, 1)
                    ]

                if parts > 1:
                    device = part * col_parts + rest // own
                    value = target[device, pl.ds(start, short)]
                    for turn in range(pack):
                        strips[j * parts + part, pl.ds(3 + k + turn * short * 8, short, stride=8)] = (
                            pltpu.roll(value, (pack - turn) * width % value.shape[1], 1)
                        )
                else:
                    repeat(number, take)
    from_col = lax.broadcasted_iota(jnp.int32, (target.shape[2], lanes), 0) - view_left
    to_lane = lax.broadcasted_iota(jnp.int32, (target.shape[2], lanes), 1)
    guide = 0.0
    for j in range(frames_own):
        for part in range(parts):
            place = (from_col * half + (j * parts + part) == to_lane) & (to_lane < count)
            guide = guide + matmul(
                strips[j * parts + part].astype(bf16),
                jnp.where(place, 1.0, 0.0).astype(bf16),
            )
    lane = lax.broadcasted_iota(jnp.int32, (8, lanes), 1)
    strips_line = lines.at[pl.ds(1, number)]
    for at in range(number):
        strips_line[at, pl.ds(8, 8)] = guide[at * 8 : at * 8 + 8]

    def line_step(at):
        line = 0.0
        for part in range(parts):
            row = view_top + part * number + at
            source = pl.ds(pl.multiple_of(row % rows * 8, 8), 8)
            line = line + jnp.concatenate(
                [
                    shown[(row // rows) * col_parts + k, source][:, : cols * half]
                    for k in range(col_parts)
                ],
                axis=1,
            )
        line = pltpu.roll(line, lax.rem(span - view_left * half, span), 1)[:, :lanes]
        line = jnp.where(lane < count, line, 0.0) + lines[at + 1, pl.ds(8, 8)]
        before = jnp.where(lane < half, 0.0, pltpu.roll(line, half, 1))
        after = jnp.where(lane >= count - half, 0.0, pltpu.roll(line, lanes - half, 1))
        lines[at + 1] = jnp.concatenate([before, line, after], axis=0)

    repeat(number, line_step, unrolled(number))
    wide_lane = lax.broadcasted_iota(jnp.int32, (24, lanes), 1)
    if parts > 1:
        part = wide_lane % parts
        inside = wide_lane < count
        low = pltpu.roll(lines[number], 1, 1)
        high = pltpu.roll(lines[1], lanes - 1, 1)
        lines[0] = jnp.where((part > 0) & inside, low, 0.0)
        lines[number + 1] = jnp.where((part < parts - 1) & inside, high, 0.0)
    else:
        lines[0] = jnp.zeros((24, lanes), f32)
        lines[number + 1] = jnp.zeros((24, lanes), f32)

    def first_step(at):
        pieces = [lines[at], lines[at + 1], lines[at + 2], jnp.zeros((56, lanes), f32)]
        patches = jnp.concatenate(pieces, axis=0).T[:count].astype(bf16)
        z = matmul(patches, weight_1[...].astype(bf16))
        plane_1[at, body] = z
        store_wide(wide_1, narrow_1, at + 1, 0.5 * z * (1.0 + gelu_tanh(z)), half)

    repeat(number, first_step, unrolled(number))
    fill_edges(parts, wide_1, narrow_1)

    def second_step(q):
        total = 0.0
        for step in range(2):
            at = 2 * q + step
            z = matmul(plane_slabs(wide_1, narrow_1, at, count, half), weight_2[...])
            plane_2[at, body] = z
            total = total + 0.5 * z * (1.0 + gelu_tanh(z))
        pooled = total.reshape(view_cols // 2, 2, half, 2 * v1)
        pooled = 0.25 * (pooled[:, 0] + pooled[:, 1])
        store_wide(wide_3, narrow_3, q + 1, pooled.reshape(count // 2, 2 * v1), half)

    repeat(number // 2, second_step, unrolled(number // 2))
    fill_edges(parts, wide_3, narrow_3)

    def third_step(q):
        z = matmul(plane_slabs(wide_3, narrow_3, q, count // 2, half), weight_3[...])
        t = gelu_tanh(z)
        value = 0.5 * z * (1.0 + t)
        delta = (64.0 / v2) * (value[:, :v2] - value[:, v2:]) * gelu_slope(z[:, :v2], t[:, :v2])
        store_wide(wide_g, narrow_g, q + 1, delta, half)

    repeat(number // 2, third_step, unrolled(number // 2))
    fill_edges(parts, wide_g, narrow_g)

    def pool_step(q):
        grad = 0.25 * matmul(plane_slabs(wide_g, narrow_g, q, count // 2, half), back_3[...])
        grad = grad.reshape(view_cols // 2, 1, half, 2 * v1)
        spread[q, body] = jnp.concatenate([grad, grad], axis=1).reshape(count, 2 * v1)

    repeat(number // 2, pool_step, unrolled(number // 2))

    def near(reach):
        size = (cols + 2 * reach) * half
        keep = col_mask(left - reach, cols + 2 * reach, width, half, half)
        start = pl.multiple_of((left - view_left + 3 - reach) * half, 8)
        return keep, pl.ds(start, size), size

    def second_delta(at):
        keep, where, _ = near(3)
        z = plane_2[at, where]
        t = gelu_tanh(z)
        value = 0.5 * z * (1.0 + t)
        delta = spread[at // 2, where] + (16.0 / v1) * (value - pltpu.roll(value, v1, 1))
        store_slab(wide_b, narrow_b, at + 1, jnp.where(keep, delta * gelu_slope(z, t), 0.0), half)

    repeat(number, second_delta, unrolled(number))
    fill_edges(parts, wide_b, narrow_b)

    def first_delta(at):
        keep, where, size = near(2)
        grad = matmul(plane_slabs(wide_b, narrow_b, at, size, half), back_2[...])
        z = plane_1[at, where]
        delta = jnp.where(keep, grad * gelu_slope(z, gelu_tanh(z)), 0.0)
        store_slab(wide_a, narrow_a, at + 1, delta, half)

    repeat(number, first_delta, unrolled(number))
    fill_edges(parts, wide_a, narrow_a)

    def pixel_step(at):
        size = (cols + 2) * half
        grad = lax.dot_general(
            back_1[...].astype(bf16), plane_slabs(wide_a, narrow_a, at, size, half), (((1,), (1,)), ((), ())),
            preferred_element_type=f32,
        )
        line = lines[at + 1, pl.ds(8, 8)]
        line = line - pltpu.roll(line, 5, 0)
        shift = lax.rem((view_left - left + 1) * half + 2 * lanes, lanes)
        line = pltpu.roll(line, shift, 1)
        grad = grad + (1.0 / 6.0) * line[:, :size]
        for k in range(3):
            grads[pl.ds(k * number + at, 1)] = grad[k : k + 1]

    repeat(number, pixel_step, unrolled(number))
    for k in range(3):
        pixels[k] = grads[k * number : (k + 1) * number].astype(bf16)


def gradient_taps(source, delta, shifted, sums, first_tap):
    rows = delta.shape[0]
    slots, channels = source.shape[-2:]
    cols = source.shape[1] - 2
    count = cols * slots

    def turn(r):
        block = delta[r].astype(jnp.float32)
        flat = block.T
        for dt in range(3):
            moved = flat if dt == 1 else pltpu.roll(flat, (dt - 1) % count, 1)
            shifted[dt, r] = moved.astype(jnp.bfloat16)

    repeat(rows, turn, rows)

    def tap_step(step):
        tap = jnp.minimum(first_tap + step, 26)
        dt, dr, dc = tap // 9, tap // 3 % 3, tap % 3
        slab = source[pl.ds(dr, rows), pl.ds(dc, cols)].reshape(rows * count, channels)
        turned = jnp.concatenate([shifted[dt, r] for r in range(rows)], axis=1)
        total = matmul(turned, slab)
        sums[pl.ds(pl.multiple_of(step * channels, channels), channels)] = total.T

    repeat(sums.shape[0] // channels, tap_step, 8)


def backward_kernel(*refs, parts, out_rows, groups, outs):
    pixels = refs[:groups]
    (
        rgb, conv_second, first_in, second_in, cells_in, hidden_in,
    ) = refs[groups : groups + 6]
    terms = refs[groups + 6 : groups + 6 + outs]
    (
        slope_first, slope_second, cells, hidden, weight, back_second, back_last, paint, shown,
        painted, hidden_grad, delta_second, delta_own, shifted, sums, sems,
    ) = refs[groups + 6 + outs :]
    copies = [
        pltpu.make_async_copy(second_in, slope_second, sems.at[0]),
        pltpu.make_async_copy(hidden_in, hidden, sems.at[1]),
        pltpu.make_async_copy(conv_second, weight, sems.at[2]),
        pltpu.make_async_copy(first_in, slope_first, sems.at[3]),
        pltpu.make_async_copy(cells_in, cells, sems.at[4]),
    ]
    for copy in copies:
        copy.start()
    slots, channels = cells.shape[-2:]
    rows, cols = cells.shape[0] - 2, cells.shape[1] - 2
    height = rows * lax.axis_size("row")
    view_rows = min(height, rows + 20)
    number = view_rows // parts
    own_slots = slots // groups
    group = lax.axis_index("grp")
    top, _, view_top, _ = corner(rows, cols)
    kept = (cols + 2) * own_slots
    paint[...] = jnp.zeros(paint.shape, jnp.float32)
    paint[0:3] = rgb[...].astype(jnp.float32)
    shown[...] = jnp.zeros(shown.shape, jnp.float32)
    for step in range(groups):
        for k in range(3):
            value = pixels[step][k].astype(jnp.float32)
            for at in range(number):
                shown[step, at * 8 + k : at * 8 + k + 1] = value[at : at + 1]

    def paint_step(at):
        for step in range(groups):
            source = partner(group, step, groups)
            slot = painted.at[at, step]
            slot[...] = lax.dot_general(
                shown[step, pl.ds(pl.multiple_of(at * 8, 8), 8)].astype(jnp.bfloat16),
                paint[...].astype(jnp.bfloat16),
                (((0,), (0,)), ((), ())),
                preferred_element_type=jnp.float32,
            )
            for part in range(parts):
                row = kept_row(view_top + part * number + at, top - 1, rows + 2)
                value = slot[pl.ds(part, kept, stride=parts)] if parts > 1 else slot[...]
                hidden_grad[row, pl.ds(source, kept, stride=groups)] = value

    repeat(number, paint_step, unrolled(number))
    copies[0].wait()

    def delta_step(a):
        row = top - 1 + a
        inside = (row >= 0) & (row < height)
        delta = jnp.where(inside, hidden_grad[a + 1] * slope_second[a], 0.0).astype(jnp.bfloat16)
        delta_second[a] = delta.reshape(cols + 2, slots, channels)

    repeat(rows + 2, delta_step, 10)

    first_row = lax.axis_index("grp") * out_rows
    first_tap = first_row // channels
    skip = pl.multiple_of(first_row - first_tap * channels, 32)
    device = lax.axis_index("row") * lax.axis_size("col") + lax.axis_index("col")

    def put(which):
        value = sums[pl.ds(skip, out_rows)]
        if len(terms[0].shape) == 3:
            terms[0][which] = value.astype(jnp.bfloat16)
            return
        chunks, _, size, _ = terms[0].shape
        chunks = chunks * outs
        for k in range(chunks):
            piece = value[k * size : (k + 1) * size].astype(jnp.bfloat16)
            if chunks & (chunks - 1):
                terms[0][lax.rem(k - device + chunks, chunks), which] = piece
            elif outs == 1:
                terms[0][device ^ k, which] = piece
            else:
                at = device ^ k

                @pl.when(at % 2 == 0)
                def _():
                    terms[0][at // 2, which] = piece

                @pl.when(at % 2 == 1)
                def _():
                    terms[1][at // 2, which] = piece

    def own_step(r):
        delta_own[r] = delta_second[r + 1, 1 : 1 + cols].reshape(cols * slots, channels)

    repeat(rows, own_step, rows)
    copies[1].wait()
    gradient_taps(hidden, delta_own, shifted, sums, first_tap)
    put(1)

    copies[2].wait()
    copies[3].wait()
    copies[4].wait()
    for dt in range(3):
        for tap in range(9):
            at = (dt * 9 + tap) * channels
            turned = weight[at : at + channels].astype(jnp.float32).T.astype(jnp.bfloat16)
            at, dr, dc = 8 - tap, (8 - tap) // 3, (8 - tap) % 3
            if dt > 0:
                back_second[
                    at * channels : (at + 1) * channels,
                    (2 - dt) * channels : (3 - dt) * channels,
                ] = turned
                continue
            into = (2 * dr + (dc == 2)) * channels
            side = channels if dc == 0 else 0
            back_last[into : into + channels, side : side + channels] = turned
            if dc == 2:
                back_last[into : into + channels, channels : 2 * channels] = jnp.zeros_like(turned)

    def back_row(r, back):
        delta_own[r] = (back * slope_first[r]).astype(jnp.bfloat16)

    conv_pairs(delta_second, rows, cols, back_second, back_last, back_row)
    gradient_taps(cells, delta_own, shifted, sums, first_tap)
    put(0)


def call(kernel, outs, scratch, sems, limit, hbm_in=(), hbm_out=(), operands=0, flops=0):
    def spec(at, chosen):
        return pl.BlockSpec(memory_space=pltpu.HBM if at in chosen else pltpu.VMEM)

    scratch = [pltpu.VMEM(*shape) for shape in scratch]
    if sems:
        scratch.append(pltpu.SemaphoreType.DMA((sems,)))
    several = isinstance(outs, tuple)
    return pl.pallas_call(
        kernel,
        out_shape=outs,
        in_specs=[spec(k, hbm_in) for k in range(operands)],
        out_specs=tuple(spec(k, hbm_out) for k in range(len(outs))) if several else spec(0, hbm_out),
        scratch_shapes=scratch,
        compiler_params=pltpu.CompilerParams(vmem_limit_bytes=limit * 2**20),
        cost_estimate=pl.CostEstimate(flops=flops, bytes_accessed=2**20, transcendentals=0),
    )


def partners(step, count):
    if count & (count - 1):
        return [(i, (i + step) % count) for i in range(count)]
    return [(i, i ^ step) for i in range(count)]


def partner(index, step, count):
    if count & (count - 1):
        return lax.rem(index - step + count, count)
    return index ^ step


def matchings(axis):
    count = lax.axis_size(axis)
    pairs = []
    for first in range(2 if count > 2 else 1):
        pairs.append([(i, i + 1) for i in range(first, count - 1, 2)])
    return pairs


def exchange_pieces(field, width):
    row_pairs, col_pairs = matchings("row"), matchings("col")
    col_count = lax.axis_size("col")
    rows, cols = field.shape[1:3]
    pieces = []
    for row_at in (None, *range(len(row_pairs))):
        for col_at in (None, *range(len(col_pairs))):
            if row_at is None and col_at is None:
                continue
            edge, moves = field, []
            for axis, dim, at, length in (("row", 1, row_at, rows), ("col", 2, col_at, cols)):
                if at is not None:
                    after = (lax.axis_index(axis) % 2 == at).astype(jnp.int32)
                    edge = lax.dynamic_slice_in_dim(edge, after * (length - width), width, axis=dim)
            row_moves = [(i, i) for i in range(lax.axis_size("row"))]
            col_moves = [(i, i) for i in range(col_count)]
            if row_at is not None:
                row_moves = [pair for a, b in row_pairs[row_at] for pair in ((a, b), (b, a))]
            if col_at is not None:
                col_moves = [pair for a, b in col_pairs[col_at] for pair in ((a, b), (b, a))]
            moves = [
                (a * col_count + c, b * col_count + d) for a, b in row_moves for c, d in col_moves
            ]
            pieces.append(((row_at, col_at), edge, moves))
    return pieces


def slotted(field, slots):
    field = jnp.transpose(field, (1, 2, 0, 3))
    return jnp.pad(field, ((0, 0), (0, 0), (0, slots - field.shape[2]), (0, 0)))


def local(dec_input, target, conv_first, conv_second, rgb_weight, vgg_first, vgg_second, vgg_third):
    f32, bf16 = jnp.float32, jnp.bfloat16
    row_count, col_count = lax.axis_size("row"), lax.axis_size("col")
    groups, devices = lax.axis_size("grp"), row_count * col_count
    blocks, block_frames, rows, cols, channels = dec_input.shape
    frames = blocks * block_frames
    frames_own = frames // groups
    parts, own_slots = split(rows, frames_own)
    slots = own_slots * groups
    half = parts * own_slots
    height, width = rows * row_count, cols * col_count
    view_rows, view_cols = min(height, rows + 20), min(width, cols + 20)
    number, count = view_rows // parts, view_cols * half
    lanes = -(-count // 128) * 128
    v1, v2 = vgg_first.shape[1], vgg_third.shape[1]

    raw = dec_input.reshape(frames, rows, cols, channels)
    pieces = exchange_pieces(raw, 3)
    places = tuple(place for place, _, _ in pieces)
    near = [lax.ppermute(slotted(edge, slots), plane, moves) for _, edge, moves in pieces]
    own = slotted(raw, slots)

    line = max(cols * half, -(-width // 128) * 128)
    pack = line // width if parts > 1 and rows % (line // width) == 0 else 1
    target_rows = 3 * blocks * target.shape[2] * rows // pack
    size = -(-(3 * rows + target_rows) // 16) * 16
    big = 16 if parts > 1 else 40

    cells, hidden, slope_first, slope_second, payload = call(
        functools.partial(forward_kernel, frames, parts, pack, places),
        (
            pltpu.HBM((rows + 2, cols + 2, slots, channels), bf16),
            pltpu.HBM((rows + 2, cols + 2, slots, channels), bf16),
            pltpu.HBM((rows, cols * slots, channels), f32),
            pltpu.HBM((rows + 2, (cols + 2) * slots, channels), f32),
            jax.ShapeDtypeStruct((size, line), bf16),
        ),
        [
            ((rows + 6, cols + 6, slots, channels), bf16),
            ((rows + 4, cols + 4, slots, channels), bf16),
            ((rows, cols * slots, channels), f32),
            ((rows + 2, (cols + 2) * slots, channels), f32),
            ((9 * channels, 2 * channels), bf16),
            ((6 * channels, 2 * channels), bf16),
            ((rows + 2, cols * slots, channels), f32),
            ((rows + 2, cols * half, channels), f32),
            (((rows + 2) * 8, cols * half), f32),
            ((8, channels), f32),
        ],
        4,
        big,
        hbm_out=(0, 1, 2, 3),
        operands=5 + len(near),
        flops=2**33,
    )(own, *near, conv_first, conv_second, rgb_weight, target)

    paired = devices == 8 and col_count % 2 == 0
    if paired:
        other = lax.ppermute(payload, plane, [(i, i ^ 1) for i in range(devices)])
        both = jnp.stack([payload, other])
        received = [both] + [
            lax.ppermute(both, plane, [(i, i ^ step) for i in range(devices)])
            for step in range(2, devices, 2)
        ]
    else:
        received = [
            lax.all_to_all(
                jnp.broadcast_to(payload[None], (devices,) + payload.shape),
                plane,
                split_axis=0,
                concat_axis=0,
                tiled=True,
            )
        ]

    wide_count = count + 6 * half
    pixels = call(
        functools.partial(
            perceptual_kernel,
            (
                rows, cols, blocks, block_frames, target.shape[2], parts, own_slots, frames_own,
                pack,
            ),
            len(received),
            paired,
        ),
        jax.ShapeDtypeStruct((3, number, (cols + 2) * half), bf16),
        [
            ((128, 2 * v1), f32),
            ((18 * v1, 2 * v1), bf16),
            ((18 * v1, 2 * v2), bf16),
            ((9 * v2, 2 * v1), bf16),
            ((18 * v1, 2 * v1), bf16),
            ((8, 18 * v1), f32),
            ((devices, rows * 8, line), f32),
            ((number * 3, (cols + 2) * half), f32),
            ((devices, size - 3 * rows, line), f32),
            ((frames_own * parts, number * 8, line), f32),
            ((number + 2, 24, lanes), f32),
            ((number + 2, count + 2 * half, 2 * v1), bf16),
            ((number + 2, count, 2 * v1), bf16),
            ((number // 2 + 2, count // 2 + 2 * half, 2 * v1), bf16),
            ((number // 2 + 2, count // 2, 2 * v1), bf16),
            ((number // 2 + 2, count // 2 + 2 * half, v2), bf16),
            ((number // 2 + 2, count // 2, v2), bf16),
            ((number, wide_count, 2 * v1), f32),
            ((number, wide_count, 2 * v1), f32),
            ((number // 2, wide_count, 2 * v1), f32),
            ((number + 2, (cols + 6) * half, 2 * v1), bf16),
            ((number + 2, (cols + 4) * half, 2 * v1), bf16),
            ((number + 2, (cols + 4) * half, 2 * v1), bf16),
            ((number + 2, (cols + 2) * half, 2 * v1), bf16),
        ],
        0,
        big,
        operands=3 + len(received),
        flops=2**32,
    )(*received, vgg_first, vgg_second.T, vgg_third)

    gathered = [pixels]
    for step in range(1, groups):
        gathered.append(lax.ppermute(pixels, "grp", partners(step, groups)))

    out_rows = conv_first.shape[0] // groups
    taps = max(
        -(-(g + 1) * out_rows // channels) - g * out_rows // channels for g in range(groups)
    )
    even = out_rows % devices == 0
    out_shape = jax.ShapeDtypeStruct((2, out_rows, channels), bf16)
    if even:
        count_out = devices // 2 if paired else devices
        out_shape = jax.ShapeDtypeStruct((count_out, 2, out_rows // devices, channels), bf16)
    if even and paired:
        out_shape = (out_shape, out_shape)
    terms = call(
        functools.partial(
            backward_kernel, parts=parts, out_rows=out_rows, groups=groups,
            outs=2 if even and paired else 1,
        ),
        out_shape,
        [
            ((rows, cols * slots, channels), f32),
            ((rows + 2, (cols + 2) * slots, channels), f32),
            ((rows + 2, cols + 2, slots, channels), bf16),
            ((rows + 2, cols + 2, slots, channels), bf16),
            (conv_second.shape, bf16),
            ((9 * channels, 2 * channels), bf16),
            ((6 * channels, 2 * channels), bf16),
            ((8, channels), f32),
            ((groups, number * 8, (cols + 2) * half), f32),
            ((number, groups, (cols + 2) * half, channels), f32),
            ((rows + 4, (cols + 2) * slots, channels), f32),
            ((rows + 2, cols + 2, slots, channels), bf16),
            ((rows, cols * slots, channels), bf16),
            ((3, rows, channels, cols * slots), bf16),
            ((taps * channels, channels), f32),
        ],
        5,
        big + 8,
        hbm_in=tuple(range(groups + 1, groups + 6)),
        operands=groups + 6,
        flops=2**32,
    )(
        *gathered, rgb_weight, conv_second, slope_first, slope_second, cells, hidden,
    )

    if even and paired:
        kept, given = terms
        came = lax.ppermute(given, plane, partners(1, devices))
        halves = [kept[k].astype(f32) + came[k].astype(f32) for k in range(devices // 2)]
        total = halves[0]
        for k in range(1, devices // 2):
            half_sum = lax.ppermute(halves[k].astype(bf16), plane, partners(2 * k, devices))
            total = total + half_sum.astype(f32)
    elif even:
        pieces = [terms[0]]
        for step in range(1, devices):
            pieces.append(lax.ppermute(terms[step], plane, partners(step, devices)))
        total = sum(piece.astype(f32) for piece in pieces)
    else:
        pieces = jnp.swapaxes(terms.reshape(2, devices, -1), 0, 1)
        pieces = lax.all_to_all(pieces, plane, split_axis=0, concat_axis=0, tiled=True)
        total = jnp.sum(pieces.astype(f32), axis=0)
    return total[0].reshape(-1), total[1].reshape(-1)


def solution(mesh):
    in_specs = (
        P(None, None, "row", "col", None),
        P(None, None, "col", "row", None),
        P(),
        P(),
        P(),
        P(),
        P(),
        P(),
    )
    out_specs = (P(("grp", "row", "col")), P(("grp", "row", "col")))
    return jax.shard_map(local, mesh=mesh, in_specs=in_specs, out_specs=out_specs, check_vma=False)
```
